128 devices in a mesh: req: 16 (over x, y), row: 8 (over z, core).
Axes of the slice: x: 4, y: 4, z: 4, core: 2. Of those that a mesh axis runs over, the one named last changes fastest.
Arguments:
- patches: bfloat16 [8, 2048, 1280], P('row', 'req'), may hold values from -6 to 6
- picture_ids: int32 [8, 2048], P('row'), may hold values from -1 to 15, as said below
- ln_attn: float32 [1280], replicated, may hold values from 0.1 to 1.9
- w_qkv: bfloat16 [3, 1280, 1280], P(None, None, 'req'), may hold values from -6 to 6
- w_out: bfloat16 [1280, 1280], P('req'), may hold values from -1.25 to 1.25
- ln_mlp: float32 [1280], replicated, may hold values from 0.1 to 1.9
- w_up: bfloat16 [1280, 5120], P(None, 'req'), may hold values from -0.15625 to 0.15625
- w_down: bfloat16 [5120, 1280], P('req'), may hold values from -0.3125 to 0.3125
- w_merge: bfloat16 [5120, 1280], replicated, may hold values from -0.078125 to 0.078125
- text_embed: bfloat16 [16384, 1280], P(('req', 'row')), may hold values from -6 to 6
- slot_dest: int32 [8, 512], P('row', 'req'), may hold values from -1 to 16383, as said below
Outputs:
- prompt_embed: bfloat16 [16384, 1280], P(('req', 'row'))
The draws below stay inside these ranges and needn't reach their ends.
Inputs may be any that keep to these rules, and one draw needn't show every extreme that they name: `picture_ids`: each group holds whole pictures one after another from its first row, each picture's length a multiple of 4 and laid out so that every aligned run of four rows is one 2x2 window; rows after the last picture are padding. `slot_dest`: A merged row has a prompt row exactly when its patch rows belong to a picture; no prompt row is named twice; a merged row of group g (rows of the row index g) names a prompt row of a device with the same row index; at most 2 merged rows of one device name prompt rows of one device, and in every draw some device sends that many to one device.
All inputs are finite; a program needn't handle non-finite values.
Results may differ from the reference program's by a relative error of at most 0.023.
Values may be sent and summed in bfloat16 or wider, within the bound.
No kernel may reach another device: no remote copies, remote signals or barrier semaphores. Data moves between devices by JAX's collectives and lax.ppermute only.
A program may use at most 128 MiB of HBM per device.

```python
import math
import jax
import jax.numpy as jnp
from jax import lax

D = 1280
HEADS = 16
HEAD = 80
FF = 5120
CAP = 2048
PTOK_DEV = 128
PTOK = 16384
N_REQ = 16
N_ROW = 8
DEVICES = 128


def picture_layout(key):
    grid_key = jax.random.fold_in(key, 11)
    key_high, key_wide, key_keep = jax.random.split(grid_key, 3)
    largest = min(16, math.isqrt(CAP // 4))
    halves_high = jax.random.randint(key_high, (N_ROW, 16), 2, largest + 1)
    halves_wide = jax.random.randint(key_wide, (N_ROW, 16), 2, largest + 1)
    first_cell = (jnp.arange(N_ROW)[:, None] == 0) & (jnp.arange(16)[None, :] == 0)
    halves_high = jnp.where(first_cell, largest, halves_high)
    halves_wide = jnp.where(first_cell, largest, halves_wide)
    last_group = (jnp.arange(N_ROW)[:, None] == N_ROW - 1) & (jnp.arange(16)[None, :] >= 0)
    halves_high = jnp.where(last_group, 2, halves_high)
    halves_wide = jnp.where(last_group, 2, halves_wide)
    keep = jax.random.randint(key_keep, (N_ROW,), 1, 17)
    keep = jnp.where(jnp.arange(N_ROW) == N_ROW - 1, 16, keep)
    lengths = 4 * halves_high * halves_wide
    lengths = jnp.where(jnp.arange(16)[None, :] < keep[:, None], lengths, 0)
    ends = jnp.cumsum(lengths, axis=1)
    used = jnp.max(jnp.where(ends <= CAP, ends, 0), axis=1)
    position = jnp.arange(CAP)
    ids = jnp.sum((ends[:, None, :] <= position[None, :, None]).astype(jnp.int32), axis=2)
    return jnp.where(position[None, :] < used[:, None], ids, -1).astype(jnp.int32)


def draw_picture_ids(key, part):
    return picture_layout(key)


def draw_slot_dest(key, part):
    ids = picture_layout(key)
    valid = ids[:, ::4] >= 0
    merged_dev = CAP // N_REQ // 4
    slot = max(2, merged_dev // N_REQ)
    merged_index = jnp.arange(CAP // 4)
    source_req = merged_index // merged_dev
    within = merged_index % merged_dev
    offsets = jax.random.randint(jax.random.fold_in(key, 23), (N_ROW, N_REQ), 0, N_REQ)
    dest_req = (offsets[:, source_req] + (within // slot)[None, :]) % N_REQ
    device = dest_req * N_ROW + jnp.arange(N_ROW)[:, None]
    lane = (slot * source_req + within % slot)[None, :] + jnp.zeros((N_ROW, 1), jnp.int32)
    scores = jax.random.randint(jax.random.fold_in(key, 29), (DEVICES, PTOK_DEV), 0, 1 << 20) * PTOK_DEV + jnp.arange(PTOK_DEV)[None, :]
    shuffle = jnp.argsort(scores, axis=1).astype(jnp.int32)
    local = shuffle[device, lane]
    return jnp.where(valid, device * PTOK_DEV + local, -1).astype(jnp.int32)


def draw_w_qkv(key, part):
    key_base = jax.random.fold_in(jax.random.fold_in(key, 37), 0)
    weights = jnp.clip(jax.random.normal(key_base, (3, D, HEADS * HEAD), jnp.float32), -6.0, 6.0) * D ** (-0.5)
    return weights.astype(jnp.bfloat16)


def level_of(rng, extent, pieces, low, high):
    factor_of = 1.0
    for dim, blocks in pieces:
        steps = jax.random.uniform(jax.random.fold_in(jax.random.fold_in(rng, 6), dim), (blocks,), jnp.float32, low / len(pieces), high / len(pieces))
        factor_of = factor_of * jnp.repeat(jnp.exp(steps), extent[dim] // blocks).reshape((-1,) + (1,) * (len(extent) - 1 - dim))
    return factor_of


def normal_values(stream_key, extent, scale, limit, cuts=(), held_as=jnp.bfloat16):
    result = scale * jax.random.normal(stream_key, extent, jnp.float32)
    if cuts:
        result = result * level_of(stream_key, extent, cuts, -0.22, 0.18)
    return jnp.clip(result, -limit, limit).astype(held_as)


def setup_inputs(seed: int = 0) -> dict:
    seeds = jax.random.split(jax.random.key(seed), 12)
    patches = normal_values(seeds[0], (N_ROW, CAP, D), 1.0, 6.0, ((0, 8), (1, 16)))
    picture_ids = draw_picture_ids(jax.random.fold_in(seeds[11], 71), 0)
    ln_attn = jnp.clip(1.0 + 0.18 * jax.random.normal(seeds[2], (D,), jnp.float32), 0.1, 1.9)
    w_qkv = draw_w_qkv(jax.random.fold_in(seeds[11], 71), 0)
    w_out = normal_values(seeds[4], (HEADS * HEAD, D), (HEADS * HEAD // 64) ** -0.5, 1.25, ((0, 16),))
    ln_mlp = jnp.clip(1.0 + 0.18 * jax.random.normal(seeds[5], (D,), jnp.float32), 0.1, 1.9)
    w_up = normal_values(seeds[6], (D, FF), D ** -0.5, 0.15625, ((1, 16),))
    w_down = normal_values(seeds[7], (FF, D), (FF // 16) ** -0.5, 0.3125, ((0, 16),))
    w_merge = normal_values(seeds[8], (4 * D, D), (4 * D) ** -0.5, 0.078125)
    text_embed = normal_values(seeds[9], (PTOK, D), 1.0, 6.0, ((0, 128),))
    slot_dest = draw_slot_dest(jax.random.fold_in(seeds[11], 71), 0)
    return dict(patches=patches, picture_ids=picture_ids, ln_attn=ln_attn, w_qkv=w_qkv, w_out=w_out, ln_mlp=ln_mlp, w_up=w_up, w_down=w_down, w_merge=w_merge, text_embed=text_embed, slot_dest=slot_dest)


def layer_norm(rows, gain):
    rows32 = rows.astype(jnp.float32)
    center = rows32 - lax.optimization_barrier(jnp.mean(rows32, axis=-1, keepdims=True))
    spread = lax.optimization_barrier(jnp.mean(center * center, axis=-1, keepdims=True))
    return center * lax.rsqrt(spread + 1e-06) * gain.astype(jnp.float32)

def attention(normed, ids, w_qkv):
    query = jnp.dot(normed, w_qkv[0], preferred_element_type=jnp.float32).astype(jnp.bfloat16)
    keys = jnp.dot(normed, w_qkv[1], preferred_element_type=jnp.float32).astype(jnp.bfloat16)
    values = jnp.dot(normed, w_qkv[2], preferred_element_type=jnp.float32).astype(jnp.bfloat16)
    same = ids[:, None] == ids[None, :]
    scale = 1.0 / math.sqrt(HEAD)

    def one_head(head):
        start = head * HEAD
        q_head = lax.dynamic_slice_in_dim(query, start, HEAD, 1)
        k_head = lax.dynamic_slice_in_dim(keys, start, HEAD, 1)
        v_head = lax.dynamic_slice_in_dim(values, start, HEAD, 1)
        scores = jnp.dot(q_head, k_head.T, preferred_element_type=jnp.float32) * scale
        scores = jnp.where(same, scores, -1e+30)
        top = lax.optimization_barrier(jnp.max(scores, axis=1, keepdims=True))
        expo = jnp.exp(scores - top)
        probs = (expo / lax.optimization_barrier(jnp.sum(expo, axis=1, keepdims=True))).astype(jnp.bfloat16)
        return jnp.dot(probs, v_head, preferred_element_type=jnp.float32).astype(jnp.bfloat16)
    per_head = lax.map(one_head, jnp.arange(HEADS, dtype=jnp.int32))
    return jnp.transpose(per_head, (1, 0, 2)).reshape(CAP, HEADS * HEAD)

def split_sum(left, right, parts):
    width = left.shape[1] // parts

    def add(total, index):
        start = index * width
        term = jnp.dot(lax.dynamic_slice_in_dim(left, start, width, 1), lax.dynamic_slice_in_dim(right, start, width, 0), preferred_element_type=jnp.float32).astype(jnp.bfloat16)
        return (total + term.astype(jnp.float32), None)
    start_total = jnp.zeros((left.shape[0], right.shape[1]), jnp.float32)
    total, _ = lax.scan(add, start_total, jnp.arange(parts, dtype=jnp.int32))
    return total

def reference(patches, picture_ids, ln_attn, w_qkv, w_out, ln_mlp, w_up, w_down, w_merge, text_embed, slot_dest):

    def one_group(item):
        rows, ids = item
        normed = layer_norm(rows, ln_attn).astype(jnp.bfloat16)
        attended = attention(normed, ids, w_qkv)
        attn = split_sum(attended, w_out, N_REQ)
        resid = (rows.astype(jnp.float32) + attn).astype(jnp.bfloat16)
        normed_two = layer_norm(resid, ln_mlp).astype(jnp.bfloat16)
        hidden = jax.nn.gelu(jnp.dot(normed_two, w_up, preferred_element_type=jnp.float32), approximate=False).astype(jnp.bfloat16)
        mlp = split_sum(hidden, w_down, N_REQ)
        return (resid.astype(jnp.float32) + mlp).astype(jnp.bfloat16)
    vision = lax.map(one_group, (patches, picture_ids))
    merged = vision.reshape(N_ROW * (CAP // 4), 4 * D)
    projected = jnp.dot(merged, w_merge, preferred_element_type=jnp.float32).astype(jnp.bfloat16)
    dest = slot_dest.reshape(-1)
    target = jnp.where(dest >= 0, dest, PTOK).astype(jnp.int32)
    return text_embed.at[target].set(projected, mode='drop')
```

```python
import math

import jax
import jax.numpy as jnp
from jax import lax
from jax.experimental import pallas as pl
from jax.experimental.pallas import tpu as pltpu
from jax.sharding import Mesh
from jax.sharding import PartitionSpec as P

HEAD = 80
N = 4
BF = jnp.bfloat16
F32 = jnp.float32
NT = (((1,), (1,)), ((), ()))
TN = (((0,), (0,)), ((), ()))
VMEM = pl.BlockSpec(memory_space=pltpu.VMEM)
SMEM = pl.BlockSpec(memory_space=pltpu.SMEM)
PARAMS = pltpu.CompilerParams(vmem_limit_bytes=56 << 20)


def norm_rows(rows32, gain):
    center = rows32 - jnp.mean(rows32, axis=-1, keepdims=True)
    spread = jnp.mean(center * center, axis=-1, keepdims=True)
    return center * lax.rsqrt(spread + 1e-06) * gain


def shift(value, axis, step):
    pairs = [(i, (i + step) % N) for i in range(N)]
    return lax.ppermute(value, axis, pairs)


def swap(value):
    return lax.ppermute(value, "c", [(0, 1), (1, 0)])


def qkv_kernel(pos, p0, p1, p2, p3, gain, w0, m1, m2, m3, s1, s2, s3, o0, o1, o2, o3, h1):
    y = pos[1]
    c = pos[3]
    half = h1.shape[2]
    rows = p0.shape[0]
    for k, piece in enumerate((p0, p1, p2, p3)):
        normed = norm_rows(piece[...].astype(F32), gain[...]).astype(BF)
        at = pl.ds(pl.multiple_of(lax.rem(y - k + N, N) * rows, rows), rows)
        h1[0, at, :] = normed[:, :half]
        h1[1, at, :] = normed[:, half:]
    own = lax.dot_general(w0[:, :half], h1[0], NT, preferred_element_type=F32)
    own += lax.dot_general(w0[:, half:], h1[1], NT, preferred_element_type=F32)
    o0[...] = own.astype(BF)
    for mine, other, out in ((m1, s1, o1), (m2, s2, o2), (m3, s3, o3)):
        total = lax.dot_general(mine[...], h1[c], NT, preferred_element_type=F32)
        total += lax.dot_general(other[...], h1[1 - c], NT, preferred_element_type=F32)
        out[...] = total.astype(BF)


def attend_kernel(pos, bounds, r0, r1, r2, r3, id_row, id_col, out, qs, ks, vs, scores):
    x = pos[0]
    chunk = ks.shape[2]
    block = qs.shape[2]
    per = block // chunk
    scale = math.log2(math.e) / math.sqrt(HEAD)
    for k, piece in enumerate((r0, r1, r2, r3)):
        at = lax.rem(x + k, N)
        qs[at] = piece[:HEAD, :]
        for j in range(per):
            cols = slice(j * chunk, (j + 1) * chunk)
            ks[at * per + j] = piece[HEAD : 2 * HEAD, cols]
            vs[at * per + j] = piece[2 * HEAD :, cols]

    for qb in range(N):
        low = bounds[0, qb]
        high = bounds[1, qb]
        query = qs[qb]
        query_ids = id_row[:, qb * block : (qb + 1) * block]

        def score(kc, query=query):
            return lax.dot_general(ks[kc], query, TN, preferred_element_type=F32)

        scores[0] = score(low)

        def step(i, carry, query=query, query_ids=query_ids, low=low, high=high):
            top, total, acc = carry
            slot = lax.rem(i - low, 2)
            raw = scores[slot]
            scores[1 - slot] = score(jnp.minimum(i + 1, high - 1))
            key_ids = id_col[pl.ds(pl.multiple_of(i * chunk, chunk), chunk), :]
            val = jnp.where(key_ids == query_ids, raw * scale, -1e30)
            new_top = jnp.maximum(top, jnp.max(val, axis=0, keepdims=True))
            alpha = jnp.exp2(top - new_top)
            expo = jnp.exp2(val - new_top)
            total = total * alpha + jnp.sum(expo, axis=0, keepdims=True)
            acc = acc * alpha + jnp.dot(vs[i], expo.astype(BF), preferred_element_type=F32)
            return new_top, total, acc

        start = (
            jnp.full((1, block), -1e30, F32),
            jnp.zeros((1, block), F32),
            jnp.zeros((HEAD, block), F32),
        )
        top, total, acc = lax.fori_loop(low, high, step, start)
        out[lax.rem(qb - x + N, N)] = (acc / total).astype(BF)


def mlp_kernel(pos, g0, g1, g2, g3, p0, p1, p2, p3, gain, w_mlp, w_out, part, own, att, resid):
    x = pos[0]
    y = pos[1]
    rows = p0.shape[0]
    for k, piece in enumerate((g0, g1, g2, g3)):
        for j in range(N):
            at = lax.rem(y - k + N, N) * N + lax.rem(x - j + N, N)
            att[at] = piece[j * HEAD : (j + 1) * HEAD, :]
    for k, piece in enumerate((p0, p1, p2, p3)):
        at = pl.ds(pl.multiple_of(lax.rem(y - k + N, N) * rows, rows), rows)
        resid[at, :] = piece[...].astype(F32)
    lhs = att[...].reshape(N * N * HEAD, N * rows)
    attn = lax.dot_general(lhs, w_out[...], TN, preferred_element_type=F32)
    resid[...] = (resid[...] + attn).astype(BF).astype(F32)
    own[...] = resid[pl.ds(pl.multiple_of(y * rows, rows), rows), :].astype(BF)
    normed = norm_rows(resid[...], gain[...]).astype(BF)
    units = 160
    up = jnp.concatenate([w_mlp[i, :units, :] for i in range(2 * N)], axis=0)
    down = jnp.concatenate([w_mlp[i, units : 2 * units, :] for i in range(2 * N)], axis=0)
    hidden = lax.dot_general(normed, up, NT, preferred_element_type=F32)
    hidden = (0.5 * hidden * (1.0 + lax.erf(hidden * math.sqrt(0.5)))).astype(BF)
    result = jnp.dot(hidden, down, preferred_element_type=F32).astype(BF)
    for yb in range(N):
        part[lax.rem(yb - y + N, N)] = result[yb * rows : (yb + 1) * rows, :]


def local(
    patches,
    picture_ids,
    ln_attn,
    w_qkv,
    w_out,
    ln_mlp,
    w_up,
    w_down,
    w_merge,
    text_embed,
    slot_dest,
):
    rows = patches[0]
    count, width = rows.shape
    x = lax.axis_index("x")
    y = lax.axis_index("y")
    c = lax.axis_index("c")
    pos = jnp.stack([x, y, lax.axis_index("z"), c]).astype(jnp.int32)
    ids = picture_ids[0]

    units = w_down.shape[0] // 2
    half_head = HEAD // 2
    packed = jnp.concatenate(
        [
            lax.dynamic_slice_in_dim(w_up.T, c * units, units, 0),
            lax.dynamic_slice_in_dim(w_down, c * units, units, 0),
            lax.dynamic_slice_in_dim(w_out, c * half_head, half_head, 0),
        ],
        axis=0,
    )

    pieces = [rows] + [shift(rows, "y", k) for k in (1, 2, 3)]
    w_heads = jnp.transpose(w_qkv, (0, 2, 1)).reshape(3 * HEAD, width)
    w_half = lax.dynamic_slice_in_dim(w_heads, c * (width // 2), width // 2, 1)
    mine = [shift(w_half, "x", k) for k in (1, 2, 3)]
    other = [swap(m) for m in mine]

    w_near = lax.all_gather(packed, ("x", "c"), axis=0, tiled=False)
    out_heads = w_near[:, 2 * units :, :].reshape(N, HEAD, width)
    out_half = lax.dynamic_slice_in_dim(out_heads, c * 2, 2, 0).reshape(2 * HEAD, width)
    w_out_all = lax.all_gather(out_half, ("y", "c"), axis=0, tiled=True)

    total_rows = count * N
    qkv = pl.pallas_call(
        qkv_kernel,
        out_shape=[jax.ShapeDtypeStruct((3 * HEAD, total_rows), BF)] * N,
        in_specs=[SMEM] + [VMEM] * 12,
        out_specs=[VMEM] * N,
        scratch_shapes=[pltpu.VMEM((2, total_rows, width // 2), BF)],
        compiler_params=PARAMS,
        name="qkv",
    )(pos, *pieces, ln_attn[None, :], w_heads, *mine, *other)
    blocks = [qkv[0]] + [shift(qkv[k], "x", -k) for k in (1, 2, 3)]

    group_rows = ids.shape[0]
    chunk = 256
    chunks = group_rows // chunk
    held = (ids[:, None] == jnp.arange(16)[None, :]).reshape(chunks, chunk, 16)
    held = jnp.any(held, axis=1)
    per = chunks // N
    wanted = jnp.any(held.reshape(N, per, 16), axis=1)
    need = jnp.any(wanted[:, None, :] & held[None, :, :], axis=2)
    where = jnp.arange(chunks)[None, :]
    low = jnp.min(jnp.where(need, where, chunks - 1), axis=1)
    high = jnp.max(jnp.where(need, where + 1, 1), axis=1)
    bounds = jnp.stack([jnp.minimum(low, high - 1), high]).astype(jnp.int32)

    attended = pl.pallas_call(
        attend_kernel,
        out_shape=jax.ShapeDtypeStruct((N, HEAD, total_rows), BF),
        in_specs=[SMEM, SMEM] + [VMEM] * 6,
        out_specs=VMEM,
        scratch_shapes=[
            pltpu.VMEM((N, HEAD, total_rows), BF),
            pltpu.VMEM((chunks, HEAD, chunk), BF),
            pltpu.VMEM((chunks, HEAD, chunk), BF),
            pltpu.VMEM((2, chunk, total_rows), F32),
        ],
        compiler_params=PARAMS,
        name="attend",
    )(pos, bounds, *blocks, ids[None, :], ids[:, None])
    heads = [attended[0]] + [shift(attended[k], "x", k) for k in (1, 2, 3)]
    heads = jnp.concatenate(heads, axis=0)
    gathered = [heads] + [shift(heads, "y", k) for k in (1, 2, 3)]

    part, resid = pl.pallas_call(
        mlp_kernel,
        out_shape=[
            jax.ShapeDtypeStruct((N, count, width), BF),
            jax.ShapeDtypeStruct((count, width), BF),
        ],
        in_specs=[SMEM] + [VMEM] * 11,
        out_specs=[VMEM] * 2,
        scratch_shapes=[
            pltpu.VMEM((N * N, HEAD, total_rows), BF),
            pltpu.VMEM((total_rows, width), F32),
        ],
        compiler_params=PARAMS,
        name="mlp",
    )(pos, *gathered, *pieces, ln_mlp[None, :], w_near, w_out_all)
    sums = part[0].astype(F32)
    for k in (1, 2, 3):
        sums = sums + shift(part[k], "y", k).astype(F32)
    vision = (resid.astype(F32) + sums).astype(BF)

    merged = vision.reshape(count // 4, 4 * width)
    projected = jnp.dot(merged, w_merge, preferred_element_type=F32).astype(BF)
    merged_count = merged.shape[0]
    dest = slot_dest[0]
    prompt_rows = text_embed.shape[0]
    req_count = N * N
    row_count = lax.axis_size("z") * lax.axis_size("c")
    slot_cap = 2
    owner = jnp.where(dest >= 0, dest // prompt_rows // row_count, -1)
    order = jnp.arange(merged_count)
    same_owner = (owner[:, None] == owner[None, :]) & (order[None, :] < order[:, None])
    ranks = jnp.sum(same_owner.astype(jnp.int32), axis=1)
    target = jnp.where(owner >= 0, owner * slot_cap + ranks, -1)
    select = target[None, :] == jnp.arange(req_count * slot_cap)[:, None]
    places = jnp.sum(jnp.where(select, (dest % prompt_rows + 1)[None, :], 0), axis=1)
    lane = jnp.arange(128)[None, :] == 0
    tail = jnp.where(lane, places[:, None], 0).astype(BF)
    outgoing = jnp.dot(select.astype(BF), projected, preferred_element_type=F32).astype(BF)
    outgoing = jnp.concatenate([outgoing, tail], axis=1)
    arrived = lax.all_to_all(
        outgoing.reshape(req_count, slot_cap, width + 128),
        ("x", "y"),
        split_axis=0,
        concat_axis=0,
        tiled=True,
    ).reshape(req_count * slot_cap, width + 128)
    landing = arrived[:, width].astype(jnp.int32) - 1
    placer = landing[None, :] == jnp.arange(prompt_rows)[:, None]
    placed = jnp.dot(
        placer.astype(BF), arrived[:, :width], preferred_element_type=F32
    ).astype(BF)
    filled = jnp.any(placer, axis=1)
    return jnp.where(filled[:, None], placed, text_embed)


def solution(mesh):
    grid = Mesh(mesh.devices.reshape(N, N, -1, 2), ("x", "y", "z", "c"))
    req = ("x", "y")
    row = ("z", "c")
    return jax.shard_map(
        local,
        mesh=grid,
        in_specs=(
            P(row, req, None),
            P(row, None),
            P(),
            P(None, None, req),
            P(req, None),
            P(),
            P(None, req),
            P(req, None),
            P(),
            P(("x", "y", "z", "c"), None),
            P(row, req),
        ),
        out_specs=P(("x", "y", "z", "c"), None),
        check_vma=False,
    )
```

```python
import math

import jax
import jax.numpy as jnp
from jax import lax
from jax.experimental import pallas as pl
from jax.experimental.pallas import tpu as pltpu
from jax.sharding import Mesh
from jax.sharding import PartitionSpec as P

HEAD = 80
N = 4
BF = jnp.bfloat16
F32 = jnp.float32
NT = (((1,), (1,)), ((), ()))
TN = (((0,), (0,)), ((), ()))
VMEM = pl.BlockSpec(memory_space=pltpu.VMEM)
SMEM = pl.BlockSpec(memory_space=pltpu.SMEM)


def params(mib):
    return pltpu.CompilerParams(vmem_limit_bytes=mib << 20)


def norm_rows(rows32, gain):
    center = rows32 - jnp.mean(rows32, axis=-1, keepdims=True)
    spread = jnp.mean(center * center, axis=-1, keepdims=True)
    return center * lax.rsqrt(spread + 1e-06) * gain


def shift(value, axis, step):
    pairs = [(i, (i + step) % N) for i in range(N)]
    return lax.ppermute(value, axis, pairs)


def swap(value):
    return lax.ppermute(value, "c", [(0, 1), (1, 0)])


def norm_kernel(pos, p0, p1, p2, p3, gain, h1):
    y = pos[1]
    half = h1.shape[2]
    rows = p0.shape[0]
    for k, piece in enumerate((p0, p1, p2, p3)):
        normed = norm_rows(piece[...].astype(F32), gain[...]).astype(BF)
        at = pl.ds(pl.multiple_of(lax.rem(y - k + N, N) * rows, rows), rows)
        h1[0, at, :] = normed[:, :half]
        h1[1, at, :] = normed[:, half:]


def qkv_kernel(pos, h1, w, o0, o1, o2, o3):
    x = pos[0]
    for k, out in enumerate((o0, o1, o2, o3)):
        at = lax.rem(x - k + N, N) * 2
        total = lax.dot_general(w[at], h1[0], NT, preferred_element_type=F32)
        total += lax.dot_general(w[at + 1], h1[1], NT, preferred_element_type=F32)
        out[...] = total.astype(BF)


def attend_kernel(
    pos, bounds, r0, r1, r2, r3, id_row, id_col, o0, o1, o2, o3, qs, ks, vs, scores, outs
):
    x = pos[0]
    chunk = ks.shape[2]
    block = qs.shape[2]
    per = block // chunk
    scale = math.log2(math.e) / math.sqrt(HEAD)
    for k, piece in enumerate((r0, r1, r2, r3)):
        at = lax.rem(x + k, N)
        qs[at] = piece[:HEAD, :]
        for j in range(per):
            cols = slice(j * chunk, (j + 1) * chunk)
            ks[at * per + j] = piece[HEAD : 2 * HEAD, cols]
            vs[at * per + j] = piece[2 * HEAD :, cols]

    for qb in range(N):
        low = bounds[0, qb]
        high = bounds[1, qb]
        query = qs[qb]
        query_ids = id_row[:, qb * block : (qb + 1) * block]

        def score(kc, query=query):
            return lax.dot_general(ks[kc], query, TN, preferred_element_type=F32)

        scores[0] = score(low)

        def step(i, carry, query=query, query_ids=query_ids, low=low, high=high):
            top, total, acc = carry
            slot = lax.rem(i - low, 2)
            raw = scores[slot]
            scores[1 - slot] = score(jnp.minimum(i + 1, high - 1))
            key_ids = id_col[pl.ds(pl.multiple_of(i * chunk, chunk), chunk), :]
            val = jnp.where(key_ids == query_ids, raw * scale, -1e30)
            new_top = jnp.maximum(top, jnp.max(val, axis=0, keepdims=True))
            alpha = jnp.exp2(top - new_top)
            expo = jnp.exp2(val - new_top)
            total = total * alpha + jnp.sum(expo, axis=0, keepdims=True)
            acc = acc * alpha + jnp.dot(vs[i], expo.astype(BF), preferred_element_type=F32)
            return new_top, total, acc

        start = (
            jnp.full((1, block), -1e30, F32),
            jnp.zeros((1, block), F32),
            jnp.zeros((HEAD, block), F32),
        )
        top, total, acc = lax.fori_loop(low, high, step, start)
        outs[lax.rem(qb - x + N, N)] = (acc / total).astype(BF)
    for k, out in enumerate((o0, o1, o2, o3)):
        out[...] = outs[k]


def mlp_kernel(pos, *refs):
    gathered = refs[0:4]
    pieces = refs[4:8]
    mine = refs[8:12]
    other = refs[12:16]
    gain, w_hbm, t0, t1, t2, t3, own, resid, w_mlp, sem = refs[16:]
    y = pos[1]
    c = pos[3]
    rows = pieces[0].shape[0]
    copy = pltpu.make_async_copy(w_hbm, w_mlp, sem)
    copy.start()
    lhs = jnp.concatenate([g[...] for g in gathered], axis=0)
    w_mine = jnp.concatenate([w[...] for w in mine], axis=0)
    w_other = jnp.concatenate([w[...] for w in other], axis=0)
    half = w_mine.shape[1]
    resid[c] = lax.dot_general(lhs, w_mine, TN, preferred_element_type=F32)
    resid[1 - c] = lax.dot_general(lhs, w_other, TN, preferred_element_type=F32)
    for k, piece in enumerate(pieces):
        at = pl.ds(pl.multiple_of(lax.rem(y - k + N, N) * rows, rows), rows)
        for h in (0, 1):
            start = piece[:, h * half : (h + 1) * half].astype(F32)
            resid[h, at, :] = (resid[h, at, :] + start).astype(BF).astype(F32)
            if k == 0:
                own[:, h * half : (h + 1) * half] = resid[h, at, :].astype(BF)
    full = jnp.concatenate([resid[0], resid[1]], axis=1)
    normed = norm_rows(full, gain[...]).astype(BF)
    copy.wait()
    count = w_mlp.shape[0]
    units = w_mlp.shape[1] // 2
    up = jnp.concatenate([w_mlp[i, :units, :] for i in range(count)], axis=0)
    down = jnp.concatenate([w_mlp[i, units:, :] for i in range(count)], axis=0)
    hidden = lax.dot_general(normed, up, NT, preferred_element_type=F32)
    hidden = (0.5 * hidden * (1.0 + lax.erf(hidden * math.sqrt(0.5)))).astype(BF)
    result = jnp.dot(hidden, down, preferred_element_type=F32)
    for h in range(N):
        resid[0, h * rows : (h + 1) * rows, :] = result[h * rows : (h + 1) * rows, :half]
        resid[1, h * rows : (h + 1) * rows, :] = result[h * rows : (h + 1) * rows, half:]
    for k, out in enumerate((t0, t1, t2, t3)):
        at = pl.ds(pl.multiple_of(lax.rem(y + k, N) * rows, rows), rows)
        out[:, :half] = resid[0, at, :].astype(BF)
        out[:, half:] = resid[1, at, :].astype(BF)


def local(
    patches,
    picture_ids,
    ln_attn,
    w_qkv,
    w_out,
    ln_mlp,
    w_up,
    w_down,
    w_merge,
    text_embed,
    slot_dest,
):
    rows = patches[0]
    count, width = rows.shape
    x = lax.axis_index("x")
    y = lax.axis_index("y")
    c = lax.axis_index("c")
    pos = jnp.stack([x, y, lax.axis_index("z"), c]).astype(jnp.int32)
    ids = picture_ids[0]

    half = width // 2
    w_heads = jnp.transpose(w_qkv, (0, 2, 1)).reshape(3 * HEAD, width)
    w_half = lax.dynamic_slice_in_dim(w_heads, c * half, half, 1)
    w_heads = lax.all_gather(w_half, ("x", "c"), axis=0, tiled=False)
    units = w_down.shape[0] // 2
    packed = jnp.concatenate(
        [
            lax.dynamic_slice_in_dim(w_up.T, c * units, units, 0),
            lax.dynamic_slice_in_dim(w_down, c * units, units, 0),
        ],
        axis=0,
    )
    packed, _ = lax.optimization_barrier((packed, w_half))
    w_near = lax.all_gather(packed, ("x", "c"), axis=0, tiled=False)

    pieces = [rows] + [shift(rows, "y", k) for k in (1, 2, 3)]
    out_half = lax.dynamic_slice_in_dim(w_out, c * half, half, 1)
    out_near = [out_half] + [shift(out_half, "x", k) for k in (1, 2, 3)]
    out_near = jnp.concatenate(out_near, axis=0)
    out_mine = [out_near] + [shift(out_near, "y", k) for k in (1, 2, 3)]
    out_other = [swap(m) for m in out_mine]

    total_rows = count * N
    h1 = pl.pallas_call(
        norm_kernel,
        out_shape=jax.ShapeDtypeStruct((2, total_rows, half), BF),
        in_specs=[SMEM] + [VMEM] * 5,
        out_specs=VMEM,
        compiler_params=params(16),
        name="norm",
    )(pos, *pieces, ln_attn[None, :])
    qkv = pl.pallas_call(
        qkv_kernel,
        out_shape=[jax.ShapeDtypeStruct((3 * HEAD, total_rows), BF)] * N,
        in_specs=[SMEM] + [VMEM] * 2,
        out_specs=[VMEM] * N,
        compiler_params=params(16),
        name="qkv",
    )(pos, h1, w_heads)
    blocks = [qkv[0]] + [shift(qkv[k], "x", -k) for k in (1, 2, 3)]

    group_rows = ids.shape[0]
    chunk = 256
    chunks = group_rows // chunk
    held = (ids[:, None] == jnp.arange(16)[None, :]).reshape(chunks, chunk, 16)
    held = jnp.any(held, axis=1)
    per = chunks // N
    wanted = jnp.any(held.reshape(N, per, 16), axis=1)
    need = jnp.any(wanted[:, None, :] & held[None, :, :], axis=2)
    where = jnp.arange(chunks)[None, :]
    low = jnp.min(jnp.where(need, where, chunks - 1), axis=1)
    high = jnp.max(jnp.where(need, where + 1, 1), axis=1)
    bounds = jnp.stack([jnp.minimum(low, high - 1), high]).astype(jnp.int32)

    attended = pl.pallas_call(
        attend_kernel,
        out_shape=[jax.ShapeDtypeStruct((HEAD, total_rows), BF)] * N,
        in_specs=[SMEM, SMEM] + [VMEM] * 6,
        out_specs=[VMEM] * N,
        scratch_shapes=[
            pltpu.VMEM((N, HEAD, total_rows), BF),
            pltpu.VMEM((chunks, HEAD, chunk), BF),
            pltpu.VMEM((chunks, HEAD, chunk), BF),
            pltpu.VMEM((2, chunk, total_rows), F32),
            pltpu.VMEM((N, HEAD, total_rows), BF),
        ],
        compiler_params=params(16),
        name="attend",
    )(pos, bounds, *blocks, ids[None, :], ids[:, None])
    heads = [attended[0]] + [shift(attended[k], "x", k) for k in (1, 2, 3)]
    heads = jnp.concatenate(heads, axis=0)
    gathered = [heads] + [shift(heads, "y", k) for k in (1, 2, 3)]

    *part, resid = pl.pallas_call(
        mlp_kernel,
        out_shape=[jax.ShapeDtypeStruct((count, width), BF)] * (N + 1),
        in_specs=[SMEM] + [VMEM] * 17 + [pl.BlockSpec(memory_space=pl.ANY)],
        out_specs=[VMEM] * (N + 1),
        scratch_shapes=[
            pltpu.VMEM((2, total_rows, half), F32),
            pltpu.VMEM(w_near.shape, BF),
            pltpu.SemaphoreType.DMA(()),
        ],
        compiler_params=params(40),
        name="mlp",
    )(pos, *gathered, *pieces, *out_mine, *out_other, ln_mlp[None, :], w_near)
    sums = part[0].astype(F32)
    for k in (1, 2, 3):
        sums = sums + shift(part[k], "y", k).astype(F32)
    vision = (resid.astype(F32) + sums).astype(BF)

    merged = vision.reshape(count // 4, 4 * width)
    projected = jnp.dot(merged, w_merge, preferred_element_type=F32).astype(BF)
    merged_count = merged.shape[0]
    dest = slot_dest[0]
    prompt_rows = text_embed.shape[0]
    req_count = N * N
    row_count = lax.axis_size("z") * lax.axis_size("c")
    slot_cap = 2
    owner = jnp.where(dest >= 0, dest // prompt_rows // row_count, -1)
    order = jnp.arange(merged_count)
    same_owner = (owner[:, None] == owner[None, :]) & (order[None, :] < order[:, None])
    ranks = jnp.sum(same_owner.astype(jnp.int32), axis=1)
    target = jnp.where(owner >= 0, owner * slot_cap + ranks, -1)
    select = target[None, :] == jnp.arange(req_count * slot_cap)[:, None]
    places = jnp.sum(jnp.where(select, (dest % prompt_rows + 1)[None, :], 0), axis=1)
    lane = jnp.arange(128)[None, :] == 0
    tail = jnp.where(lane, places[:, None], 0).astype(BF)
    outgoing = jnp.dot(select.astype(BF), projected, preferred_element_type=F32).astype(BF)
    outgoing = jnp.concatenate([outgoing, tail], axis=1)
    arrived = lax.all_to_all(
        outgoing.reshape(req_count, slot_cap, width + 128),
        ("x", "y"),
        split_axis=0,
        concat_axis=0,
        tiled=True,
    ).reshape(req_count * slot_cap, width + 128)
    landing = arrived[:, width].astype(jnp.int32) - 1
    placer = landing[None, :] == jnp.arange(prompt_rows)[:, None]
    placed = jnp.dot(
        placer.astype(BF), arrived[:, :width], preferred_element_type=F32
    ).astype(BF)
    filled = jnp.any(placer, axis=1)
    return jnp.where(filled[:, None], placed, text_embed)


def solution(mesh):
    grid = Mesh(mesh.devices.reshape(N, N, -1, 2), ("x", "y", "z", "c"))
    req = ("x", "y")
    row = ("z", "c")
    return jax.shard_map(
        local,
        mesh=grid,
        in_specs=(
            P(row, req, None),
            P(row, None),
            P(),
            P(None, None, req),
            P(req, None),
            P(),
            P(None, req),
            P(req, None),
            P(),
            P(("x", "y", "z", "c"), None),
            P(row, req),
        ),
        out_specs=P(("x", "y", "z", "c"), None),
        check_vma=False,
    )
```

```python
import math

import jax
import jax.numpy as jnp
from jax import lax
from jax.experimental import pallas as pl
from jax.experimental.pallas import tpu as pltpu
from jax.sharding import Mesh
from jax.sharding import PartitionSpec as P

HEAD = 80
N = 4
BF = jnp.bfloat16
F32 = jnp.float32
NT = (((1,), (1,)), ((), ()))
TN = (((0,), (0,)), ((), ()))
HBM = pl.BlockSpec(memory_space=pltpu.HBM)
VMEM = pl.BlockSpec(memory_space=pltpu.VMEM)
SMEM = pl.BlockSpec(memory_space=pltpu.SMEM)


def params(mib):
    return pltpu.CompilerParams(vmem_limit_bytes=mib << 20)


def norm_rows(rows32, gain):
    center = rows32 - jnp.mean(rows32, axis=-1, keepdims=True)
    spread = jnp.mean(center * center, axis=-1, keepdims=True)
    return center * lax.rsqrt(spread + 1e-06) * gain


def shift(value, axis, step):
    pairs = [(i, (i + step) % N) for i in range(N)]
    return lax.ppermute(value, axis, pairs)


def far(value):
    return pltpu.with_memory_space_constraint(value, pltpu.HBM)


def swap(value):
    return lax.ppermute(value, "c", [(0, 1), (1, 0)])


def norm_kernel(pos, p0, p1, p2, p3, gain, h1):
    y = pos[1]
    half = h1.shape[2]
    rows = p0.shape[0]
    for k, piece in enumerate((p0, p1, p2, p3)):
        normed = norm_rows(piece[...].astype(F32), gain[...]).astype(BF)
        at = pl.ds(pl.multiple_of(lax.rem(y - k + N, N) * rows, rows), rows)
        h1[0, at, :] = normed[:, :half]
        h1[1, at, :] = normed[:, half:]


def qkv_kernel(pos, h1, w_hbm, o0, o1, o2, o3, w, sem):
    x = pos[0]
    copy = pltpu.make_async_copy(w_hbm.at[:, : w.shape[1], :], w, sem)
    copy.start()
    copy.wait()
    for k, out in enumerate((o0, o1, o2, o3)):
        at = lax.rem(x - k + N, N) * 2
        total = lax.dot_general(w[at], h1[0], NT, preferred_element_type=F32)
        total += lax.dot_general(w[at + 1], h1[1], NT, preferred_element_type=F32)
        out[...] = total.astype(BF)


def attend_kernel(
    pos, bounds, r0, r1, r2, r3, id_row, id_col, o0, o1, o2, o3, qs, ks, vs, scores, outs
):
    x = pos[0]
    chunk = ks.shape[2]
    block = qs.shape[2]
    per = block // chunk
    scale = math.log2(math.e) / math.sqrt(HEAD)
    for k, piece in enumerate((r0, r1, r2, r3)):
        at = lax.rem(x + k, N)
        qs[at] = piece[:HEAD, :]
        for j in range(per):
            cols = slice(j * chunk, (j + 1) * chunk)
            ks[at * per + j] = piece[HEAD : 2 * HEAD, cols]
            vs[at * per + j] = piece[2 * HEAD :, cols]

    for qb in range(N):
        low = bounds[0, qb]
        high = bounds[1, qb]
        query = qs[qb]
        query_ids = id_row[:, qb * block : (qb + 1) * block]

        def score(kc, query=query):
            return lax.dot_general(ks[kc], query, TN, preferred_element_type=F32)

        scores[0] = score(low)

        def step(i, carry, query=query, query_ids=query_ids, low=low, high=high):
            top, total, acc = carry
            slot = lax.rem(i - low, 2)
            raw = scores[slot]
            scores[1 - slot] = score(jnp.minimum(i + 1, high - 1))
            key_ids = id_col[pl.ds(pl.multiple_of(i * chunk, chunk), chunk), :]
            val = jnp.where(key_ids == query_ids, raw * scale, -1e30)
            new_top = jnp.maximum(top, jnp.max(val, axis=0, keepdims=True))
            alpha = jnp.exp2(top - new_top)
            expo = jnp.exp2(val - new_top)
            total = total * alpha + jnp.sum(expo, axis=0, keepdims=True)
            acc = acc * alpha + jnp.dot(vs[i], expo.astype(BF), preferred_element_type=F32)
            return new_top, total, acc

        start = (
            jnp.full((1, block), -1e30, F32),
            jnp.zeros((1, block), F32),
            jnp.zeros((HEAD, block), F32),
        )
        top, total, acc = lax.fori_loop(low, high, step, start)
        outs[lax.rem(qb - x + N, N)] = (acc / total).astype(BF)
    for k, out in enumerate((o0, o1, o2, o3)):
        out[...] = outs[k]


def pack_kernel(pos, g0, g1, g2, g3, out):
    x = pos[0]
    for k, piece in enumerate((g0, g1, g2, g3)):
        out[lax.rem(x - k + N, N)] = piece[...]


def mlp_kernel(pos, *refs):
    gathered = refs[0:4]
    pieces = refs[4:8]
    gain, near, w_hbm = refs[8:11]
    mine = refs[11:14]
    other = refs[14:17]
    merge_hbm = refs[17]
    t0, t1, t2, t3, own, w_merge, resid, w_mine, w_other, up, down, sems = refs[18:]
    y = pos[1]
    c = pos[3]
    rows = pieces[0].shape[0]
    half = w_mine.shape[1]
    group = N * HEAD
    skip = near.shape[1] - HEAD
    first = []
    for j in range(N):
        to = pl.ds(j * HEAD, HEAD)
        src = near.at[2 * j + c, skip : skip + HEAD, :]
        first.append(pltpu.make_async_copy(src, w_mine.at[to, :], sems.at[j]))
        src = near.at[2 * j + 1 - c, skip : skip + HEAD, :]
        first.append(pltpu.make_async_copy(src, w_other.at[to, :], sems.at[N + j]))
    for k in range(N - 1):
        to = pl.ds((k + 1) * group, group)
        first.append(pltpu.make_async_copy(mine[k], w_mine.at[to, :], sems.at[2 * N + k]))
        first.append(pltpu.make_async_copy(other[k], w_other.at[to, :], sems.at[3 * N + k]))
    units = up.shape[1]
    second = [
        pltpu.make_async_copy(w_hbm.at[:, :units, :], up, sems.at[4 * N]),
        pltpu.make_async_copy(w_hbm.at[:, units:, :], down, sems.at[4 * N + 1]),
    ]
    ahead = pltpu.make_async_copy(merge_hbm, w_merge, sems.at[4 * N + 2])
    for copy in first + second + [ahead]:
        copy.start()
    lhs = jnp.concatenate([g[...].reshape(group, N * rows) for g in gathered], axis=0)
    for copy in first:
        copy.wait()
    resid[c] = lax.dot_general(lhs, w_mine[...], TN, preferred_element_type=F32)
    resid[1 - c] = lax.dot_general(lhs, w_other[...], TN, preferred_element_type=F32)
    for k, piece in enumerate(pieces):
        at = pl.ds(pl.multiple_of(lax.rem(y - k + N, N) * rows, rows), rows)
        for h in (0, 1):
            start = piece[:, h * half : (h + 1) * half].astype(F32)
            resid[h, at, :] = (resid[h, at, :] + start).astype(BF).astype(F32)
            if k == 0:
                own[:, h * half : (h + 1) * half] = resid[h, at, :].astype(BF)
    full = jnp.concatenate([resid[0], resid[1]], axis=1)
    normed = norm_rows(full, gain[...]).astype(BF)
    width = 2 * half
    count = up.shape[0] * units
    second[0].wait()
    hidden = lax.dot_general(
        normed, up[...].reshape(count, width), NT, preferred_element_type=F32
    )
    hidden = (0.5 * hidden * (1.0 + lax.erf(hidden * math.sqrt(0.5)))).astype(BF)
    second[1].wait()
    result = jnp.dot(hidden, down[...].reshape(count, width), preferred_element_type=F32)
    resid[0] = result[:, :half]
    resid[1] = result[:, half:]
    for k, out in enumerate((t0, t1, t2, t3)):
        at = pl.ds(pl.multiple_of(lax.rem(y + k, N) * rows, rows), rows)
        out[:, :half] = resid[0, at, :].astype(BF)
        out[:, half:] = resid[1, at, :].astype(BF)
    ahead.wait()


def merge_kernel(resid, t0, t1, t2, t3, w, select, tail, out, vision):
    sums = t0[...].astype(F32) + t1[...].astype(F32) + t2[...].astype(F32) + t3[...].astype(F32)
    sums = (resid[...].astype(F32) + sums).astype(BF).astype(F32)
    full, width = resid.shape
    count = full // 4
    tiles = width // 128
    for i in range(tiles):
        vision[i * full : (i + 1) * full, :] = sums[:, i * 128 : (i + 1) * 128]
    total = jnp.zeros((count, width), F32)
    for j in range(4):
        rows = [vision[pl.ds(i * full + j, count, stride=4), :] for i in range(tiles)]
        rows = jnp.concatenate(rows, axis=1).astype(BF)
        total += jnp.dot(rows, w[j * width : (j + 1) * width, :], preferred_element_type=F32)
    sent = jnp.dot(select[...], total.astype(BF), preferred_element_type=F32)
    out[:, :width] = sent.astype(BF)
    out[:, width:] = tail[...]


def local(
    patches,
    picture_ids,
    ln_attn,
    w_qkv,
    w_out,
    ln_mlp,
    w_up,
    w_down,
    w_merge,
    text_embed,
    slot_dest,
):
    rows = patches[0]
    count, width = rows.shape
    x = lax.axis_index("x")
    y = lax.axis_index("y")
    c = lax.axis_index("c")
    pos = jnp.stack([x, y, lax.axis_index("z"), c]).astype(jnp.int32)
    ids = picture_ids[0]

    half = width // 2
    w_heads = jnp.transpose(w_qkv, (0, 2, 1)).reshape(3 * HEAD, width)
    w_heads = jnp.concatenate([w_heads, w_out], axis=0)
    w_half = lax.dynamic_slice_in_dim(w_heads, c * half, half, 1)
    near = lax.all_gather(w_half, ("x", "c"), axis=0, tiled=False)
    units = w_down.shape[0] // 2
    packed = jnp.concatenate(
        [
            lax.dynamic_slice_in_dim(w_up.T, c * units, units, 0),
            lax.dynamic_slice_in_dim(w_down, c * units, units, 0),
        ],
        axis=0,
    )
    packed, _ = lax.optimization_barrier((packed, w_half))
    w_near = lax.all_gather(packed, ("x", "c"), axis=0, tiled=False)

    pieces = [rows] + [shift(rows, "y", k) for k in (1, 2, 3)]
    mine = near.reshape(N, 2, near.shape[1], half)
    mine = lax.dynamic_index_in_dim(mine, c, axis=1, keepdims=False)[:, 3 * HEAD :, :]
    mine = mine.reshape(N * HEAD, half)
    mine1 = shift(mine, "y", 1)
    mine3 = shift(mine, "y", 3)

    total_rows = count * N
    h1 = pl.pallas_call(
        norm_kernel,
        out_shape=jax.ShapeDtypeStruct((2, total_rows, half), BF),
        in_specs=[SMEM] + [VMEM] * 5,
        out_specs=VMEM,
        compiler_params=params(16),
        name="norm",
    )(pos, *pieces, ln_attn[None, :])
    qkv = pl.pallas_call(
        qkv_kernel,
        out_shape=[jax.ShapeDtypeStruct((3 * HEAD, total_rows), BF)] * N,
        in_specs=[SMEM, VMEM, HBM],
        out_specs=[VMEM] * N,
        scratch_shapes=[
            pltpu.VMEM((2 * N, 3 * HEAD, half), BF),
            pltpu.SemaphoreType.DMA(()),
        ],
        compiler_params=params(16),
        name="qkv",
    )(pos, h1, far(near))
    blocks = [qkv[0]] + [shift(qkv[k], "x", -k) for k in (1, 2, 3)]
    blocks, mine, mine1, mine3 = lax.optimization_barrier((blocks, mine, mine1, mine3))
    mine2 = shift(mine, "y", 2)
    other1 = swap(mine1)
    other3 = swap(mine3)

    group_rows = ids.shape[0]
    chunk = 256
    chunks = group_rows // chunk
    held = (ids[:, None] == jnp.arange(16)[None, :]).reshape(chunks, chunk, 16)
    held = jnp.any(held, axis=1)
    per = chunks // N
    wanted = jnp.any(held.reshape(N, per, 16), axis=1)
    need = jnp.any(wanted[:, None, :] & held[None, :, :], axis=2)
    where = jnp.arange(chunks)[None, :]
    low = jnp.min(jnp.where(need, where, chunks - 1), axis=1)
    high = jnp.max(jnp.where(need, where + 1, 1), axis=1)
    bounds = jnp.stack([jnp.minimum(low, high - 1), high]).astype(jnp.int32)

    attended = pl.pallas_call(
        attend_kernel,
        out_shape=[jax.ShapeDtypeStruct((HEAD, total_rows), BF)] * N,
        in_specs=[SMEM, SMEM] + [VMEM] * 6,
        out_specs=[VMEM] * N,
        scratch_shapes=[
            pltpu.VMEM((N, HEAD, total_rows), BF),
            pltpu.VMEM((chunks, HEAD, chunk), BF),
            pltpu.VMEM((chunks, HEAD, chunk), BF),
            pltpu.VMEM((2, chunk, total_rows), F32),
            pltpu.VMEM((N, HEAD, total_rows), BF),
        ],
        compiler_params=params(16),
        name="attend",
    )(pos, bounds, *blocks, ids[None, :], ids[:, None])
    attended, mine2, other1, other3 = lax.optimization_barrier(
        (attended, mine2, other1, other3)
    )
    other2 = swap(mine2)
    heads = [attended[0]] + [shift(attended[k], "x", k) for k in (1, 2, 3)]
    heads = pl.pallas_call(
        pack_kernel,
        out_shape=jax.ShapeDtypeStruct((N, HEAD, total_rows), BF),
        in_specs=[SMEM] + [VMEM] * N,
        out_specs=VMEM,
        compiler_params=params(8),
        name="pack",
    )(pos, *heads)
    gathered = [heads] + [shift(heads, "y", k) for k in (1, 2, 3)]

    *part, resid, w_merge = pl.pallas_call(
        mlp_kernel,
        out_shape=[jax.ShapeDtypeStruct((count, width), BF)] * (N + 1)
        + [jax.ShapeDtypeStruct(w_merge.shape, BF)],
        in_specs=[SMEM] + [VMEM] * 9 + [HBM] * 9,
        out_specs=[VMEM] * (N + 2),
        scratch_shapes=[
            pltpu.VMEM((2, total_rows, half), F32),
            pltpu.VMEM((N * N * HEAD, half), BF),
            pltpu.VMEM((N * N * HEAD, half), BF),
            pltpu.VMEM((2 * N, units, width), BF),
            pltpu.VMEM((2 * N, units, width), BF),
            pltpu.SemaphoreType.DMA((4 * N + 3,)),
        ],
        compiler_params=params(32),
        name="mlp",
    )(
        pos,
        *gathered,
        *pieces,
        ln_mlp[None, :],
        *[far(v) for v in (near, w_near, mine1, mine2, mine3)],
        *[far(v) for v in (other1, other2, other3, w_merge)],
    )
    sums = [part[0]] + [shift(part[k], "y", k) for k in (1, 2, 3)]

    merged_count = count // 4
    dest = slot_dest[0]
    prompt_rows = text_embed.shape[0]
    req_count = N * N
    row_count = lax.axis_size("z") * lax.axis_size("c")
    slot_cap = 2
    owner = jnp.where(dest >= 0, dest // prompt_rows // row_count, -1)
    order = jnp.arange(merged_count)
    same_owner = (owner[:, None] == owner[None, :]) & (order[None, :] < order[:, None])
    ranks = jnp.sum(same_owner.astype(jnp.int32), axis=1)
    target = jnp.where(owner >= 0, owner * slot_cap + ranks, -1)
    select = target[None, :] == jnp.arange(req_count * slot_cap)[:, None]
    places = jnp.sum(jnp.where(select, (dest % prompt_rows + 1)[None, :], 0), axis=1)
    lane = jnp.arange(128)[None, :] == 0
    tail = jnp.where(lane, places[:, None], 0).astype(BF)
    outgoing = pl.pallas_call(
        merge_kernel,
        out_shape=jax.ShapeDtypeStruct((req_count * slot_cap, width + 128), BF),
        in_specs=[VMEM] * 8,
        out_specs=VMEM,
        scratch_shapes=[pltpu.VMEM((count * width // 128, 128), F32)],
        compiler_params=params(8),
        name="merge",
    )(resid, *sums, w_merge, select.astype(BF), tail)
    arrived = lax.all_to_all(
        outgoing.reshape(req_count, slot_cap, width + 128),
        ("x", "y"),
        split_axis=0,
        concat_axis=0,
        tiled=True,
    ).reshape(req_count * slot_cap, width + 128)
    landing = arrived[:, width].astype(jnp.int32) - 1
    placer = landing[None, :] == jnp.arange(prompt_rows)[:, None]
    placed = jnp.dot(
        placer.astype(BF), arrived[:, :width], preferred_element_type=F32
    ).astype(BF)
    filled = jnp.any(placer, axis=1)
    return jnp.where(filled[:, None], placed, text_embed)


def solution(mesh):
    grid = Mesh(mesh.devices.reshape(N, N, -1, 2), ("x", "y", "z", "c"))
    req = ("x", "y")
    row = ("z", "c")
    return jax.shard_map(
        local,
        mesh=grid,
        in_specs=(
            P(row, req, None),
            P(row, None),
            P(),
            P(None, None, req),
            P(req, None),
            P(),
            P(None, req),
            P(req, None),
            P(),
            P(("x", "y", "z", "c"), None),
            P(row, req),
        ),
        out_specs=P(("x", "y", "z", "c"), None),
        check_vma=False,
    )
```

```python
import math

import jax
import jax.numpy as jnp
from jax import lax
from jax.experimental import pallas as pl
from jax.experimental.pallas import tpu as pltpu
from jax.sharding import Mesh
from jax.sharding import PartitionSpec as P

HEAD = 80
N = 4
BF = jnp.bfloat16
F32 = jnp.float32
NT = (((1,), (1,)), ((), ()))
TN = (((0,), (0,)), ((), ()))
HBM = pl.BlockSpec(memory_space=pltpu.HBM)
VMEM = pl.BlockSpec(memory_space=pltpu.VMEM)
SMEM = pl.BlockSpec(memory_space=pltpu.SMEM)


def params(mib):
    return pltpu.CompilerParams(vmem_limit_bytes=mib << 20)


def norm_rows(rows32, gain):
    center = rows32 - jnp.mean(rows32, axis=-1, keepdims=True)
    spread = jnp.mean(center * center, axis=-1, keepdims=True)
    return center * lax.rsqrt(spread + 1e-06) * gain


def shift(value, axis, step):
    pairs = [(i, (i + step) % N) for i in range(N)]
    return lax.ppermute(value, axis, pairs)


def far(value):
    return pltpu.with_memory_space_constraint(value, pltpu.HBM)


def swap(value):
    return lax.ppermute(value, "c", [(0, 1), (1, 0)])


def norm_kernel(pos, p0, p1, p2, p3, gain, h1, held, sems):
    y = pos[1]
    half = h1.shape[2]
    rows = p0.shape[0]
    copies = []
    for k, piece in enumerate((p0, p1, p2, p3)):
        copies.append(pltpu.make_async_copy(piece, held.at[k], sems.at[k]))
    for copy in copies:
        copy.start()
    for k in range(N):
        copies[k].wait()
        normed = norm_rows(held[k].astype(F32), gain[...]).astype(BF)
        at = pl.ds(pl.multiple_of(lax.rem(y - k + N, N) * rows, rows), rows)
        h1[0, at, :] = normed[:, :half]
        h1[1, at, :] = normed[:, half:]


def qkv_kernel(pos, h1, w_hbm, o0, o1, o2, o3, share, w, sems):
    x = pos[0]
    c = pos[3]
    cols = w.shape[1]
    copies = []
    for k in range(N):
        at = pl.ds(lax.rem(x - k + N, N) * 2, 2)
        copies.append(pltpu.make_async_copy(w_hbm.at[at, :cols, :], w.at[at], sems.at[k]))
    for j in range(N):
        src = w_hbm.at[2 * j + c, cols : cols + HEAD, :]
        copies.append(pltpu.make_async_copy(src, share.at[j], sems.at[N + j]))
    for copy in copies:
        copy.start()
    for k, out in enumerate((o0, o1, o2, o3)):
        at = lax.rem(x - k + N, N) * 2
        copies[k].wait()
        total = lax.dot_general(w[at], h1[0], NT, preferred_element_type=F32)
        total += lax.dot_general(w[at + 1], h1[1], NT, preferred_element_type=F32)
        out[...] = total.astype(BF)
    for copy in copies[N:]:
        copy.wait()


def attend_kernel(
    pos, bounds, r0, r1, r2, r3, id_row, id_col, o0, o1, o2, o3, qs, ks, vs, scores, outs
):
    x = pos[0]
    chunk = ks.shape[2]
    block = qs.shape[2]
    per = block // chunk
    scale = math.log2(math.e) / math.sqrt(HEAD)
    rows = block // N
    y = pos[1]
    for k, piece in enumerate((r0, r1, r2, r3)):
        at = lax.rem(x + k, N)
        qs[at] = piece[:HEAD, :]
        for j in range(per):
            cols = slice(j * chunk, (j + 1) * chunk)
            ks[at * per + j] = piece[HEAD : 2 * HEAD, cols]
            vs[at * per + j] = piece[2 * HEAD :, cols]

    for qb in range(N):
        low = bounds[0, qb]
        high = bounds[1, qb]
        query = qs[qb]
        query_ids = id_row[:, qb * block : (qb + 1) * block]

        def score(kc, query=query):
            return lax.dot_general(ks[kc], query, TN, preferred_element_type=F32)

        scores[0] = score(low)

        def step(i, carry, query=query, query_ids=query_ids, low=low, high=high):
            top, total, acc = carry
            slot = lax.rem(i - low, 2)
            raw = scores[slot]
            scores[1 - slot] = score(jnp.minimum(i + 1, high - 1))
            key_ids = id_col[pl.ds(pl.multiple_of(i * chunk, chunk), chunk), :]
            val = jnp.where(key_ids == query_ids, raw * scale, -1e30)
            new_top = jnp.maximum(top, jnp.max(val, axis=0, keepdims=True))
            alpha = jnp.exp2(top - new_top)
            expo = jnp.exp2(val - new_top)
            total = total * alpha + jnp.sum(expo, axis=0, keepdims=True)
            acc = acc * alpha + jnp.dot(vs[i], expo.astype(BF), preferred_element_type=F32)
            return new_top, total, acc

        start = (
            jnp.full((1, block), -1e30, F32),
            jnp.zeros((1, block), F32),
            jnp.zeros((HEAD, block), F32),
        )
        top, total, acc = lax.fori_loop(low, high, step, start)
        result = (acc / total).astype(BF)
        for yb in range(N):
            part = result[:, yb * rows : (yb + 1) * rows]
            outs[lax.rem(yb - y + N, N), :, qb * rows : (qb + 1) * rows] = part
    for k, out in enumerate((o0, o1, o2, o3)):
        out[...] = outs[k]


def pack_kernel(pos, g0, g1, g2, g3, out):
    y = pos[1]
    for k, piece in enumerate((g0, g1, g2, g3)):
        out[lax.rem(y - k + N, N)] = piece[...]


def mlp_kernel(pos, *refs):
    gathered = refs[0:4]
    pieces = refs[4:8]
    gain, near, w_hbm = refs[8:11]
    mine = refs[11:14]
    other = refs[14:17]
    merge_hbm = refs[17]
    t0, t1, t2, t3, own, w_merge, resid, w_mine, w_other, up, down, held, sems = refs[18:]
    x = pos[0]
    y = pos[1]
    c = pos[3]
    rows = pieces[0].shape[0]
    half = w_mine.shape[1]
    group = N * HEAD
    skip = near.shape[1] - HEAD
    first = []
    for k in range(N):
        for j in range(N):
            at = (lax.rem(x - j + N, N) * N + lax.rem(y - k + N, N)) * HEAD
            to = pl.ds(pl.multiple_of(at, 16), HEAD)
            if k == 0:
                sources = (
                    near.at[2 * j + c, skip : skip + HEAD, :],
                    near.at[2 * j + 1 - c, skip : skip + HEAD, :],
                )
            else:
                sources = (mine[k - 1].at[j], other[k - 1].at[j])
            for src, dst in zip(sources, (w_mine, w_other)):
                sem = sems.at[len(first)]
                first.append(pltpu.make_async_copy(src, dst.at[to, :], sem))
    for k in range(N):
        sem = sems.at[len(first)]
        first.append(pltpu.make_async_copy(pieces[k], held.at[k], sem))
    units = up.shape[1]
    second = [
        pltpu.make_async_copy(w_hbm.at[:, :units, :], up, sems.at[36]),
        pltpu.make_async_copy(w_hbm.at[:, units:, :], down, sems.at[37]),
    ]
    ahead = pltpu.make_async_copy(merge_hbm, w_merge, sems.at[38])
    for copy in first + second + [ahead]:
        copy.start()
    lhs = jnp.concatenate([g[...].reshape(group, N * rows) for g in gathered], axis=0)
    for copy in first:
        copy.wait()
    resid[c] = lax.dot_general(lhs, w_mine[...], TN, preferred_element_type=F32)
    resid[1 - c] = lax.dot_general(lhs, w_other[...], TN, preferred_element_type=F32)
    for k in range(N):
        at = pl.ds(pl.multiple_of(lax.rem(x - k + N, N) * rows, rows), rows)
        for h in (0, 1):
            start = held[k, :, h * half : (h + 1) * half].astype(F32)
            resid[h, at, :] = (resid[h, at, :] + start).astype(BF).astype(F32)
            if k == 0:
                own[:, h * half : (h + 1) * half] = resid[h, at, :].astype(BF)
    full = jnp.concatenate([resid[0], resid[1]], axis=1)
    normed = norm_rows(full, gain[...]).astype(BF)
    width = 2 * half
    count = up.shape[0] * units
    second[0].wait()
    hidden = lax.dot_general(
        normed, up[...].reshape(count, width), NT, preferred_element_type=F32
    )
    hidden = (0.5 * hidden * (1.0 + lax.erf(hidden * math.sqrt(0.5)))).astype(BF)
    second[1].wait()
    result = jnp.dot(hidden, down[...].reshape(count, width), preferred_element_type=F32)
    resid[0] = result[:, :half]
    resid[1] = result[:, half:]
    for k, out in enumerate((t0, t1, t2, t3)):
        at = pl.ds(pl.multiple_of(lax.rem(x + k, N) * rows, rows), rows)
        out[:, :half] = resid[0, at, :].astype(BF)
        out[:, half:] = resid[1, at, :].astype(BF)
    ahead.wait()


def merge_kernel(resid, t0, t1, t2, t3, w, select, tail, out, vision):
    sums = t0[...].astype(F32) + t1[...].astype(F32) + t2[...].astype(F32) + t3[...].astype(F32)
    sums = (resid[...].astype(F32) + sums).astype(BF).astype(F32)
    full, width = resid.shape
    count = full // 4
    tiles = width // 128
    for i in range(tiles):
        vision[i * full : (i + 1) * full, :] = sums[:, i * 128 : (i + 1) * 128]
    total = jnp.zeros((count, width), F32)
    for j in range(4):
        rows = [vision[pl.ds(i * full + j, count, stride=4), :] for i in range(tiles)]
        rows = jnp.concatenate(rows, axis=1).astype(BF)
        total += jnp.dot(rows, w[j * width : (j + 1) * width, :], preferred_element_type=F32)
    sent = jnp.dot(select[...], total.astype(BF), preferred_element_type=F32)
    out[:, :width] = sent.astype(BF)
    out[:, width:] = tail[...]


def local(
    patches,
    picture_ids,
    ln_attn,
    w_qkv,
    w_out,
    ln_mlp,
    w_up,
    w_down,
    w_merge,
    text_embed,
    slot_dest,
):
    rows = patches[0]
    count, width = rows.shape
    x = lax.axis_index("x")
    y = lax.axis_index("y")
    c = lax.axis_index("c")
    pos = jnp.stack([x, y, lax.axis_index("z"), c]).astype(jnp.int32)
    ids = picture_ids[0]

    half = width // 2
    w_heads = jnp.transpose(w_qkv, (0, 2, 1)).reshape(3 * HEAD, width)
    w_heads = jnp.concatenate([w_heads, w_out], axis=0)
    w_half = lax.dynamic_slice_in_dim(w_heads, c * half, half, 1)
    near = lax.all_gather(w_half, ("x", "c"), axis=0, tiled=False)
    units = w_down.shape[0] // 2
    packed = jnp.concatenate(
        [
            lax.dynamic_slice_in_dim(w_up.T, c * units, units, 0),
            lax.dynamic_slice_in_dim(w_down, c * units, units, 0),
        ],
        axis=0,
    )
    packed, _ = lax.optimization_barrier((packed, w_half))
    w_near = lax.all_gather(packed, ("y", "c"), axis=0, tiled=False)

    pieces = [rows] + [shift(rows, "y", k) for k in (1, 2, 3)]
    across = [rows] + [shift(rows, "x", k) for k in (1, 2, 3)]

    total_rows = count * N
    h1 = pl.pallas_call(
        norm_kernel,
        out_shape=jax.ShapeDtypeStruct((2, total_rows, half), BF),
        in_specs=[SMEM] + [HBM] * N + [VMEM],
        out_specs=VMEM,
        scratch_shapes=[
            pltpu.VMEM((N, count, width), BF),
            pltpu.SemaphoreType.DMA((N,)),
        ],
        compiler_params=params(16),
        name="norm",
    )(pos, *[far(piece) for piece in pieces], ln_attn[None, :])
    near, h1, across = lax.optimization_barrier((near, h1, across))
    *qkv, mine = pl.pallas_call(
        qkv_kernel,
        out_shape=[jax.ShapeDtypeStruct((3 * HEAD, total_rows), BF)] * N
        + [jax.ShapeDtypeStruct((N, HEAD, half), BF)],
        in_specs=[SMEM, VMEM, HBM],
        out_specs=[VMEM] * (N + 1),
        scratch_shapes=[
            pltpu.VMEM((2 * N, 3 * HEAD, half), BF),
            pltpu.SemaphoreType.DMA((2 * N,)),
        ],
        compiler_params=params(16),
        name="qkv",
    )(pos, h1, far(near))
    blocks = [qkv[0]] + [shift(qkv[k], "x", -k) for k in (1, 2, 3)]
    pass1 = shift(mine, "y", 1)
    pass3 = shift(mine, "y", 3)
    blocks, mine, pass1, pass3 = lax.optimization_barrier((blocks, mine, pass1, pass3))
    pass2 = shift(mine, "y", 2)
    swap1 = swap(pass1)
    swap3 = swap(pass3)

    group_rows = ids.shape[0]
    chunk = 256
    chunks = group_rows // chunk
    held = (ids[:, None] == jnp.arange(16)[None, :]).reshape(chunks, chunk, 16)
    held = jnp.any(held, axis=1)
    per = chunks // N
    wanted = jnp.any(held.reshape(N, per, 16), axis=1)
    need = jnp.any(wanted[:, None, :] & held[None, :, :], axis=2)
    where = jnp.arange(chunks)[None, :]
    low = jnp.min(jnp.where(need, where, chunks - 1), axis=1)
    high = jnp.max(jnp.where(need, where + 1, 1), axis=1)
    bounds = jnp.stack([jnp.minimum(low, high - 1), high]).astype(jnp.int32)

    attended = pl.pallas_call(
        attend_kernel,
        out_shape=[jax.ShapeDtypeStruct((HEAD, total_rows), BF)] * N,
        in_specs=[SMEM, SMEM] + [VMEM] * 6,
        out_specs=[VMEM] * N,
        scratch_shapes=[
            pltpu.VMEM((N, HEAD, total_rows), BF),
            pltpu.VMEM((chunks, HEAD, chunk), BF),
            pltpu.VMEM((chunks, HEAD, chunk), BF),
            pltpu.VMEM((2, chunk, total_rows), F32),
            pltpu.VMEM((N, HEAD, total_rows), BF),
        ],
        compiler_params=params(16),
        name="attend",
    )(pos, bounds, *blocks, ids[None, :], ids[:, None])
    attended, pass2, swap1, swap3 = lax.optimization_barrier((attended, pass2, swap1, swap3))
    heads = [attended[0]] + [shift(attended[k], "y", k) for k in (1, 2, 3)]
    heads = pl.pallas_call(
        pack_kernel,
        out_shape=jax.ShapeDtypeStruct((N, HEAD, total_rows), BF),
        in_specs=[SMEM] + [VMEM] * N,
        out_specs=VMEM,
        compiler_params=params(8),
        name="pack",
    )(pos, *heads)
    gathered = [heads] + [shift(heads, "x", k) for k in (1, 2, 3)]
    swap2 = swap(pass2)
    passed = [pass1, pass2, pass3]
    swapped = [swap1, swap2, swap3]

    *part, resid, w_merge = pl.pallas_call(
        mlp_kernel,
        out_shape=[jax.ShapeDtypeStruct((count, width), BF)] * (N + 1)
        + [jax.ShapeDtypeStruct(w_merge.shape, BF)],
        in_specs=[SMEM] + [VMEM] * N + [HBM] * N + [VMEM] + [HBM] * 9,
        out_specs=[VMEM] * (N + 2),
        scratch_shapes=[
            pltpu.VMEM((2, total_rows, half), F32),
            pltpu.VMEM((N * N * HEAD, half), BF),
            pltpu.VMEM((N * N * HEAD, half), BF),
            pltpu.VMEM((2 * N, units, width), BF),
            pltpu.VMEM((2 * N, units, width), BF),
            pltpu.VMEM((N, count, width), BF),
            pltpu.SemaphoreType.DMA((39,)),
        ],
        compiler_params=params(32),
        name="mlp",
    )(
        pos,
        *gathered,
        *[far(v) for v in across],
        ln_mlp[None, :],
        *[far(v) for v in (near, w_near, *passed, *swapped, w_merge)],
    )
    sums = [part[0]] + [shift(part[k], "x", k) for k in (1, 2, 3)]

    merged_count = count // 4
    dest = slot_dest[0]
    prompt_rows = text_embed.shape[0]
    req_count = N * N
    row_count = lax.axis_size("z") * lax.axis_size("c")
    slot_cap = 2
    owner = jnp.where(dest >= 0, dest // prompt_rows // row_count, -1)
    order = jnp.arange(merged_count)
    same_owner = (owner[:, None] == owner[None, :]) & (order[None, :] < order[:, None])
    ranks = jnp.sum(same_owner.astype(jnp.int32), axis=1)
    target = jnp.where(owner >= 0, owner * slot_cap + ranks, -1)
    select = target[None, :] == jnp.arange(req_count * slot_cap)[:, None]
    places = jnp.sum(jnp.where(select, (dest % prompt_rows + 1)[None, :], 0), axis=1)
    lane = jnp.arange(128)[None, :] == 0
    tail = jnp.where(lane, places[:, None], 0).astype(BF)
    outgoing = pl.pallas_call(
        merge_kernel,
        out_shape=jax.ShapeDtypeStruct((req_count * slot_cap, width + 128), BF),
        in_specs=[VMEM] * 8,
        out_specs=VMEM,
        scratch_shapes=[pltpu.VMEM((count * width // 128, 128), F32)],
        compiler_params=params(8),
        name="merge",
    )(resid, *sums, w_merge, select.astype(BF), tail)
    arrived = lax.all_to_all(
        outgoing.reshape(req_count, slot_cap, width + 128),
        ("x", "y"),
        split_axis=0,
        concat_axis=0,
        tiled=True,
    ).reshape(req_count * slot_cap, width + 128)
    landing = arrived[:, width].astype(jnp.int32) - 1
    placer = landing[None, :] == jnp.arange(prompt_rows)[:, None]
    placed = jnp.dot(
        placer.astype(BF), arrived[:, :width], preferred_element_type=F32
    ).astype(BF)
    filled = jnp.any(placer, axis=1)
    return jnp.where(filled[:, None], placed, text_embed)


def solution(mesh):
    grid = Mesh(mesh.devices.reshape(N, N, -1, 2), ("x", "y", "z", "c"))
    req = ("x", "y")
    row = ("z", "c")
    return jax.shard_map(
        local,
        mesh=grid,
        in_specs=(
            P(row, req, None),
            P(row, None),
            P(),
            P(None, None, req),
            P(req, None),
            P(),
            P(None, req),
            P(req, None),
            P(),
            P(("x", "y", "z", "c"), None),
            P(row, req),
        ),
        out_specs=P(("x", "y", "z", "c"), None),
        check_vma=False,
    )
```

```python
import math

import jax
import jax.numpy as jnp
from jax import lax
from jax.experimental import pallas as pl
from jax.experimental.pallas import tpu as pltpu
from jax.sharding import Mesh
from jax.sharding import PartitionSpec as P

HEAD = 80
N = 4
BF = jnp.bfloat16
F32 = jnp.float32
NT = (((1,), (1,)), ((), ()))
TN = (((0,), (0,)), ((), ()))
HBM = pl.BlockSpec(memory_space=pltpu.HBM)
VMEM = pl.BlockSpec(memory_space=pltpu.VMEM)
SMEM = pl.BlockSpec(memory_space=pltpu.SMEM)


def params(mib):
    return pltpu.CompilerParams(vmem_limit_bytes=mib << 20)


def norm_rows(rows32, gain):
    center = rows32 - jnp.mean(rows32, axis=-1, keepdims=True)
    spread = jnp.mean(center * center, axis=-1, keepdims=True)
    return center * lax.rsqrt(spread + 1e-06) * gain


def shift(value, axis, step):
    pairs = [(i, (i + step) % N) for i in range(N)]
    return lax.ppermute(value, axis, pairs)


def far(value):
    return pltpu.with_memory_space_constraint(value, pltpu.HBM)


def swap(value):
    return lax.ppermute(value, "c", [(0, 1), (1, 0)])


def norm_kernel(pos, p0, p1, p2, p3, gain, h1, held, sems):
    y = pos[1]
    half = h1.shape[2]
    rows = p0.shape[0]
    copies = []
    for k, piece in enumerate((p0, p1, p2, p3)):
        copies.append(pltpu.make_async_copy(piece, held.at[k], sems.at[k]))
    for copy in copies:
        copy.start()
    for k in range(N):
        copies[k].wait()
        normed = norm_rows(held[k].astype(F32), gain[...]).astype(BF)
        at = pl.ds(pl.multiple_of(lax.rem(y - k + N, N) * rows, rows), rows)
        h1[0, at, :] = normed[:, :half]
        h1[1, at, :] = normed[:, half:]


def qkv_kernel(pos, h1, w_hbm, o0, o1, o2, o3, share, w, sems):
    x = pos[0]
    c = pos[3]
    cols = w.shape[1]
    copies = []
    for k in range(N):
        at = pl.ds(lax.rem(x - k + N, N) * 2, 2)
        copies.append(pltpu.make_async_copy(w_hbm.at[at, :cols, :], w.at[at], sems.at[k]))
    for j in range(N):
        src = w_hbm.at[2 * j + c, cols : cols + HEAD, :]
        copies.append(pltpu.make_async_copy(src, share.at[j], sems.at[N + j]))
    for copy in copies:
        copy.start()
    for k, out in enumerate((o0, o1, o2, o3)):
        at = lax.rem(x - k + N, N) * 2
        copies[k].wait()
        total = lax.dot_general(w[at], h1[0], NT, preferred_element_type=F32)
        total += lax.dot_general(w[at + 1], h1[1], NT, preferred_element_type=F32)
        out[...] = total.astype(BF)
    for copy in copies[N:]:
        copy.wait()


def attend_kernel(
    pos, bounds, r0, r1, r2, r3, id_row, id_col, o0, o1, o2, o3, qs, ks, vs, scores, outs
):
    x = pos[0]
    chunk = ks.shape[2]
    block = qs.shape[2]
    per = block // chunk
    scale = math.log2(math.e) / math.sqrt(HEAD)
    for k, piece in enumerate((r0, r1, r2, r3)):
        at = lax.rem(x + k, N)
        qs[at] = piece[:HEAD, :]
        for j in range(per):
            cols = slice(j * chunk, (j + 1) * chunk)
            ks[at * per + j] = piece[HEAD : 2 * HEAD, cols]
            vs[at * per + j] = piece[2 * HEAD :, cols]

    for qb in range(N):
        low = bounds[0, qb]
        high = bounds[1, qb]
        query = qs[qb]
        query_ids = id_row[:, qb * block : (qb + 1) * block]

        def score(kc, query=query):
            return lax.dot_general(ks[kc], query, TN, preferred_element_type=F32)

        scores[0] = score(low)

        def step(i, carry, query=query, query_ids=query_ids, low=low, high=high):
            top, total, acc = carry
            slot = lax.rem(i - low, 2)
            raw = scores[slot]
            scores[1 - slot] = score(jnp.minimum(i + 1, high - 1))
            key_ids = id_col[pl.ds(pl.multiple_of(i * chunk, chunk), chunk), :]
            val = jnp.where(key_ids == query_ids, raw * scale, -1e30)
            new_top = jnp.maximum(top, jnp.max(val, axis=0, keepdims=True))
            alpha = jnp.exp2(top - new_top)
            expo = jnp.exp2(val - new_top)
            total = total * alpha + jnp.sum(expo, axis=0, keepdims=True)
            acc = acc * alpha + jnp.dot(vs[i], expo.astype(BF), preferred_element_type=F32)
            return new_top, total, acc

        start = (
            jnp.full((1, block), -1e30, F32),
            jnp.zeros((1, block), F32),
            jnp.zeros((HEAD, block), F32),
        )
        top, total, acc = lax.fori_loop(low, high, step, start)
        outs[lax.rem(qb - x + N, N)] = (acc / total).astype(BF)
    for k, out in enumerate((o0, o1, o2, o3)):
        out[...] = outs[k]


def pack_kernel(pos, g0, g1, g2, g3, out):
    x = pos[0]
    for k, piece in enumerate((g0, g1, g2, g3)):
        out[lax.rem(x - k + N, N)] = piece[...]


def mlp_kernel(pos, *refs):
    gathered = refs[0:4]
    pieces = refs[4:8]
    gain, near, w_hbm = refs[8:11]
    mine = refs[11:14]
    other = refs[14:17]
    merge_hbm = refs[17]
    t0, t1, t2, t3, own, w_merge, resid, w_mine, w_other, up, down, held, sems = refs[18:]
    y = pos[1]
    c = pos[3]
    rows = pieces[0].shape[0]
    half = w_mine.shape[2]
    group = N * HEAD
    skip = near.shape[1] - HEAD
    moves = []
    for j in range(N):
        moves.append((near.at[2 * j + c, skip : skip + HEAD, :], w_mine.at[j]))
        moves.append((near.at[2 * j + 1 - c, skip : skip + HEAD, :], w_other.at[j]))
    for k in range(1, N):
        to = slice(k * N, (k + 1) * N)
        moves.append((mine[k - 1], w_mine.at[to]))
        moves.append((other[k - 1], w_other.at[to]))
    for k in range(N):
        moves.append((pieces[k], held.at[k]))
    early = len(moves)
    units = up.shape[1]
    for h in (0, 1):
        cols = slice(h * half, (h + 1) * half)
        moves.append((w_hbm.at[:, h, :units, :], up.at[:, :, cols]))
    for h in (0, 1):
        cols = slice(h * half, (h + 1) * half)
        moves.append((w_hbm.at[:, h, units:, :], down.at[:, :, cols]))
    moves.append((merge_hbm, w_merge))
    copies = [pltpu.make_async_copy(a, b, sems.at[i]) for i, (a, b) in enumerate(moves)]
    for copy in copies:
        copy.start()
    lhs = jnp.concatenate([g[...].reshape(group, N * rows) for g in gathered], axis=0)
    for copy in copies[:early]:
        copy.wait()
    heads = N * group
    part = w_mine[...].reshape(heads, half)
    resid[c] = lax.dot_general(lhs, part, TN, preferred_element_type=F32)
    part = w_other[...].reshape(heads, half)
    resid[1 - c] = lax.dot_general(lhs, part, TN, preferred_element_type=F32)
    for k in range(N):
        at = pl.ds(pl.multiple_of(lax.rem(y - k + N, N) * rows, rows), rows)
        for h in (0, 1):
            start = held[k, :, h * half : (h + 1) * half].astype(F32)
            resid[h, at, :] = (resid[h, at, :] + start).astype(BF).astype(F32)
            if k == 0:
                own[:, h * half : (h + 1) * half] = resid[h, at, :].astype(BF)
    full = jnp.concatenate([resid[0], resid[1]], axis=1)
    normed = norm_rows(full, gain[...]).astype(BF)
    width = 2 * half
    count = up.shape[0] * units
    copies[early].wait()
    copies[early + 1].wait()
    hidden = lax.dot_general(
        normed, up[...].reshape(count, width), NT, preferred_element_type=F32
    )
    hidden = (0.5 * hidden * (1.0 + lax.erf(hidden * math.sqrt(0.5)))).astype(BF)
    copies[early + 2].wait()
    copies[early + 3].wait()
    result = jnp.dot(hidden, down[...].reshape(count, width), preferred_element_type=F32)
    resid[0] = result[:, :half]
    resid[1] = result[:, half:]
    for k, out in enumerate((t0, t1, t2, t3)):
        at = pl.ds(pl.multiple_of(lax.rem(y + k, N) * rows, rows), rows)
        out[:, :half] = resid[0, at, :].astype(BF)
        out[:, half:] = resid[1, at, :].astype(BF)
    copies[early + 4].wait()


def merge_kernel(resid, t0, t1, t2, t3, w, select, tail, out, vision):
    sums = t0[...].astype(F32) + t1[...].astype(F32) + t2[...].astype(F32) + t3[...].astype(F32)
    sums = (resid[...].astype(F32) + sums).astype(BF).astype(F32)
    full, width = resid.shape
    count = full // 4
    tiles = width // 128
    for i in range(tiles):
        vision[i * full : (i + 1) * full, :] = sums[:, i * 128 : (i + 1) * 128]
    total = jnp.zeros((count, width), F32)
    for j in range(4):
        rows = [vision[pl.ds(i * full + j, count, stride=4), :] for i in range(tiles)]
        rows = jnp.concatenate(rows, axis=1).astype(BF)
        total += jnp.dot(rows, w[j * width : (j + 1) * width, :], preferred_element_type=F32)
    sent = jnp.dot(select[...], total.astype(BF), preferred_element_type=F32)
    out[:, :width] = sent.astype(BF)
    out[:, width:] = tail[...]


def local(
    patches,
    picture_ids,
    ln_attn,
    w_qkv,
    w_out,
    ln_mlp,
    w_up,
    w_down,
    w_merge,
    text_embed,
    slot_dest,
):
    rows = patches[0]
    count, width = rows.shape
    x = lax.axis_index("x")
    y = lax.axis_index("y")
    c = lax.axis_index("c")
    pos = jnp.stack([x, y, lax.axis_index("z"), c]).astype(jnp.int32)
    ids = picture_ids[0]

    half = width // 2
    w_heads = jnp.transpose(w_qkv, (0, 2, 1)).reshape(3 * HEAD, width)
    w_heads = jnp.concatenate([w_heads, w_out], axis=0)
    w_half = lax.dynamic_slice_in_dim(w_heads, c * half, half, 1)
    near = lax.all_gather(w_half, ("x", "c"), axis=0, tiled=False)
    z = lax.axis_index("z")
    units = w_down.shape[0] // N
    sizes = (units, half)
    packed = jnp.concatenate(
        [
            lax.dynamic_slice(w_up.T, (z * units, c * half), sizes),
            lax.dynamic_slice(w_down, (z * units, c * half), sizes),
        ],
        axis=0,
    )
    packed, _ = lax.optimization_barrier((packed, w_half))
    w_near = lax.all_gather(packed, ("x", "z", "c"), axis=0, tiled=False)
    w_near = w_near.reshape(N * N, 2, 2 * units, half)

    pieces = [rows] + [shift(rows, "y", k) for k in (1, 2, 3)]
    total_rows = count * N
    h1 = pl.pallas_call(
        norm_kernel,
        out_shape=jax.ShapeDtypeStruct((2, total_rows, half), BF),
        in_specs=[SMEM] + [HBM] * N + [VMEM],
        out_specs=VMEM,
        scratch_shapes=[
            pltpu.VMEM((N, count, width), BF),
            pltpu.SemaphoreType.DMA((N,)),
        ],
        compiler_params=params(16),
        name="norm",
    )(pos, *[far(piece) for piece in pieces], ln_attn[None, :])
    near, h1 = lax.optimization_barrier((near, h1))
    *qkv, mine = pl.pallas_call(
        qkv_kernel,
        out_shape=[jax.ShapeDtypeStruct((3 * HEAD, total_rows), BF)] * N
        + [jax.ShapeDtypeStruct((N, HEAD, half), BF)],
        in_specs=[SMEM, VMEM, HBM],
        out_specs=[VMEM] * (N + 1),
        scratch_shapes=[
            pltpu.VMEM((2 * N, 3 * HEAD, half), BF),
            pltpu.SemaphoreType.DMA((2 * N,)),
        ],
        compiler_params=params(16),
        name="qkv",
    )(pos, h1, far(near))
    blocks = [qkv[0]] + [shift(qkv[k], "x", -k) for k in (1, 2, 3)]
    pass1 = shift(mine, "y", 1)
    pass3 = shift(mine, "y", 3)
    blocks, mine, pass1, pass3 = lax.optimization_barrier((blocks, mine, pass1, pass3))
    pass2 = shift(mine, "y", 2)
    swap1 = swap(pass1)
    swap3 = swap(pass3)

    group_rows = ids.shape[0]
    chunk = 256
    chunks = group_rows // chunk
    held = (ids[:, None] == jnp.arange(16)[None, :]).reshape(chunks, chunk, 16)
    held = jnp.any(held, axis=1)
    per = chunks // N
    wanted = jnp.any(held.reshape(N, per, 16), axis=1)
    need = jnp.any(wanted[:, None, :] & held[None, :, :], axis=2)
    where = jnp.arange(chunks)[None, :]
    low = jnp.min(jnp.where(need, where, chunks - 1), axis=1)
    high = jnp.max(jnp.where(need, where + 1, 1), axis=1)
    bounds = jnp.stack([jnp.minimum(low, high - 1), high]).astype(jnp.int32)

    attended = pl.pallas_call(
        attend_kernel,
        out_shape=[jax.ShapeDtypeStruct((HEAD, total_rows), BF)] * N,
        in_specs=[SMEM, SMEM] + [VMEM] * 6,
        out_specs=[VMEM] * N,
        scratch_shapes=[
            pltpu.VMEM((N, HEAD, total_rows), BF),
            pltpu.VMEM((chunks, HEAD, chunk), BF),
            pltpu.VMEM((chunks, HEAD, chunk), BF),
            pltpu.VMEM((2, chunk, total_rows), F32),
            pltpu.VMEM((N, HEAD, total_rows), BF),
        ],
        compiler_params=params(16),
        name="attend",
    )(pos, bounds, *blocks, ids[None, :], ids[:, None])
    attended, pass2, swap1, swap3 = lax.optimization_barrier((attended, pass2, swap1, swap3))
    swap2 = swap(pass2)
    heads = [attended[0]] + [shift(attended[k], "x", k) for k in (1, 2, 3)]
    heads = pl.pallas_call(
        pack_kernel,
        out_shape=jax.ShapeDtypeStruct((N, HEAD, total_rows), BF),
        in_specs=[SMEM] + [VMEM] * N,
        out_specs=VMEM,
        compiler_params=params(8),
        name="pack",
    )(pos, *heads)
    gathered = [heads] + [shift(heads, "y", k) for k in (1, 2, 3)]

    *part, resid, w_merge = pl.pallas_call(
        mlp_kernel,
        out_shape=[jax.ShapeDtypeStruct((count, width), BF)] * (N + 1)
        + [jax.ShapeDtypeStruct(w_merge.shape, BF)],
        in_specs=[SMEM] + [VMEM] * N + [HBM] * N + [VMEM] + [HBM] * 9,
        out_specs=[VMEM] * (N + 2),
        scratch_shapes=[
            pltpu.VMEM((2, total_rows, half), F32),
            pltpu.VMEM((N * N, HEAD, half), BF),
            pltpu.VMEM((N * N, HEAD, half), BF),
            pltpu.VMEM((N * N, units, width), BF),
            pltpu.VMEM((N * N, units, width), BF),
            pltpu.VMEM((N, count, width), BF),
            pltpu.SemaphoreType.DMA((23,)),
        ],
        compiler_params=params(32),
        name="mlp",
    )(
        pos,
        *gathered,
        *[far(v) for v in pieces],
        ln_mlp[None, :],
        *[far(v) for v in (near, w_near, pass1, pass2, pass3)],
        *[far(v) for v in (swap1, swap2, swap3, w_merge)],
    )
    sums = [part[0]] + [shift(part[k], "y", k) for k in (1, 2, 3)]

    merged_count = count // 4
    dest = slot_dest[0]
    prompt_rows = text_embed.shape[0]
    req_count = N * N
    row_count = lax.axis_size("z") * lax.axis_size("c")
    slot_cap = 2
    owner = jnp.where(dest >= 0, dest // prompt_rows // row_count, -1)
    order = jnp.arange(merged_count)
    same_owner = (owner[:, None] == owner[None, :]) & (order[None, :] < order[:, None])
    ranks = jnp.sum(same_owner.astype(jnp.int32), axis=1)
    target = jnp.where(owner >= 0, owner * slot_cap + ranks, -1)
    select = target[None, :] == jnp.arange(req_count * slot_cap)[:, None]
    places = jnp.sum(jnp.where(select, (dest % prompt_rows + 1)[None, :], 0), axis=1)
    lane = jnp.arange(128)[None, :] == 0
    tail = jnp.where(lane, places[:, None], 0).astype(BF)
    outgoing = pl.pallas_call(
        merge_kernel,
        out_shape=jax.ShapeDtypeStruct((req_count * slot_cap, width + 128), BF),
        in_specs=[VMEM] * 8,
        out_specs=VMEM,
        scratch_shapes=[pltpu.VMEM((count * width // 128, 128), F32)],
        compiler_params=params(8),
        name="merge",
    )(resid, *sums, w_merge, select.astype(BF), tail)
    arrived = lax.all_to_all(
        outgoing.reshape(req_count, slot_cap, width + 128),
        ("x", "y"),
        split_axis=0,
        concat_axis=0,
        tiled=True,
    ).reshape(req_count * slot_cap, width + 128)
    landing = arrived[:, width].astype(jnp.int32) - 1
    placer = landing[None, :] == jnp.arange(prompt_rows)[:, None]
    placed = jnp.dot(
        placer.astype(BF), arrived[:, :width], preferred_element_type=F32
    ).astype(BF)
    filled = jnp.any(placer, axis=1)
    return jnp.where(filled[:, None], placed, text_embed)


def solution(mesh):
    grid = Mesh(mesh.devices.reshape(N, N, -1, 2), ("x", "y", "z", "c"))
    req = ("x", "y")
    row = ("z", "c")
    return jax.shard_map(
        local,
        mesh=grid,
        in_specs=(
            P(row, req, None),
            P(row, None),
            P(),
            P(None, None, req),
            P(req, None),
            P(),
            P(None, req),
            P(req, None),
            P(),
            P(("x", "y", "z", "c"), None),
            P(row, req),
        ),
        out_specs=P(("x", "y", "z", "c"), None),
        check_vma=False,
    )
```

```python
import functools
import math

import jax
import jax.numpy as jnp
from jax import lax
from jax.experimental import pallas as pl
from jax.experimental.pallas import tpu as pltpu
from jax.sharding import Mesh
from jax.sharding import PartitionSpec as P

HEAD = 80
SCALE = math.log2(math.e) / math.sqrt(HEAD)
N = 4
BF = jnp.bfloat16
F32 = jnp.float32
NT = (((1,), (1,)), ((), ()))
TN = (((0,), (0,)), ((), ()))
HBM = pl.BlockSpec(memory_space=pltpu.HBM)
VMEM = pl.BlockSpec(memory_space=pltpu.VMEM)
SMEM = pl.BlockSpec(memory_space=pltpu.SMEM)


def params(mib):
    return pltpu.CompilerParams(vmem_limit_bytes=mib << 20)


def norm_rows(rows32, gain):
    center = rows32 - jnp.mean(rows32, axis=-1, keepdims=True)
    spread = jnp.mean(center * center, axis=-1, keepdims=True)
    return center * lax.rsqrt(spread + 1e-06) * gain


def shift(value, axis, step):
    pairs = [(i, (i + step) % N) for i in range(N)]
    return lax.ppermute(value, axis, pairs)


def far(value):
    return pltpu.with_memory_space_constraint(value, pltpu.HBM)


def swap(value):
    return lax.ppermute(value, "c", [(0, 1), (1, 0)])


def norm_kernel(pos, p0, p1, p2, p3, gain, h1, held, sems):
    y = pos[1]
    half = h1.shape[2]
    rows = p0.shape[0]
    copies = []
    for k, piece in enumerate((p0, p1, p2, p3)):
        copies.append(pltpu.make_async_copy(piece, held.at[k], sems.at[k]))
    for copy in copies:
        copy.start()
    for k in range(N):
        copies[k].wait()
        normed = norm_rows(held[k].astype(F32), gain[...]).astype(BF)
        at = pl.ds(pl.multiple_of(lax.rem(y - k + N, N) * rows, rows), rows)
        h1[0, at, :] = normed[:, :half]
        h1[1, at, :] = normed[:, half:]


def qkv_kernel(pos, h1, w_hbm, o0, o1, o2, o3, share, w, sems):
    x = pos[0]
    c = pos[3]
    cols = w.shape[1]
    copies = []
    for k in range(N):
        at = pl.ds(lax.rem(x - k + N, N) * 2, 2)
        copies.append(pltpu.make_async_copy(w_hbm.at[at, :cols, :], w.at[at], sems.at[k]))
    for j in range(N):
        src = w_hbm.at[2 * j + c, cols : cols + HEAD, :]
        copies.append(pltpu.make_async_copy(src, share.at[j], sems.at[N + j]))
    for copy in copies:
        copy.start()
    for k, out in enumerate((o0, o1, o2, o3)):
        at = lax.rem(x - k + N, N) * 2
        copies[k].wait()
        total = lax.dot_general(w[at], h1[0], NT, preferred_element_type=F32)
        total += lax.dot_general(w[at + 1], h1[1], NT, preferred_element_type=F32)
        out[:HEAD, :] = (total[:HEAD, :] * SCALE).astype(BF)
        out[HEAD:, :] = total[HEAD:, :].astype(BF)
    for copy in copies[N:]:
        copy.wait()


def attend_kernel(
    pos, work, r0, r1, r2, r3, id_row, id_col, o0, o1, o2, o3, qs, ks, vs, scores, outs
):
    x = pos[0]
    chunk = ks.shape[1]
    block = qs.shape[2]
    per = block // chunk
    for k, piece in enumerate((r0, r1, r2, r3)):
        at = lax.rem(x + k, N)
        qs[at] = piece[:HEAD, :]
        keys = jnp.transpose(piece[HEAD : 2 * HEAD, :])
        for j in range(per):
            ks[at * per + j] = keys[j * chunk : (j + 1) * chunk, :]
            vs[at * per + j] = piece[2 * HEAD :, j * chunk : (j + 1) * chunk]
    count = work[4, 0]

    def score(i):
        return jnp.dot(ks[work[1, i]], qs[work[0, i]], preferred_element_type=F32)

    scores[0] = score(0)

    def step(i, carry):
        top, total, acc = carry
        slot = lax.rem(i, 2)
        qb = work[0, i]
        kc = work[1, i]
        raw = scores[slot]
        scores[1 - slot] = score(jnp.minimum(i + 1, count - 1))
        key_ids = id_col[pl.ds(pl.multiple_of(kc * chunk, chunk), chunk), :]
        val = jnp.where(key_ids == id_row[qb], raw, -1e30)
        top = jnp.where(work[2, i] == 1, -1e30, top)
        new_top = jnp.maximum(top, jnp.max(val, axis=0, keepdims=True))
        alpha = jnp.exp2(top - new_top)
        alpha = jnp.where(work[2, i] == 1, 0.0, alpha)
        expo = jnp.exp2(val - new_top)
        total = total * alpha + jnp.sum(expo, axis=0, keepdims=True)
        acc = acc * alpha + jnp.dot(vs[kc], expo.astype(BF), preferred_element_type=F32)

        @pl.when(work[3, i] == 1)
        def _():
            outs[lax.rem(qb - x + N, N)] = (acc / total).astype(BF)

        return new_top, total, acc

    start = (
        jnp.full((1, block), -1e30, F32),
        jnp.zeros((1, block), F32),
        jnp.zeros((HEAD, block), F32),
    )
    lax.fori_loop(0, count, step, start)
    for k, out in enumerate((o0, o1, o2, o3)):
        out[...] = outs[k]


def pack_kernel(pos, g0, g1, g2, g3, out):
    x = pos[0]
    for k, piece in enumerate((g0, g1, g2, g3)):
        out[lax.rem(x - k + N, N)] = piece[...]


def copy_all(moves, sems):
    copies = [pltpu.make_async_copy(a, b, sems.at[i]) for i, (a, b) in enumerate(moves)]
    for copy in copies:
        copy.start()
    for copy in copies:
        copy.wait()


def fetch_kernel(pos, *refs):
    pieces = refs[0:4]
    near, w_hbm = refs[4:6]
    mine = refs[6:9]
    other = refs[9:12]
    w_all, up, down, held, sems = refs[12:]
    y = pos[1]
    c = pos[3]
    half = w_all.shape[3]
    skip = near.shape[1] - HEAD
    moves = []
    for j in range(N):
        moves.append((near.at[2 * j, skip : skip + HEAD, :], w_all.at[0, j]))
        moves.append((near.at[2 * j + 1, skip : skip + HEAD, :], w_all.at[1, j]))
    for k in range(1, N):
        to = slice(k * N, (k + 1) * N)
        moves.append((mine[k - 1], w_all.at[c, to]))
        moves.append((other[k - 1], w_all.at[1 - c, to]))
    for k in range(N):
        moves.append((pieces[k], held.at[lax.rem(y - k + N, N)]))
    units = up.shape[1]
    for h in (0, 1):
        cols = slice(h * half, (h + 1) * half)
        moves.append((w_hbm.at[:, h, :units, :], up.at[:, :, cols]))
        moves.append((w_hbm.at[:, h, units:, :], down.at[:, :, cols]))
    copy_all(moves, sems)


def fetch_merge_kernel(w_hbm, w, sems):
    parts = sems.shape[0]
    rows = w.shape[0] // parts
    cuts = [slice(i * rows, (i + 1) * rows) for i in range(parts)]
    copy_all([(w_hbm.at[cut], w.at[cut]) for cut in cuts], sems)


def mlp_kernel(offsets, pos, *refs):
    gathered = refs[0:4]
    w_all, up, down, held, gain = refs[4:9]
    outs = refs[9:]
    y = pos[1]
    rows = held.shape[1]
    width = held.shape[2]
    half = width // 2
    group = N * HEAD
    blocks = [lax.rem(y + k, N) for k in offsets]
    lhs = []
    start = []
    for block in blocks:
        cols = pl.ds(pl.multiple_of(block * rows, rows), rows)
        parts = [g[:, :, cols].reshape(group, rows) for g in gathered]
        lhs.append(jnp.transpose(jnp.concatenate(parts, axis=0)))
        start.append(held[block].astype(F32))
    lhs = jnp.concatenate(lhs, axis=0)
    start = jnp.concatenate(start, axis=0)
    heads = N * group
    attn = [
        jnp.dot(lhs, w_all[h].reshape(heads, half), preferred_element_type=F32) for h in (0, 1)
    ]
    resid = (start + jnp.concatenate(attn, axis=1)).astype(BF)
    normed = norm_rows(resid.astype(F32), gain[...]).astype(BF)
    count = up.shape[0] * up.shape[1]
    hidden = lax.dot_general(
        normed, up[...].reshape(count, width), NT, preferred_element_type=F32
    )
    hidden = (0.5 * hidden * (1.0 + lax.erf(hidden * math.sqrt(0.5)))).astype(BF)
    result = jnp.dot(hidden, down[...].reshape(count, width), preferred_element_type=F32)
    result = result.astype(BF)
    for i, k in enumerate(offsets):
        outs[i][...] = result[i * rows : (i + 1) * rows, :]
        if k == 0:
            outs[-1][...] = resid[i * rows : (i + 1) * rows, :]


def merge_kernel(early, late, w, select, tail, out, vision):
    sums = (early[...] + late[...].astype(F32)).astype(BF).astype(F32)
    full, width = early.shape
    count = full // 4
    tiles = width // 128
    for i in range(tiles):
        vision[i * full : (i + 1) * full, :] = sums[:, i * 128 : (i + 1) * 128]
    total = jnp.zeros((count, width), F32)
    for j in range(4):
        rows = [vision[pl.ds(i * full + j, count, stride=4), :] for i in range(tiles)]
        rows = jnp.concatenate(rows, axis=1).astype(BF)
        total += jnp.dot(rows, w[j * width : (j + 1) * width, :], preferred_element_type=F32)
    sent = jnp.dot(select[...], total.astype(BF), preferred_element_type=F32)
    out[:, :width] = sent.astype(BF)
    out[:, width:] = tail[...]


def local(
    patches,
    picture_ids,
    ln_attn,
    w_qkv,
    w_out,
    ln_mlp,
    w_up,
    w_down,
    w_merge,
    text_embed,
    slot_dest,
):
    rows = patches[0]
    count, width = rows.shape
    x = lax.axis_index("x")
    y = lax.axis_index("y")
    c = lax.axis_index("c")
    pos = jnp.stack([x, y, lax.axis_index("z"), c]).astype(jnp.int32)
    ids = picture_ids[0]

    half = width // 2
    w_heads = jnp.transpose(w_qkv, (0, 2, 1)).reshape(3 * HEAD, width)
    w_heads = jnp.concatenate([w_heads, w_out], axis=0)
    w_half = lax.dynamic_slice_in_dim(w_heads, c * half, half, 1)
    near = lax.all_gather(w_half, ("x", "c"), axis=0, tiled=False)
    z = lax.axis_index("z")
    units = w_down.shape[0] // N
    sizes = (units, half)
    packed = jnp.concatenate(
        [
            lax.dynamic_slice(w_up.T, (z * units, c * half), sizes),
            lax.dynamic_slice(w_down, (z * units, c * half), sizes),
        ],
        axis=0,
    )
    packed, _ = lax.optimization_barrier((packed, w_half))
    w_near = lax.all_gather(packed, ("x", "z", "c"), axis=0, tiled=False)
    w_near = w_near.reshape(N * N, 2, 2 * units, half)

    pieces = [rows] + [shift(rows, "y", k) for k in (1, 2, 3)]
    total_rows = count * N
    h1 = pl.pallas_call(
        norm_kernel,
        out_shape=jax.ShapeDtypeStruct((2, total_rows, half), BF),
        in_specs=[SMEM] + [HBM] * N + [VMEM],
        out_specs=VMEM,
        scratch_shapes=[
            pltpu.VMEM((N, count, width), BF),
            pltpu.SemaphoreType.DMA((N,)),
        ],
        compiler_params=params(16),
        name="norm",
    )(pos, *[far(piece) for piece in pieces], ln_attn[None, :])
    group_rows = ids.shape[0]
    chunk = 256
    chunks = group_rows // chunk
    held = (ids[:, None] == jnp.arange(16)[None, :]).reshape(chunks, chunk, 16)
    held = jnp.any(held, axis=1)
    per = chunks // N
    wanted = jnp.any(held.reshape(N, per, 16), axis=1)
    need = jnp.any(wanted[:, None, :] & held[None, :, :], axis=2)
    where = jnp.arange(chunks)[None, :]
    low = jnp.min(jnp.where(need, where, chunks - 1), axis=1)
    high = jnp.max(jnp.where(need, where + 1, 1), axis=1)
    low = jnp.minimum(low, high - 1)
    spans = high - low
    index = jnp.arange(N)
    ends = jnp.sum(jnp.where(index[None, :] <= index[:, None], spans[None, :], 0), axis=1)
    item = jnp.arange(N * chunks)
    block = jnp.sum((item[:, None] >= ends[None, :]).astype(jnp.int32), axis=1)
    block = jnp.minimum(block, N - 1)
    mark = block[:, None] == index[None, :]
    begin = jnp.sum(jnp.where(mark, (low + spans - ends)[None, :], 0), axis=1)
    key = jnp.clip(begin + item, 0, chunks - 1)
    is_first = jnp.any(mark & ((ends - spans)[None, :] == item[:, None]), axis=1)
    is_last = jnp.any(mark & ((ends - 1)[None, :] == item[:, None]), axis=1)
    total_items = jnp.full_like(item, 1) * ends[N - 1]
    work = jnp.stack([block, key, is_first, is_last, total_items]).astype(jnp.int32)

    merged_count = count // 4
    dest = slot_dest[0]
    prompt_rows = text_embed.shape[0]
    req_count = N * N
    row_count = lax.axis_size("z") * lax.axis_size("c")
    slot_cap = 2
    owner = jnp.where(dest >= 0, dest // prompt_rows // row_count, -1)
    order = jnp.arange(merged_count)
    same_owner = (owner[:, None] == owner[None, :]) & (order[None, :] < order[:, None])
    ranks = jnp.sum(same_owner.astype(jnp.int32), axis=1)
    target = jnp.where(owner >= 0, owner * slot_cap + ranks, -1)
    select = target[None, :] == jnp.arange(req_count * slot_cap)[:, None]
    places = jnp.sum(jnp.where(select, (dest % prompt_rows + 1)[None, :], 0), axis=1)
    lane = jnp.arange(128)[None, :] == 0
    tail = jnp.where(lane, places[:, None], 0).astype(BF)
    id_row = ids.reshape(N, 1, total_rows)
    id_col = ids[:, None]
    select = select.astype(BF)
    near, h1, work, id_col, select, tail = lax.optimization_barrier(
        (near, h1, work, id_col, select, tail)
    )
    *qkv, mine = pl.pallas_call(
        qkv_kernel,
        out_shape=[jax.ShapeDtypeStruct((3 * HEAD, total_rows), BF)] * N
        + [jax.ShapeDtypeStruct((N, HEAD, half), BF)],
        in_specs=[SMEM, VMEM, HBM],
        out_specs=[VMEM] * (N + 1),
        scratch_shapes=[
            pltpu.VMEM((2 * N, 3 * HEAD, half), BF),
            pltpu.SemaphoreType.DMA((2 * N,)),
        ],
        compiler_params=params(16),
        name="qkv",
    )(pos, h1, far(near))
    blocks = [qkv[0]] + [shift(qkv[k], "x", -k) for k in (1, 2, 3)]
    pass1 = shift(mine, "y", 1)
    pass3 = shift(mine, "y", 3)
    blocks, mine, pass1, pass3 = lax.optimization_barrier((blocks, mine, pass1, pass3))
    pass2 = shift(mine, "y", 2)
    swap1 = swap(pass1)
    swap3 = swap(pass3)

    attended = pl.pallas_call(
        attend_kernel,
        out_shape=[jax.ShapeDtypeStruct((HEAD, total_rows), BF)] * N,
        in_specs=[SMEM, SMEM] + [VMEM] * 6,
        out_specs=[VMEM] * N,
        scratch_shapes=[
            pltpu.VMEM((N, HEAD, total_rows), BF),
            pltpu.VMEM((chunks, chunk, HEAD), BF),
            pltpu.VMEM((chunks, HEAD, chunk), BF),
            pltpu.VMEM((2, chunk, total_rows), F32),
            pltpu.VMEM((N, HEAD, total_rows), BF),
        ],
        compiler_params=params(16),
        name="attend",
    )(pos, work, *blocks, id_row, id_col)
    attended, pass2, swap1, swap3 = lax.optimization_barrier((attended, pass2, swap1, swap3))
    swap2 = swap(pass2)
    heads = [attended[0]] + [shift(attended[k], "x", k) for k in (1, 2, 3)]
    heads = pl.pallas_call(
        pack_kernel,
        out_shape=jax.ShapeDtypeStruct((N, HEAD, total_rows), BF),
        in_specs=[SMEM] + [VMEM] * N,
        out_specs=VMEM,
        compiler_params=params(8),
        name="pack",
    )(pos, *heads)
    gathered = [heads] + [shift(heads, "y", k) for k in (1, 2, 3)]
    _, near, w_near, w_merge = lax.optimization_barrier((heads, near, w_near, w_merge))

    fetched = pl.pallas_call(
        fetch_kernel,
        out_shape=[
            jax.ShapeDtypeStruct((2, N * N, HEAD, half), BF),
            jax.ShapeDtypeStruct((N * N, units, width), BF),
            jax.ShapeDtypeStruct((N * N, units, width), BF),
            jax.ShapeDtypeStruct((N, count, width), BF),
        ],
        in_specs=[SMEM] + [HBM] * 12,
        out_specs=[VMEM] * 4,
        scratch_shapes=[pltpu.SemaphoreType.DMA((22,))],
        compiler_params=params(4),
        name="fetch",
    )(
        pos,
        *[far(v) for v in pieces],
        *[far(v) for v in (near, w_near, pass1, pass2, pass3, swap1, swap2, swap3)],
    )

    w_merge = pl.pallas_call(
        fetch_merge_kernel,
        out_shape=jax.ShapeDtypeStruct(w_merge.shape, BF),
        in_specs=[HBM],
        out_specs=VMEM,
        scratch_shapes=[pltpu.SemaphoreType.DMA((8,))],
        compiler_params=params(4),
        name="fetch_merge",
    )(far(w_merge))

    def mlp(offsets, name):
        outputs = len(offsets) + (0 in offsets)
        return pl.pallas_call(
            functools.partial(mlp_kernel, offsets),
            out_shape=[jax.ShapeDtypeStruct((count, width), BF)] * outputs,
            in_specs=[SMEM] + [VMEM] * 9,
            out_specs=[VMEM] * outputs,
            compiler_params=params(24),
            cost_estimate=pl.CostEstimate(
                flops=6 * len(offsets) * count * width * width,
                transcendentals=len(offsets) * count * width,
                bytes_accessed=6 * width * width,
            ),
            name=name,
        )(pos, *gathered, *fetched, ln_mlp[None, :])

    part2, part1 = mlp((2, 1), "mlp_first")
    gathered[0], w_merge, part2, part1 = lax.optimization_barrier(
        (gathered[0], w_merge, part2, part1)
    )
    part3, part0, resid = mlp((3, 0), "mlp_second")
    early = shift(part1, "y", 1).astype(F32) + shift(part2, "y", 2).astype(F32)
    sums = [resid.astype(F32) + part0.astype(F32) + early, shift(part3, "y", 3)]
    outgoing = pl.pallas_call(
        merge_kernel,
        out_shape=jax.ShapeDtypeStruct((req_count * slot_cap, width + 128), BF),
        in_specs=[VMEM] * 5,
        out_specs=VMEM,
        scratch_shapes=[pltpu.VMEM((count * width // 128, 128), F32)],
        compiler_params=params(8),
        name="merge",
    )(*sums, w_merge, select, tail)
    arrived = lax.all_to_all(
        outgoing.reshape(req_count, slot_cap, width + 128),
        ("x", "y"),
        split_axis=0,
        concat_axis=0,
        tiled=True,
    ).reshape(req_count * slot_cap, width + 128)
    landing = arrived[:, width].astype(jnp.int32) - 1
    placer = landing[None, :] == jnp.arange(prompt_rows)[:, None]
    placed = jnp.dot(
        placer.astype(BF), arrived[:, :width], preferred_element_type=F32
    ).astype(BF)
    filled = jnp.any(placer, axis=1)
    return jnp.where(filled[:, None], placed, text_embed)


def solution(mesh):
    grid = Mesh(mesh.devices.reshape(N, N, -1, 2), ("x", "y", "z", "c"))
    req = ("x", "y")
    row = ("z", "c")
    return jax.shard_map(
        local,
        mesh=grid,
        in_specs=(
            P(row, req, None),
            P(row, None),
            P(),
            P(None, None, req),
            P(req, None),
            P(),
            P(None, req),
            P(req, None),
            P(),
            P(("x", "y", "z", "c"), None),
            P(row, req),
        ),
        out_specs=P(("x", "y", "z", "c"), None),
        check_vma=False,
    )
```

```python
import functools
import math

import jax
import jax.numpy as jnp
from jax import lax
from jax.experimental import pallas as pl
from jax.experimental.pallas import tpu as pltpu
from jax.sharding import Mesh
from jax.sharding import PartitionSpec as P

HEAD = 80
SCALE = math.log2(math.e) / math.sqrt(HEAD)
N = 4
SLOT = 8
BF = jnp.bfloat16
F32 = jnp.float32
NT = (((1,), (1,)), ((), ()))
TN = (((0,), (0,)), ((), ()))
HBM = pl.BlockSpec(memory_space=pltpu.HBM)
VMEM = pl.BlockSpec(memory_space=pltpu.VMEM)
SMEM = pl.BlockSpec(memory_space=pltpu.SMEM)


def params(mib):
    return pltpu.CompilerParams(vmem_limit_bytes=mib << 20)


def norm_rows(rows32, gain):
    center = rows32 - jnp.mean(rows32, axis=-1, keepdims=True)
    spread = jnp.mean(center * center, axis=-1, keepdims=True)
    return center * lax.rsqrt(spread + 1e-06) * gain


def shift(value, axis, step):
    pairs = [(i, (i + step) % N) for i in range(N)]
    return lax.ppermute(value, axis, pairs)


def far(value):
    return pltpu.with_memory_space_constraint(value, pltpu.HBM)


def swap(value):
    return lax.ppermute(value, "c", [(0, 1), (1, 0)])


def norm_kernel(pos, p0, p1, p2, p3, gain, h1, held, sems):
    y = pos[1]
    half = h1.shape[2]
    rows = p0.shape[0]
    copies = []
    for k, piece in enumerate((p0, p1, p2, p3)):
        copies.append(pltpu.make_async_copy(piece, held.at[k], sems.at[k]))
    for copy in copies:
        copy.start()
    for k in range(N):
        copies[k].wait()
        normed = norm_rows(held[k].astype(F32), gain[...]).astype(BF)
        at = pl.ds(pl.multiple_of(lax.rem(y - k + N, N) * rows, rows), rows)
        h1[0, at, :] = normed[:, :half]
        h1[1, at, :] = normed[:, half:]


def qkv_kernel(pos, h1, w_hbm, o0, o1, o2, o3, share, w, sems):
    x = pos[0]
    c = pos[3]
    cols = w.shape[1]
    copies = []
    for k in range(N):
        at = pl.ds(lax.rem(x - k + N, N) * 2, 2)
        copies.append(pltpu.make_async_copy(w_hbm.at[at, :cols, :], w.at[at], sems.at[k]))
    for j in range(N):
        src = w_hbm.at[2 * j + c, cols : cols + HEAD, :]
        copies.append(pltpu.make_async_copy(src, share.at[j], sems.at[N + j]))
    for copy in copies:
        copy.start()
    for k, out in enumerate((o0, o1, o2, o3)):
        at = lax.rem(x - k + N, N) * 2
        copies[k].wait()
        total = lax.dot_general(w[at], h1[0], NT, preferred_element_type=F32)
        total += lax.dot_general(w[at + 1], h1[1], NT, preferred_element_type=F32)
        out[:HEAD, :] = (total[:HEAD, :] * SCALE).astype(BF)
        out[HEAD:, :] = total[HEAD:, :].astype(BF)
    for copy in copies[N:]:
        copy.wait()


def attend_kernel(
    pos, work, r0, r1, r2, r3, id_row, id_col, o0, o1, o2, o3, qs, ks, vs, scores, outs
):
    x = pos[0]
    chunk = ks.shape[1]
    block = qs.shape[2]
    per = block // chunk
    for k, piece in enumerate((r0, r1, r2, r3)):
        at = lax.rem(x + k, N)
        qs[at] = piece[:HEAD, :]
        keys = jnp.transpose(piece[HEAD : 2 * HEAD, :])
        for j in range(per):
            ks[at * per + j] = keys[j * chunk : (j + 1) * chunk, :]
            vs[at * per + j] = piece[2 * HEAD :, j * chunk : (j + 1) * chunk]
    count = work[4, 0]

    def score(i):
        return jnp.dot(ks[work[1, i]], qs[work[0, i]], preferred_element_type=F32)

    scores[0] = score(0)

    def step(i, carry):
        top, total, acc = carry
        slot = lax.rem(i, 2)
        qb = work[0, i]
        kc = work[1, i]
        raw = scores[slot]
        scores[1 - slot] = score(jnp.minimum(i + 1, count - 1))
        key_ids = id_col[pl.ds(pl.multiple_of(kc * chunk, chunk), chunk), :]
        val = jnp.where(key_ids == id_row[qb], raw, -1e30)
        top = jnp.where(work[2, i] == 1, -1e30, top)
        new_top = jnp.maximum(top, jnp.max(val, axis=0, keepdims=True))
        alpha = jnp.exp2(top - new_top)
        alpha = jnp.where(work[2, i] == 1, 0.0, alpha)
        expo = jnp.exp2(val - new_top)
        total = total * alpha + jnp.sum(expo, axis=0, keepdims=True)
        acc = acc * alpha + jnp.dot(vs[kc], expo.astype(BF), preferred_element_type=F32)

        @pl.when(work[3, i] == 1)
        def _():
            outs[lax.rem(qb - x + N, N)] = (acc / total).astype(BF)

        return new_top, total, acc

    start = (
        jnp.full((1, block), -1e30, F32),
        jnp.zeros((1, block), F32),
        jnp.zeros((HEAD, block), F32),
    )
    lax.fori_loop(0, count, step, start)
    for k, out in enumerate((o0, o1, o2, o3)):
        out[...] = outs[k]


def pack_kernel(pos, g0, g1, g2, g3, out):
    x = pos[0]
    for k, piece in enumerate((g0, g1, g2, g3)):
        out[lax.rem(x - k + N, N)] = piece[...]


def copy_all(moves, sems):
    copies = [pltpu.make_async_copy(a, b, sems.at[i]) for i, (a, b) in enumerate(moves)]
    for copy in copies:
        copy.start()
    for copy in copies:
        copy.wait()


def fetch_kernel(pos, *refs):
    pieces = refs[0:4]
    near, w_hbm = refs[4:6]
    mine = refs[6:9]
    other = refs[9:12]
    w_all, up, down, held, sems = refs[12:]
    y = pos[1]
    c = pos[3]
    half = w_all.shape[3]
    skip = near.shape[1] - HEAD
    moves = []
    for j in range(N):
        moves.append((near.at[2 * j, skip : skip + HEAD, :], w_all.at[0, j]))
        moves.append((near.at[2 * j + 1, skip : skip + HEAD, :], w_all.at[1, j]))
    for k in range(1, N):
        to = slice(k * N, (k + 1) * N)
        moves.append((mine[k - 1], w_all.at[c, to]))
        moves.append((other[k - 1], w_all.at[1 - c, to]))
    for k in range(N):
        moves.append((pieces[k], held.at[lax.rem(y - k + N, N)]))
    units = up.shape[1]
    for h in (0, 1):
        cols = slice(h * half, (h + 1) * half)
        moves.append((w_hbm.at[:, h, :units, :], up.at[:, :, cols]))
        moves.append((w_hbm.at[:, h, units:, :], down.at[:, :, cols]))
    copy_all(moves, sems)


def fetch_merge_kernel(w_hbm, w, sems):
    parts = sems.shape[0]
    rows = w.shape[0] // parts
    cuts = [slice(i * rows, (i + 1) * rows) for i in range(parts)]
    copy_all([(w_hbm.at[cut], w.at[cut]) for cut in cuts], sems)


def mlp_kernel(offsets, pos, *refs):
    gathered = refs[0:4]
    w_all, up, down, held, gain = refs[4:9]
    outs = refs[9:]
    y = pos[1]
    rows = held.shape[1]
    width = held.shape[2]
    half = width // 2
    group = N * HEAD
    blocks = [lax.rem(y + k, N) for k in offsets]
    lhs = []
    start = []
    for block in blocks:
        cols = pl.ds(pl.multiple_of(block * rows, rows), rows)
        parts = [g[:, :, cols].reshape(group, rows) for g in gathered]
        lhs.append(jnp.transpose(jnp.concatenate(parts, axis=0)))
        start.append(held[block].astype(F32))
    lhs = jnp.concatenate(lhs, axis=0)
    start = jnp.concatenate(start, axis=0)
    heads = N * group
    attn = [
        jnp.dot(lhs, w_all[h].reshape(heads, half), preferred_element_type=F32) for h in (0, 1)
    ]
    resid = (start + jnp.concatenate(attn, axis=1)).astype(BF)
    normed = norm_rows(resid.astype(F32), gain[...]).astype(BF)
    count = up.shape[0] * up.shape[1]
    hidden = lax.dot_general(
        normed, up[...].reshape(count, width), NT, preferred_element_type=F32
    )
    hidden = (0.5 * hidden * (1.0 + lax.erf(hidden * math.sqrt(0.5)))).astype(BF)
    result = jnp.dot(hidden, down[...].reshape(count, width), preferred_element_type=F32)
    result = result.astype(BF)
    for i, k in enumerate(offsets):
        outs[i][...] = result[i * rows : (i + 1) * rows, :]
        if k == 0:
            outs[-1][...] = resid[i * rows : (i + 1) * rows, :]


def merge_kernel(early, late, w, select, tail, o0, o1, o2, o3, vision):
    sums = (early[...] + late[...].astype(F32)).astype(BF).astype(F32)
    full, width = early.shape
    count = full // 4
    tiles = width // 128
    for i in range(tiles):
        vision[i * full : (i + 1) * full, :] = sums[:, i * 128 : (i + 1) * 128]
    total = jnp.zeros((count, width), F32)
    for j in range(4):
        rows = [vision[pl.ds(i * full + j, count, stride=4), :] for i in range(tiles)]
        rows = jnp.concatenate(rows, axis=1).astype(BF)
        total += jnp.dot(rows, w[j * width : (j + 1) * width, :], preferred_element_type=F32)
    sent = jnp.dot(select[...], total.astype(BF), preferred_element_type=F32).astype(BF)
    for k, out in enumerate((o0, o1, o2, o3)):
        for j in range(N):
            at = slice((k * N + j) * SLOT, (k * N + j + 1) * SLOT)
            out[j, :, :width] = sent[at, :]
            out[j, :, width:] = tail[at, :]


def turn_kernel(a0, a1, a2, a3, o0, o1, o2, o3):
    for k, piece in enumerate((a0, a1, a2, a3)):
        for j, out in enumerate((o0, o1, o2, o3)):
            out[k] = piece[j]


def place_kernel(b0, b1, b2, b3, text, out):
    rows, width = text.shape
    arrived = [b[...].reshape(N * SLOT, b.shape[2]) for b in (b0, b1, b2, b3)]
    arrived = jnp.concatenate(arrived, axis=0)
    landing = arrived[:, width : width + 1].astype(F32)
    spot = lax.broadcasted_iota(jnp.int32, (arrived.shape[0], rows), 1) + 1
    mark = jnp.where(landing == spot.astype(F32), 1.0, 0.0).astype(BF)
    placed = lax.dot_general(mark, arrived[:, :width], TN, preferred_element_type=F32)
    ones = jnp.ones((arrived.shape[0], 128), BF)
    filled = lax.dot_general(mark, ones, TN, preferred_element_type=F32)
    out[...] = jnp.where(filled[:, :1] > 0.5, placed.astype(BF), text[...])


def local(
    patches,
    picture_ids,
    ln_attn,
    w_qkv,
    w_out,
    ln_mlp,
    w_up,
    w_down,
    w_merge,
    text_embed,
    slot_dest,
):
    rows = patches[0]
    count, width = rows.shape
    x = lax.axis_index("x")
    y = lax.axis_index("y")
    c = lax.axis_index("c")
    pos = jnp.stack([x, y, lax.axis_index("z"), c]).astype(jnp.int32)
    ids = picture_ids[0]

    half = width // 2
    w_heads = jnp.transpose(w_qkv, (0, 2, 1)).reshape(3 * HEAD, width)
    w_heads = jnp.concatenate([w_heads, w_out], axis=0)
    w_half = lax.dynamic_slice_in_dim(w_heads, c * half, half, 1)
    near = lax.all_gather(w_half, ("x", "c"), axis=0, tiled=False)
    z = lax.axis_index("z")
    units = w_down.shape[0] // N
    sizes = (units, half)
    packed = jnp.concatenate(
        [
            lax.dynamic_slice(w_up.T, (z * units, c * half), sizes),
            lax.dynamic_slice(w_down, (z * units, c * half), sizes),
        ],
        axis=0,
    )
    packed, _ = lax.optimization_barrier((packed, w_half))
    w_near = lax.all_gather(packed, ("x", "z", "c"), axis=0, tiled=False)
    w_near = w_near.reshape(N * N, 2, 2 * units, half)

    pieces = [rows] + [shift(rows, "y", k) for k in (1, 2, 3)]
    total_rows = count * N
    h1 = pl.pallas_call(
        norm_kernel,
        out_shape=jax.ShapeDtypeStruct((2, total_rows, half), BF),
        in_specs=[SMEM] + [HBM] * N + [VMEM],
        out_specs=VMEM,
        scratch_shapes=[
            pltpu.VMEM((N, count, width), BF),
            pltpu.SemaphoreType.DMA((N,)),
        ],
        compiler_params=params(16),
        name="norm",
    )(pos, *[far(piece) for piece in pieces], ln_attn[None, :])
    group_rows = ids.shape[0]
    chunk = 512
    chunks = group_rows // chunk
    held = (ids[:, None] == jnp.arange(16)[None, :]).reshape(chunks, chunk, 16)
    held = jnp.any(held, axis=1)
    per = chunks // N
    wanted = jnp.any(held.reshape(N, per, 16), axis=1)
    need = jnp.any(wanted[:, None, :] & held[None, :, :], axis=2)
    where = jnp.arange(chunks)[None, :]
    low = jnp.min(jnp.where(need, where, chunks - 1), axis=1)
    high = jnp.max(jnp.where(need, where + 1, 1), axis=1)
    low = jnp.minimum(low, high - 1)
    spans = high - low
    index = jnp.arange(N)
    ends = jnp.sum(jnp.where(index[None, :] <= index[:, None], spans[None, :], 0), axis=1)
    item = jnp.arange(N * chunks)
    block = jnp.sum((item[:, None] >= ends[None, :]).astype(jnp.int32), axis=1)
    block = jnp.minimum(block, N - 1)
    mark = block[:, None] == index[None, :]
    begin = jnp.sum(jnp.where(mark, (low + spans - ends)[None, :], 0), axis=1)
    key = jnp.clip(begin + item, 0, chunks - 1)
    is_first = jnp.any(mark & ((ends - spans)[None, :] == item[:, None]), axis=1)
    is_last = jnp.any(mark & ((ends - 1)[None, :] == item[:, None]), axis=1)
    total_items = jnp.full_like(item, 1) * ends[N - 1]
    work = jnp.stack([block, key, is_first, is_last, total_items]).astype(jnp.int32)

    merged_count = count // 4
    dest = slot_dest[0]
    prompt_rows = text_embed.shape[0]
    row_count = lax.axis_size("z") * lax.axis_size("c")
    owner = jnp.where(dest >= 0, dest // prompt_rows // row_count, -1)
    order = jnp.arange(merged_count)
    same_owner = (owner[:, None] == owner[None, :]) & (order[None, :] < order[:, None])
    ranks = jnp.sum(same_owner.astype(jnp.int32), axis=1)
    away = lax.rem(owner // N - x + N, N) * N + lax.rem(owner % N - y + N, N)
    target = jnp.where(owner >= 0, away * SLOT + ranks, -1)
    select = target[None, :] == jnp.arange(N * N * SLOT)[:, None]
    places = jnp.sum(jnp.where(select, (dest % prompt_rows + 1)[None, :], 0), axis=1)
    lane = jnp.arange(128)[None, :] == 0
    tail = jnp.where(lane, places[:, None], 0).astype(BF)
    id_row = ids.reshape(N, 1, total_rows)
    id_col = ids[:, None]
    select = select.astype(BF)
    near, h1, work, id_col, select, tail = lax.optimization_barrier(
        (near, h1, work, id_col, select, tail)
    )
    *qkv, mine = pl.pallas_call(
        qkv_kernel,
        out_shape=[jax.ShapeDtypeStruct((3 * HEAD, total_rows), BF)] * N
        + [jax.ShapeDtypeStruct((N, HEAD, half), BF)],
        in_specs=[SMEM, VMEM, HBM],
        out_specs=[VMEM] * (N + 1),
        scratch_shapes=[
            pltpu.VMEM((2 * N, 3 * HEAD, half), BF),
            pltpu.SemaphoreType.DMA((2 * N,)),
        ],
        compiler_params=params(16),
        name="qkv",
    )(pos, h1, far(near))
    blocks = [qkv[0]] + [shift(qkv[k], "x", -k) for k in (1, 2, 3)]
    pass1 = shift(mine, "y", 1)
    pass3 = shift(mine, "y", 3)
    blocks, mine, pass1, pass3 = lax.optimization_barrier((blocks, mine, pass1, pass3))
    pass2 = shift(mine, "y", 2)
    swap1 = swap(pass1)
    swap3 = swap(pass3)

    attended = pl.pallas_call(
        attend_kernel,
        out_shape=[jax.ShapeDtypeStruct((HEAD, total_rows), BF)] * N,
        in_specs=[SMEM, SMEM] + [VMEM] * 6,
        out_specs=[VMEM] * N,
        scratch_shapes=[
            pltpu.VMEM((N, HEAD, total_rows), BF),
            pltpu.VMEM((chunks, chunk, HEAD), BF),
            pltpu.VMEM((chunks, HEAD, chunk), BF),
            pltpu.VMEM((2, chunk, total_rows), F32),
            pltpu.VMEM((N, HEAD, total_rows), BF),
        ],
        compiler_params=params(16),
        name="attend",
    )(pos, work, *blocks, id_row, id_col)
    attended, pass2, swap1, swap3 = lax.optimization_barrier((attended, pass2, swap1, swap3))
    swap2 = swap(pass2)
    heads = [attended[0]] + [shift(attended[k], "x", k) for k in (1, 2, 3)]
    heads = pl.pallas_call(
        pack_kernel,
        out_shape=jax.ShapeDtypeStruct((N, HEAD, total_rows), BF),
        in_specs=[SMEM] + [VMEM] * N,
        out_specs=VMEM,
        compiler_params=params(8),
        name="pack",
    )(pos, *heads)
    gathered = [heads] + [shift(heads, "y", k) for k in (1, 2, 3)]
    _, near, w_near, w_merge = lax.optimization_barrier((heads, near, w_near, w_merge))

    fetched = pl.pallas_call(
        fetch_kernel,
        out_shape=[
            jax.ShapeDtypeStruct((2, N * N, HEAD, half), BF),
            jax.ShapeDtypeStruct((N * N, units, width), BF),
            jax.ShapeDtypeStruct((N * N, units, width), BF),
            jax.ShapeDtypeStruct((N, count, width), BF),
        ],
        in_specs=[SMEM] + [HBM] * 12,
        out_specs=[VMEM] * 4,
        scratch_shapes=[pltpu.SemaphoreType.DMA((22,))],
        compiler_params=params(4),
        name="fetch",
    )(
        pos,
        *[far(v) for v in pieces],
        *[far(v) for v in (near, w_near, pass1, pass2, pass3, swap1, swap2, swap3)],
    )

    w_merge = pl.pallas_call(
        fetch_merge_kernel,
        out_shape=jax.ShapeDtypeStruct(w_merge.shape, BF),
        in_specs=[HBM],
        out_specs=VMEM,
        scratch_shapes=[pltpu.SemaphoreType.DMA((8,))],
        compiler_params=params(4),
        name="fetch_merge",
    )(far(w_merge))

    def mlp(offsets, name):
        outputs = len(offsets) + (0 in offsets)
        return pl.pallas_call(
            functools.partial(mlp_kernel, offsets),
            out_shape=[jax.ShapeDtypeStruct((count, width), BF)] * outputs,
            in_specs=[SMEM] + [VMEM] * 9,
            out_specs=[VMEM] * outputs,
            compiler_params=params(24),
            cost_estimate=pl.CostEstimate(
                flops=6 * len(offsets) * count * width * width,
                transcendentals=len(offsets) * count * width,
                bytes_accessed=6 * width * width,
            ),
            name=name,
        )(pos, *gathered, *fetched, ln_mlp[None, :])

    part2, part1 = mlp((2, 1), "mlp_first")
    gathered[0], w_merge, part2, part1 = lax.optimization_barrier(
        (gathered[0], w_merge, part2, part1)
    )
    part3, part0, resid = mlp((3, 0), "mlp_second")
    early = shift(part1, "y", 1).astype(F32) + shift(part2, "y", 2).astype(F32)
    sums = [resid.astype(F32) + part0.astype(F32) + early, shift(part3, "y", 3)]
    block = jax.ShapeDtypeStruct((N, SLOT, width + 128), BF)
    sent = pl.pallas_call(
        merge_kernel,
        out_shape=[block] * N,
        in_specs=[VMEM] * 5,
        out_specs=[VMEM] * N,
        scratch_shapes=[pltpu.VMEM((count * width // 128, 128), F32)],
        compiler_params=params(8),
        name="merge",
    )(*sums, w_merge, select, tail)
    sent = [sent[0]] + [shift(sent[k], "x", k) for k in (1, 2, 3)]
    sent = pl.pallas_call(
        turn_kernel,
        out_shape=[block] * N,
        in_specs=[VMEM] * N,
        out_specs=[VMEM] * N,
        compiler_params=params(4),
        name="turn",
    )(*sent)
    sent = [sent[0]] + [shift(sent[k], "y", k) for k in (1, 2, 3)]
    return pl.pallas_call(
        place_kernel,
        out_shape=jax.ShapeDtypeStruct(text_embed.shape, BF),
        in_specs=[VMEM] * (N + 1),
        out_specs=VMEM,
        compiler_params=params(8),
        name="place",
    )(*sent, text_embed)


def solution(mesh):
    grid = Mesh(mesh.devices.reshape(N, N, -1, 2), ("x", "y", "z", "c"))
    req = ("x", "y")
    row = ("z", "c")
    return jax.shard_map(
        local,
        mesh=grid,
        in_specs=(
            P(row, req, None),
            P(row, None),
            P(),
            P(None, None, req),
            P(req, None),
            P(),
            P(None, req),
            P(req, None),
            P(),
            P(("x", "y", "z", "c"), None),
            P(row, req),
        ),
        out_specs=P(("x", "y", "z", "c"), None),
        check_vma=False,
    )
```

```python
import functools
import math

import jax
import jax.numpy as jnp
from jax import lax
from jax.experimental import pallas as pl
from jax.experimental.pallas import tpu as pltpu
from jax.sharding import Mesh
from jax.sharding import PartitionSpec as P

HEAD = 80
SCALE = math.log2(math.e) / math.sqrt(HEAD)
N = 4
BF = jnp.bfloat16
F32 = jnp.float32
NT = (((1,), (1,)), ((), ()))
TN = (((0,), (0,)), ((), ()))
HBM = pl.BlockSpec(memory_space=pltpu.HBM)
VMEM = pl.BlockSpec(memory_space=pltpu.VMEM)
SMEM = pl.BlockSpec(memory_space=pltpu.SMEM)


def params(mib):
    return pltpu.CompilerParams(vmem_limit_bytes=mib << 20)


def norm_rows(rows32, gain):
    center = rows32 - jnp.mean(rows32, axis=-1, keepdims=True)
    spread = jnp.mean(center * center, axis=-1, keepdims=True)
    return center * lax.rsqrt(spread + 1e-06) * gain


def shift(value, axis, step):
    pairs = [(i, (i + step) % N) for i in range(N)]
    return lax.ppermute(value, axis, pairs)


def far(value):
    return pltpu.with_memory_space_constraint(value, pltpu.HBM)


def norm_kernel(pos, p0, p1, p2, p3, gain, h1, held, sems):
    y = pos[1]
    half = h1.shape[2]
    rows = p0.shape[0]
    copies = []
    for k, piece in enumerate((p0, p1, p2, p3)):
        copies.append(pltpu.make_async_copy(piece, held.at[k], sems.at[k]))
    for copy in copies:
        copy.start()
    for k in range(N):
        copies[k].wait()
        normed = norm_rows(held[k].astype(F32), gain[...]).astype(BF)
        at = pl.ds(pl.multiple_of(lax.rem(y - k + N, N) * rows, rows), rows)
        h1[0, at, :] = normed[:, :half]
        h1[1, at, :] = normed[:, half:]


def qkv_kernel(pos, h1, w_hbm, o0, o1, o2, o3, share, w, sems):
    x = pos[0]
    cols = w.shape[1]
    half = w.shape[2]
    copies = []
    for k in range(N):
        at = pl.ds(lax.rem(x - k + N, N) * 2, 2)
        copies.append(pltpu.make_async_copy(w_hbm.at[at, :cols, :], w.at[at], sems.at[k]))
    for j in range(2 * N):
        src = w_hbm.at[j, cols : cols + HEAD, :]
        dst = share.at[j // 2, :, j % 2 * half : (j % 2 + 1) * half]
        copies.append(pltpu.make_async_copy(src, dst, sems.at[N + j]))
    for copy in copies:
        copy.start()
    for k, out in enumerate((o0, o1, o2, o3)):
        at = lax.rem(x - k + N, N) * 2
        copies[k].wait()
        total = lax.dot_general(w[at], h1[0], NT, preferred_element_type=F32)
        total += lax.dot_general(w[at + 1], h1[1], NT, preferred_element_type=F32)
        out[:HEAD, :] = (total[:HEAD, :] * SCALE).astype(BF)
        out[HEAD:, :] = total[HEAD:, :].astype(BF)
    for copy in copies[N:]:
        copy.wait()


def attend_kernel(
    pos, work, r0, r1, r2, r3, id_row, id_col, o0, o1, o2, o3, qs, ks, vs, scores, outs
):
    x = pos[0]
    chunk = ks.shape[1]
    block = qs.shape[2]
    per = block // chunk
    for k, piece in enumerate((r0, r1, r2, r3)):
        at = lax.rem(x + k, N)
        qs[at] = piece[:HEAD, :]
        keys = jnp.transpose(piece[HEAD : 2 * HEAD, :])
        for j in range(per):
            ks[at * per + j] = keys[j * chunk : (j + 1) * chunk, :]
            vs[at * per + j] = piece[2 * HEAD :, j * chunk : (j + 1) * chunk]
    count = work[4, 0]

    def score(i):
        return jnp.dot(ks[work[1, i]], qs[work[0, i]], preferred_element_type=F32)

    scores[0] = score(0)

    def step(i, carry):
        top, total, acc = carry
        slot = lax.rem(i, 2)
        qb = work[0, i]
        kc = work[1, i]
        raw = scores[slot]
        scores[1 - slot] = score(jnp.minimum(i + 1, count - 1))
        key_ids = id_col[pl.ds(pl.multiple_of(kc * chunk, chunk), chunk), :]
        val = jnp.where(key_ids == id_row[qb], raw, -1e30)
        top = jnp.where(work[2, i] == 1, -1e30, top)
        new_top = jnp.maximum(top, jnp.max(val, axis=0, keepdims=True))
        alpha = jnp.exp2(top - new_top)
        alpha = jnp.where(work[2, i] == 1, 0.0, alpha)
        expo = jnp.exp2(val - new_top)
        total = total * alpha + jnp.sum(expo, axis=0, keepdims=True)
        acc = acc * alpha + jnp.dot(vs[kc], expo.astype(BF), preferred_element_type=F32)

        @pl.when(work[3, i] == 1)
        def _():
            outs[lax.rem(qb - x + N, N)] = (acc / total).astype(BF)

        return new_top, total, acc

    start = (
        jnp.full((1, block), -1e30, F32),
        jnp.zeros((1, block), F32),
        jnp.zeros((HEAD, block), F32),
    )
    lax.fori_loop(0, count, step, start)
    for k, out in enumerate((o0, o1, o2, o3)):
        out[...] = outs[k]


def pack_kernel(pos, g0, g1, g2, g3, out):
    x = pos[0]
    for k, piece in enumerate((g0, g1, g2, g3)):
        out[lax.rem(x - k + N, N)] = piece[...]


def copy_all(moves, sems):
    copies = [pltpu.make_async_copy(a, b, sems.at[i]) for i, (a, b) in enumerate(moves)]
    for copy in copies:
        copy.start()
    for copy in copies:
        copy.wait()


def fetch_kernel(pos, *refs):
    pieces = refs[0:4]
    near, w_hbm = refs[4:6]
    passed = refs[6:9]
    w_all, up, down, held, sems = refs[9:]
    y = pos[1]
    half = w_hbm.shape[3]
    skip = near.shape[1] - HEAD
    moves = []
    for j in range(N):
        for h in (0, 1):
            cols = slice(h * half, (h + 1) * half)
            moves.append((near.at[2 * j + h, skip : skip + HEAD, :], w_all.at[j, :, cols]))
    for k in range(1, N):
        moves.append((passed[k - 1], w_all.at[k * N : (k + 1) * N]))
    for k in range(N):
        moves.append((pieces[k], held.at[lax.rem(y - k + N, N)]))
    units = up.shape[1]
    for h in (0, 1):
        cols = slice(h * half, (h + 1) * half)
        moves.append((w_hbm.at[:, h, :units, :], up.at[:, :, cols]))
        moves.append((w_hbm.at[:, h, units:, :], down.at[:, :, cols]))
    copy_all(moves, sems)


def fetch_merge_kernel(w_hbm, w, sems):
    parts = sems.shape[0]
    rows = w.shape[0] // parts
    cuts = [slice(i * rows, (i + 1) * rows) for i in range(parts)]
    copy_all([(w_hbm.at[cut], w.at[cut]) for cut in cuts], sems)


def mlp_kernel(offsets, pos, *refs):
    gathered = refs[0:4]
    w_all, up, down, held, gain = refs[4:9]
    outs = refs[9:]
    y = pos[1]
    rows = held.shape[1]
    width = held.shape[2]
    group = N * HEAD
    blocks = [lax.rem(y + k, N) for k in offsets]
    lhs = []
    start = []
    for block in blocks:
        cols = pl.ds(pl.multiple_of(block * rows, rows), rows)
        parts = [g[:, :, cols].reshape(group, rows) for g in gathered]
        lhs.append(jnp.transpose(jnp.concatenate(parts, axis=0)))
        start.append(held[block].astype(F32))
    lhs = jnp.concatenate(lhs, axis=0)
    start = jnp.concatenate(start, axis=0)
    attn = jnp.dot(lhs, w_all[...].reshape(N * group, width), preferred_element_type=F32)
    resid = (start + attn).astype(BF)
    normed = norm_rows(resid.astype(F32), gain[...]).astype(BF)
    count = up.shape[0] * up.shape[1]
    hidden = lax.dot_general(
        normed, up[...].reshape(count, width), NT, preferred_element_type=F32
    )
    hidden = (0.5 * hidden * (1.0 + lax.erf(hidden * math.sqrt(0.5)))).astype(BF)
    result = jnp.dot(hidden, down[...].reshape(count, width), preferred_element_type=F32)
    result = result.astype(BF)
    for i, k in enumerate(offsets):
        outs[i][...] = result[i * rows : (i + 1) * rows, :]
        if k == 0:
            outs[-1][...] = resid[i * rows : (i + 1) * rows, :]


def merge_kernel(early, late, w, select, tail, out, vision):
    sums = (early[...] + late[...].astype(F32)).astype(BF).astype(F32)
    full, width = early.shape
    count = full // 4
    tiles = width // 128
    for i in range(tiles):
        vision[i * full : (i + 1) * full, :] = sums[:, i * 128 : (i + 1) * 128]
    total = jnp.zeros((count, width), F32)
    for j in range(4):
        rows = [vision[pl.ds(i * full + j, count, stride=4), :] for i in range(tiles)]
        rows = jnp.concatenate(rows, axis=1).astype(BF)
        total += jnp.dot(rows, w[j * width : (j + 1) * width, :], preferred_element_type=F32)
    sent = jnp.dot(select[...], total.astype(BF), preferred_element_type=F32)
    out[:, :width] = sent.astype(BF)
    out[:, width:] = tail[...]


def local(
    patches,
    picture_ids,
    ln_attn,
    w_qkv,
    w_out,
    ln_mlp,
    w_up,
    w_down,
    w_merge,
    text_embed,
    slot_dest,
):
    rows = patches[0]
    count, width = rows.shape
    x = lax.axis_index("x")
    y = lax.axis_index("y")
    c = lax.axis_index("c")
    pos = jnp.stack([x, y, lax.axis_index("z"), c]).astype(jnp.int32)
    ids = picture_ids[0]

    half = width // 2
    w_heads = jnp.transpose(w_qkv, (0, 2, 1)).reshape(3 * HEAD, width)
    w_heads = jnp.concatenate([w_heads, w_out], axis=0)
    w_half = lax.dynamic_slice_in_dim(w_heads, c * half, half, 1)
    near = lax.all_gather(w_half, ("x", "c"), axis=0, tiled=False)
    z = lax.axis_index("z")
    units = w_down.shape[0] // N
    sizes = (units, half)
    packed = jnp.concatenate(
        [
            lax.dynamic_slice(w_up.T, (z * units, c * half), sizes),
            lax.dynamic_slice(w_down, (z * units, c * half), sizes),
        ],
        axis=0,
    )
    packed, _ = lax.optimization_barrier((packed, w_half))
    w_near = lax.all_gather(packed, ("x", "z", "c"), axis=0, tiled=False)
    w_near = w_near.reshape(N * N, 2, 2 * units, half)

    pieces = [rows] + [shift(rows, "y", k) for k in (1, 2, 3)]
    total_rows = count * N
    h1 = pl.pallas_call(
        norm_kernel,
        out_shape=jax.ShapeDtypeStruct((2, total_rows, half), BF),
        in_specs=[SMEM] + [HBM] * N + [VMEM],
        out_specs=VMEM,
        scratch_shapes=[
            pltpu.VMEM((N, count, width), BF),
            pltpu.SemaphoreType.DMA((N,)),
        ],
        compiler_params=params(16),
        name="norm",
    )(pos, *[far(piece) for piece in pieces], ln_attn[None, :])
    group_rows = ids.shape[0]
    chunk = 512
    chunks = group_rows // chunk
    held = (ids[:, None] == jnp.arange(16)[None, :]).reshape(chunks, chunk, 16)
    held = jnp.any(held, axis=1)
    per = chunks // N
    wanted = jnp.any(held.reshape(N, per, 16), axis=1)
    need = jnp.any(wanted[:, None, :] & held[None, :, :], axis=2)
    where = jnp.arange(chunks)[None, :]
    low = jnp.min(jnp.where(need, where, chunks - 1), axis=1)
    high = jnp.max(jnp.where(need, where + 1, 1), axis=1)
    low = jnp.minimum(low, high - 1)
    spans = high - low
    index = jnp.arange(N)
    ends = jnp.sum(jnp.where(index[None, :] <= index[:, None], spans[None, :], 0), axis=1)
    item = jnp.arange(N * chunks)
    block = jnp.sum((item[:, None] >= ends[None, :]).astype(jnp.int32), axis=1)
    block = jnp.minimum(block, N - 1)
    mark = block[:, None] == index[None, :]
    begin = jnp.sum(jnp.where(mark, (low + spans - ends)[None, :], 0), axis=1)
    key = jnp.clip(begin + item, 0, chunks - 1)
    is_first = jnp.any(mark & ((ends - spans)[None, :] == item[:, None]), axis=1)
    is_last = jnp.any(mark & ((ends - 1)[None, :] == item[:, None]), axis=1)
    total_items = jnp.full_like(item, 1) * ends[N - 1]
    work = jnp.stack([block, key, is_first, is_last, total_items]).astype(jnp.int32)

    merged_count = count // 4
    dest = slot_dest[0]
    prompt_rows = text_embed.shape[0]
    req_count = N * N
    row_count = lax.axis_size("z") * lax.axis_size("c")
    slot_cap = 2
    owner = jnp.where(dest >= 0, dest // prompt_rows // row_count, -1)
    order = jnp.arange(merged_count)
    same_owner = (owner[:, None] == owner[None, :]) & (order[None, :] < order[:, None])
    ranks = jnp.sum(same_owner.astype(jnp.int32), axis=1)
    target = jnp.where(owner >= 0, owner * slot_cap + ranks, -1)
    select = target[None, :] == jnp.arange(req_count * slot_cap)[:, None]
    places = jnp.sum(jnp.where(select, (dest % prompt_rows + 1)[None, :], 0), axis=1)
    lane = jnp.arange(128)[None, :] == 0
    tail = jnp.where(lane, places[:, None], 0).astype(BF)
    id_row = ids.reshape(N, 1, total_rows)
    id_col = ids[:, None]
    select = select.astype(BF)
    near, h1, work, id_col, select, tail = lax.optimization_barrier(
        (near, h1, work, id_col, select, tail)
    )
    *qkv, mine = pl.pallas_call(
        qkv_kernel,
        out_shape=[jax.ShapeDtypeStruct((3 * HEAD, total_rows), BF)] * N
        + [jax.ShapeDtypeStruct((N, HEAD, width), BF)],
        in_specs=[SMEM, VMEM, HBM],
        out_specs=[VMEM] * (N + 1),
        scratch_shapes=[
            pltpu.VMEM((2 * N, 3 * HEAD, half), BF),
            pltpu.SemaphoreType.DMA((3 * N,)),
        ],
        compiler_params=params(16),
        name="qkv",
    )(pos, h1, far(near))
    blocks = [qkv[0]] + [shift(qkv[k], "x", -k) for k in (1, 2, 3)]
    pass1 = shift(mine, "y", 1)
    pass3 = shift(mine, "y", 3)
    blocks, mine = lax.optimization_barrier((blocks, mine))
    pass2 = shift(mine, "y", 2)

    attended = pl.pallas_call(
        attend_kernel,
        out_shape=[jax.ShapeDtypeStruct((HEAD, total_rows), BF)] * N,
        in_specs=[SMEM, SMEM] + [VMEM] * 6,
        out_specs=[VMEM] * N,
        scratch_shapes=[
            pltpu.VMEM((N, HEAD, total_rows), BF),
            pltpu.VMEM((chunks, chunk, HEAD), BF),
            pltpu.VMEM((chunks, HEAD, chunk), BF),
            pltpu.VMEM((2, chunk, total_rows), F32),
            pltpu.VMEM((N, HEAD, total_rows), BF),
        ],
        compiler_params=params(16),
        name="attend",
    )(pos, work, *blocks, id_row, id_col)
    attended, pass1, pass3 = lax.optimization_barrier((attended, pass1, pass3))
    heads = [attended[0]] + [shift(attended[k], "x", k) for k in (1, 2, 3)]
    heads, pass1, pass2, pass3 = lax.optimization_barrier((heads, pass1, pass2, pass3))
    heads = pl.pallas_call(
        pack_kernel,
        out_shape=jax.ShapeDtypeStruct((N, HEAD, total_rows), BF),
        in_specs=[SMEM] + [VMEM] * N,
        out_specs=VMEM,
        compiler_params=params(8),
        name="pack",
    )(pos, *heads)
    gathered = [heads] + [shift(heads, "y", k) for k in (1, 2, 3)]
    _, near, w_near, w_merge = lax.optimization_barrier((heads, near, w_near, w_merge))

    fetched = pl.pallas_call(
        fetch_kernel,
        out_shape=[
            jax.ShapeDtypeStruct((N * N, HEAD, width), BF),
            jax.ShapeDtypeStruct((N * N, units, width), BF),
            jax.ShapeDtypeStruct((N * N, units, width), BF),
            jax.ShapeDtypeStruct((N, count, width), BF),
        ],
        in_specs=[SMEM] + [HBM] * 9,
        out_specs=[VMEM] * 4,
        scratch_shapes=[pltpu.SemaphoreType.DMA((19,))],
        compiler_params=params(4),
        name="fetch",
    )(
        pos,
        *[far(v) for v in pieces],
        *[far(v) for v in (near, w_near, pass1, pass2, pass3)],
    )

    w_merge = pl.pallas_call(
        fetch_merge_kernel,
        out_shape=jax.ShapeDtypeStruct(w_merge.shape, BF),
        in_specs=[HBM],
        out_specs=VMEM,
        scratch_shapes=[pltpu.SemaphoreType.DMA((8,))],
        compiler_params=params(4),
        name="fetch_merge",
    )(far(w_merge))

    def mlp(offsets, name):
        outputs = len(offsets) + (0 in offsets)
        return pl.pallas_call(
            functools.partial(mlp_kernel, offsets),
            out_shape=[jax.ShapeDtypeStruct((count, width), BF)] * outputs,
            in_specs=[SMEM] + [VMEM] * 9,
            out_specs=[VMEM] * outputs,
            compiler_params=params(24),
            cost_estimate=pl.CostEstimate(
                flops=6 * len(offsets) * count * width * width,
                transcendentals=len(offsets) * count * width,
                bytes_accessed=6 * width * width,
            ),
            name=name,
        )(pos, *gathered, *fetched, ln_mlp[None, :])

    part2, part1 = mlp((2, 1), "mlp_first")
    gathered[0], w_merge, part2, part1 = lax.optimization_barrier(
        (gathered[0], w_merge, part2, part1)
    )
    part3, part0, resid = mlp((3, 0), "mlp_second")
    early = shift(part1, "y", 1).astype(F32) + shift(part2, "y", 2).astype(F32)
    sums = [resid.astype(F32) + part0.astype(F32) + early, shift(part3, "y", 3)]
    outgoing = pl.pallas_call(
        merge_kernel,
        out_shape=jax.ShapeDtypeStruct((req_count * slot_cap, width + 128), BF),
        in_specs=[VMEM] * 5,
        out_specs=VMEM,
        scratch_shapes=[pltpu.VMEM((count * width // 128, 128), F32)],
        compiler_params=params(8),
        name="merge",
    )(*sums, w_merge, select, tail)
    arrived = lax.all_to_all(
        outgoing.reshape(req_count, slot_cap, width + 128),
        ("x", "y"),
        split_axis=0,
        concat_axis=0,
        tiled=True,
    ).reshape(req_count * slot_cap, width + 128)
    landing = arrived[:, width].astype(jnp.int32) - 1
    placer = landing[None, :] == jnp.arange(prompt_rows)[:, None]
    placed = jnp.dot(
        placer.astype(BF), arrived[:, :width], preferred_element_type=F32
    ).astype(BF)
    filled = jnp.any(placer, axis=1)
    return jnp.where(filled[:, None], placed, text_embed)


def solution(mesh):
    grid = Mesh(mesh.devices.reshape(N, N, -1, 2), ("x", "y", "z", "c"))
    req = ("x", "y")
    row = ("z", "c")
    return jax.shard_map(
        local,
        mesh=grid,
        in_specs=(
            P(row, req, None),
            P(row, None),
            P(),
            P(None, None, req),
            P(req, None),
            P(),
            P(None, req),
            P(req, None),
            P(),
            P(("x", "y", "z", "c"), None),
            P(row, req),
        ),
        out_specs=P(("x", "y", "z", "c"), None),
        check_vma=False,
    )
```

```python
import functools
import math

import jax
import jax.numpy as jnp
from jax import lax
from jax.experimental import pallas as pl
from jax.experimental.pallas import tpu as pltpu
from jax.sharding import Mesh
from jax.sharding import PartitionSpec as P

HEAD = 80
SCALE = math.log2(math.e) / math.sqrt(HEAD)
N = 4
BF = jnp.bfloat16
F32 = jnp.float32
NT = (((1,), (1,)), ((), ()))
TN = (((0,), (0,)), ((), ()))
HBM = pl.BlockSpec(memory_space=pltpu.HBM)
VMEM = pl.BlockSpec(memory_space=pltpu.VMEM)
SMEM = pl.BlockSpec(memory_space=pltpu.SMEM)


def params(mib):
    return pltpu.CompilerParams(vmem_limit_bytes=mib << 20)


def norm_rows(rows32, gain):
    center = rows32 - jnp.mean(rows32, axis=-1, keepdims=True)
    spread = jnp.mean(center * center, axis=-1, keepdims=True)
    return center * lax.rsqrt(spread + 1e-06) * gain


def shift(value, axis, step):
    pairs = [(i, (i + step) % N) for i in range(N)]
    return lax.ppermute(value, axis, pairs)


def far(value):
    return pltpu.with_memory_space_constraint(value, pltpu.HBM)


def norm_kernel(pos, p0, p1, p2, p3, gain, h1, held, sems):
    y = pos[1]
    half = h1.shape[2]
    rows = p0.shape[0]
    copies = []
    for k, piece in enumerate((p0, p1, p2, p3)):
        copies.append(pltpu.make_async_copy(piece, held.at[k], sems.at[k]))
    for copy in copies:
        copy.start()
    for k in range(N):
        copies[k].wait()
        normed = norm_rows(held[k].astype(F32), gain[...]).astype(BF)
        at = pl.ds(pl.multiple_of(lax.rem(y - k + N, N) * rows, rows), rows)
        h1[0, at, :] = normed[:, :half]
        h1[1, at, :] = normed[:, half:]


def qkv_kernel(pos, h1, w_hbm, o0, o1, o2, o3, share, w, sems):
    x = pos[0]
    cols = w.shape[1]
    half = w.shape[2]
    copies = []
    for k in range(N):
        at = pl.ds(lax.rem(x - k + N, N) * 2, 2)
        copies.append(pltpu.make_async_copy(w_hbm.at[at, :cols, :], w.at[at], sems.at[k]))
    for j in range(2 * N):
        src = w_hbm.at[j, cols : cols + HEAD, :]
        dst = share.at[j // 2, :, j % 2 * half : (j % 2 + 1) * half]
        copies.append(pltpu.make_async_copy(src, dst, sems.at[N + j]))
    for copy in copies:
        copy.start()
    for k, out in enumerate((o0, o1, o2, o3)):
        at = lax.rem(x - k + N, N) * 2
        copies[k].wait()
        total = lax.dot_general(w[at], h1[0], NT, preferred_element_type=F32)
        total += lax.dot_general(w[at + 1], h1[1], NT, preferred_element_type=F32)
        out[:HEAD, :] = (total[:HEAD, :] * SCALE).astype(BF)
        out[HEAD:, :] = total[HEAD:, :].astype(BF)
    for copy in copies[N:]:
        copy.wait()


def attend_kernel(
    pos, work, r0, r1, r2, r3, id_row, id_col, o0, o1, o2, o3, qs, ks, vs, scores, outs
):
    x = pos[0]
    chunk = ks.shape[1]
    block = qs.shape[2]
    per = block // chunk
    for k, piece in enumerate((r0, r1, r2, r3)):
        at = lax.rem(x + k, N)
        qs[at] = piece[:HEAD, :]
        keys = jnp.transpose(piece[HEAD : 2 * HEAD, :])
        for j in range(per):
            ks[at * per + j] = keys[j * chunk : (j + 1) * chunk, :]
            vs[at * per + j] = piece[2 * HEAD :, j * chunk : (j + 1) * chunk]
    count = work[4, 0]

    def score(i):
        return jnp.dot(ks[work[1, i]], qs[work[0, i]], preferred_element_type=F32)

    scores[0] = score(0)

    def step(i, carry):
        top, total, acc = carry
        slot = lax.rem(i, 2)
        qb = work[0, i]
        kc = work[1, i]
        raw = scores[slot]
        scores[1 - slot] = score(jnp.minimum(i + 1, count - 1))
        key_ids = id_col[pl.ds(pl.multiple_of(kc * chunk, chunk), chunk), :]
        val = jnp.where(key_ids == id_row[qb], raw, -1e30)
        top = jnp.where(work[2, i] == 1, -1e30, top)
        new_top = jnp.maximum(top, jnp.max(val, axis=0, keepdims=True))
        alpha = jnp.exp2(top - new_top)
        alpha = jnp.where(work[2, i] == 1, 0.0, alpha)
        expo = jnp.exp2(val - new_top)
        total = total * alpha + jnp.sum(expo, axis=0, keepdims=True)
        acc = acc * alpha + jnp.dot(vs[kc], expo.astype(BF), preferred_element_type=F32)

        @pl.when(work[3, i] == 1)
        def _():
            outs[lax.rem(qb - x + N, N)] = (acc / total).astype(BF)

        return new_top, total, acc

    start = (
        jnp.full((1, block), -1e30, F32),
        jnp.zeros((1, block), F32),
        jnp.zeros((HEAD, block), F32),
    )
    lax.fori_loop(0, count, step, start)
    for k, out in enumerate((o0, o1, o2, o3)):
        out[...] = outs[k]


def pack_kernel(pos, g0, g1, g2, g3, out):
    x = pos[0]
    for k, piece in enumerate((g0, g1, g2, g3)):
        out[lax.rem(x - k + N, N)] = piece[...]


def copy_all(moves, sems):
    copies = [pltpu.make_async_copy(a, b, sems.at[i]) for i, (a, b) in enumerate(moves)]
    for copy in copies:
        copy.start()
    for copy in copies:
        copy.wait()


def fetch_kernel(pos, *refs):
    pieces = refs[0:4]
    near, w_hbm = refs[4:6]
    passed = refs[6:9]
    w_all, up, down, held, sems = refs[9:]
    y = pos[1]
    half = w_hbm.shape[3]
    skip = near.shape[1] - HEAD
    moves = []
    for j in range(N):
        for h in (0, 1):
            cols = slice(h * half, (h + 1) * half)
            moves.append((near.at[2 * j + h, skip : skip + HEAD, :], w_all.at[j, :, cols]))
    for k in range(1, N):
        moves.append((passed[k - 1], w_all.at[k * N : (k + 1) * N]))
    for k in range(N):
        moves.append((pieces[k], held.at[lax.rem(y - k + N, N)]))
    units = up.shape[1]
    for h in (0, 1):
        cols = slice(h * half, (h + 1) * half)
        moves.append((w_hbm.at[:, h, :units, :], up.at[:, :, cols]))
        moves.append((w_hbm.at[:, h, units:, :], down.at[:, :, cols]))
    copy_all(moves, sems)


def fetch_merge_kernel(w_hbm, w, sems):
    parts = sems.shape[0]
    rows = w.shape[0] // parts
    cuts = [slice(i * rows, (i + 1) * rows) for i in range(parts)]
    copy_all([(w_hbm.at[cut], w.at[cut]) for cut in cuts], sems)


def mlp_kernel(offsets, pos, *refs):
    gathered = refs[0:4]
    w_all, up, down, held, gain = refs[4:9]
    outs = refs[9:]
    y = pos[1]
    rows = held.shape[1]
    width = held.shape[2]
    group = N * HEAD
    blocks = [lax.rem(y + k, N) for k in offsets]
    lhs = []
    start = []
    for block in blocks:
        cols = pl.ds(pl.multiple_of(block * rows, rows), rows)
        parts = [g[:, :, cols].reshape(group, rows) for g in gathered]
        lhs.append(jnp.transpose(jnp.concatenate(parts, axis=0)))
        start.append(held[block].astype(F32))
    lhs = jnp.concatenate(lhs, axis=0)
    start = jnp.concatenate(start, axis=0)
    attn = jnp.dot(lhs, w_all[...].reshape(N * group, width), preferred_element_type=F32)
    resid = (start + attn).astype(BF)
    normed = norm_rows(resid.astype(F32), gain[...]).astype(BF)
    count = up.shape[0] * up.shape[1]
    hidden = lax.dot_general(
        normed, up[...].reshape(count, width), NT, preferred_element_type=F32
    )
    hidden = (0.5 * hidden * (1.0 + lax.erf(hidden * math.sqrt(0.5)))).astype(BF)
    result = jnp.dot(hidden, down[...].reshape(count, width), preferred_element_type=F32)
    result = result.astype(BF)
    for i, k in enumerate(offsets):
        outs[i][...] = result[i * rows : (i + 1) * rows, :]
        if k == 0:
            outs[-1][...] = resid[i * rows : (i + 1) * rows, :]


def merge_kernel(early, late, w, select, tail, out, vision):
    sums = (early[...] + late[...].astype(F32)).astype(BF).astype(F32)
    full, width = early.shape
    count = full // 4
    tiles = width // 128
    for i in range(tiles):
        vision[i * full : (i + 1) * full, :] = sums[:, i * 128 : (i + 1) * 128]
    total = jnp.zeros((count, width), F32)
    for j in range(4):
        rows = [vision[pl.ds(i * full + j, count, stride=4), :] for i in range(tiles)]
        rows = jnp.concatenate(rows, axis=1).astype(BF)
        total += jnp.dot(rows, w[j * width : (j + 1) * width, :], preferred_element_type=F32)
    sent = jnp.dot(select[...], total.astype(BF), preferred_element_type=F32)
    out[:, :width] = sent.astype(BF)
    out[:, width:] = tail[...]


def local(
    patches,
    picture_ids,
    ln_attn,
    w_qkv,
    w_out,
    ln_mlp,
    w_up,
    w_down,
    w_merge,
    text_embed,
    slot_dest,
):
    rows = patches[0]
    count, width = rows.shape
    x = lax.axis_index("x")
    y = lax.axis_index("y")
    c = lax.axis_index("c")
    pos = jnp.stack([x, y, lax.axis_index("z"), c]).astype(jnp.int32)
    ids = picture_ids[0]

    half = width // 2
    w_heads = jnp.transpose(w_qkv, (0, 2, 1)).reshape(3 * HEAD, width)
    w_heads = jnp.concatenate([w_heads, w_out], axis=0)
    w_half = lax.dynamic_slice_in_dim(w_heads, c * half, half, 1)
    near = lax.all_gather(w_half, ("x", "c"), axis=0, tiled=False)
    z = lax.axis_index("z")
    units = w_down.shape[0] // N
    sizes = (units, half)
    packed = jnp.concatenate(
        [
            lax.dynamic_slice(w_up.T, (z * units, c * half), sizes),
            lax.dynamic_slice(w_down, (z * units, c * half), sizes),
        ],
        axis=0,
    )
    packed, _ = lax.optimization_barrier((packed, w_half))
    w_near = lax.all_gather(packed, ("x", "z", "c"), axis=0, tiled=False)
    w_near = w_near.reshape(N * N, 2, 2 * units, half)

    pieces = [rows] + [shift(rows, "y", k) for k in (1, 2, 3)]
    total_rows = count * N
    h1 = pl.pallas_call(
        norm_kernel,
        out_shape=jax.ShapeDtypeStruct((2, total_rows, half), BF),
        in_specs=[SMEM] + [HBM] * N + [VMEM],
        out_specs=VMEM,
        scratch_shapes=[
            pltpu.VMEM((N, count, width), BF),
            pltpu.SemaphoreType.DMA((N,)),
        ],
        compiler_params=params(16),
        name="norm",
    )(pos, *[far(piece) for piece in pieces], ln_attn[None, :])
    group_rows = ids.shape[0]
    chunk = 512
    chunks = group_rows // chunk
    held = (ids[:, None] == jnp.arange(16)[None, :]).reshape(chunks, chunk, 16)
    held = jnp.any(held, axis=1)
    per = chunks // N
    wanted = jnp.any(held.reshape(N, per, 16), axis=1)
    need = jnp.any(wanted[:, None, :] & held[None, :, :], axis=2)
    where = jnp.arange(chunks)[None, :]
    low = jnp.min(jnp.where(need, where, chunks - 1), axis=1)
    high = jnp.max(jnp.where(need, where + 1, 1), axis=1)
    low = jnp.minimum(low, high - 1)
    spans = high - low
    index = jnp.arange(N)
    ends = jnp.sum(jnp.where(index[None, :] <= index[:, None], spans[None, :], 0), axis=1)
    item = jnp.arange(N * chunks)
    block = jnp.sum((item[:, None] >= ends[None, :]).astype(jnp.int32), axis=1)
    block = jnp.minimum(block, N - 1)
    mark = block[:, None] == index[None, :]
    begin = jnp.sum(jnp.where(mark, (low + spans - ends)[None, :], 0), axis=1)
    key = jnp.clip(begin + item, 0, chunks - 1)
    is_first = jnp.any(mark & ((ends - spans)[None, :] == item[:, None]), axis=1)
    is_last = jnp.any(mark & ((ends - 1)[None, :] == item[:, None]), axis=1)
    total_items = jnp.full_like(item, 1) * ends[N - 1]
    work = jnp.stack([block, key, is_first, is_last, total_items]).astype(jnp.int32)

    merged_count = count // 4
    dest = slot_dest[0]
    prompt_rows = text_embed.shape[0]
    req_count = N * N
    row_count = lax.axis_size("z") * lax.axis_size("c")
    slot_cap = 2
    owner = jnp.where(dest >= 0, dest // prompt_rows // row_count, -1)
    order = jnp.arange(merged_count)
    same_owner = (owner[:, None] == owner[None, :]) & (order[None, :] < order[:, None])
    ranks = jnp.sum(same_owner.astype(jnp.int32), axis=1)
    target = jnp.where(owner >= 0, owner * slot_cap + ranks, -1)
    select = target[None, :] == jnp.arange(req_count * slot_cap)[:, None]
    places = jnp.sum(jnp.where(select, (dest % prompt_rows + 1)[None, :], 0), axis=1)
    lane = jnp.arange(128)[None, :] == 0
    tail = jnp.where(lane, places[:, None], 0).astype(BF)
    id_row = ids.reshape(N, 1, total_rows)
    id_col = ids[:, None]
    select = select.astype(BF)
    near, h1, work, id_col, select, tail = lax.optimization_barrier(
        (near, h1, work, id_col, select, tail)
    )
    *qkv, mine = pl.pallas_call(
        qkv_kernel,
        out_shape=[jax.ShapeDtypeStruct((3 * HEAD, total_rows), BF)] * N
        + [jax.ShapeDtypeStruct((N, HEAD, width), BF)],
        in_specs=[SMEM, VMEM, HBM],
        out_specs=[VMEM] * (N + 1),
        scratch_shapes=[
            pltpu.VMEM((2 * N, 3 * HEAD, half), BF),
            pltpu.SemaphoreType.DMA((3 * N,)),
        ],
        compiler_params=params(16),
        name="qkv",
    )(pos, h1, far(near))
    blocks = [qkv[0]] + [shift(qkv[k], "x", -k) for k in (1, 2, 3)]
    pass1 = shift(mine, "y", 1)
    pass3 = shift(mine, "y", 3)
    blocks, mine = lax.optimization_barrier((blocks, mine))
    pass2 = shift(mine, "y", 2)

    attended = pl.pallas_call(
        attend_kernel,
        out_shape=[jax.ShapeDtypeStruct((HEAD, total_rows), BF)] * N,
        in_specs=[SMEM, SMEM] + [VMEM] * 6,
        out_specs=[VMEM] * N,
        scratch_shapes=[
            pltpu.VMEM((N, HEAD, total_rows), BF),
            pltpu.VMEM((chunks, chunk, HEAD), BF),
            pltpu.VMEM((chunks, HEAD, chunk), BF),
            pltpu.VMEM((2, chunk, total_rows), F32),
            pltpu.VMEM((N, HEAD, total_rows), BF),
        ],
        compiler_params=params(16),
        name="attend",
    )(pos, work, *blocks, id_row, id_col)
    heads = [attended[0]] + [shift(attended[k], "x", k) for k in (1, 2, 3)]
    heads, pass1, pass2, pass3 = lax.optimization_barrier((heads, pass1, pass2, pass3))
    heads = pl.pallas_call(
        pack_kernel,
        out_shape=jax.ShapeDtypeStruct((N, HEAD, total_rows), BF),
        in_specs=[SMEM] + [VMEM] * N,
        out_specs=VMEM,
        compiler_params=params(8),
        name="pack",
    )(pos, *heads)
    gathered = [heads] + [shift(heads, "y", k) for k in (1, 2, 3)]
    _, near, w_near, w_merge = lax.optimization_barrier((heads, near, w_near, w_merge))

    fetched = pl.pallas_call(
        fetch_kernel,
        out_shape=[
            jax.ShapeDtypeStruct((N * N, HEAD, width), BF),
            jax.ShapeDtypeStruct((N * N, units, width), BF),
            jax.ShapeDtypeStruct((N * N, units, width), BF),
            jax.ShapeDtypeStruct((N, count, width), BF),
        ],
        in_specs=[SMEM] + [HBM] * 9,
        out_specs=[VMEM] * 4,
        scratch_shapes=[pltpu.SemaphoreType.DMA((19,))],
        compiler_params=params(4),
        name="fetch",
    )(
        pos,
        *[far(v) for v in pieces],
        *[far(v) for v in (near, w_near, pass1, pass2, pass3)],
    )

    w_merge = pl.pallas_call(
        fetch_merge_kernel,
        out_shape=jax.ShapeDtypeStruct(w_merge.shape, BF),
        in_specs=[HBM],
        out_specs=VMEM,
        scratch_shapes=[pltpu.SemaphoreType.DMA((8,))],
        compiler_params=params(4),
        name="fetch_merge",
    )(far(w_merge))

    def mlp(offsets, name):
        outputs = len(offsets) + (0 in offsets)
        return pl.pallas_call(
            functools.partial(mlp_kernel, offsets),
            out_shape=[jax.ShapeDtypeStruct((count, width), BF)] * outputs,
            in_specs=[SMEM] + [VMEM] * 9,
            out_specs=[VMEM] * outputs,
            compiler_params=params(24),
            cost_estimate=pl.CostEstimate(
                flops=6 * len(offsets) * count * width * width,
                transcendentals=len(offsets) * count * width,
                bytes_accessed=6 * width * width,
            ),
            name=name,
        )(pos, *gathered, *fetched, ln_mlp[None, :])

    part2, part1 = mlp((2, 1), "mlp_first")
    gathered[0], w_merge, part2, part1 = lax.optimization_barrier(
        (gathered[0], w_merge, part2, part1)
    )
    part3, part0, resid = mlp((3, 0), "mlp_second")
    early = shift(part1, "y", 1).astype(F32) + shift(part2, "y", 2).astype(F32)
    sums = [resid.astype(F32) + part0.astype(F32) + early, shift(part3, "y", 3)]
    outgoing = pl.pallas_call(
        merge_kernel,
        out_shape=jax.ShapeDtypeStruct((req_count * slot_cap, width + 128), BF),
        in_specs=[VMEM] * 5,
        out_specs=VMEM,
        scratch_shapes=[pltpu.VMEM((count * width // 128, 128), F32)],
        compiler_params=params(8),
        name="merge",
    )(*sums, w_merge, select, tail)
    arrived = lax.all_to_all(
        outgoing.reshape(req_count, slot_cap, width + 128),
        ("x", "y"),
        split_axis=0,
        concat_axis=0,
        tiled=True,
    ).reshape(req_count * slot_cap, width + 128)
    landing = arrived[:, width].astype(jnp.int32) - 1
    placer = landing[None, :] == jnp.arange(prompt_rows)[:, None]
    placed = jnp.dot(
        placer.astype(BF), arrived[:, :width], preferred_element_type=F32
    ).astype(BF)
    filled = jnp.any(placer, axis=1)
    return jnp.where(filled[:, None], placed, text_embed)


def solution(mesh):
    grid = Mesh(mesh.devices.reshape(N, N, -1, 2), ("x", "y", "z", "c"))
    req = ("x", "y")
    row = ("z", "c")
    return jax.shard_map(
        local,
        mesh=grid,
        in_specs=(
            P(row, req, None),
            P(row, None),
            P(),
            P(None, None, req),
            P(req, None),
            P(),
            P(None, req),
            P(req, None),
            P(),
            P(("x", "y", "z", "c"), None),
            P(row, req),
        ),
        out_specs=P(("x", "y", "z", "c"), None),
        check_vma=False,
    )
```

```python
import functools
import math

import jax
import jax.numpy as jnp
from jax import lax
from jax.experimental import pallas as pl
from jax.experimental.pallas import tpu as pltpu
from jax.sharding import Mesh
from jax.sharding import PartitionSpec as P

HEAD = 80
SCALE = math.log2(math.e) / math.sqrt(HEAD)
N = 4
BF = jnp.bfloat16
F32 = jnp.float32
NT = (((1,), (1,)), ((), ()))
TN = (((0,), (0,)), ((), ()))
HBM = pl.BlockSpec(memory_space=pltpu.HBM)
VMEM = pl.BlockSpec(memory_space=pltpu.VMEM)
SMEM = pl.BlockSpec(memory_space=pltpu.SMEM)


def params(mib):
    return pltpu.CompilerParams(vmem_limit_bytes=mib << 20)


def norm_rows(rows32, gain):
    center = rows32 - jnp.mean(rows32, axis=-1, keepdims=True)
    spread = jnp.mean(center * center, axis=-1, keepdims=True)
    return center * lax.rsqrt(spread + 1e-06) * gain


def shift(value, axis, step):
    pairs = [(i, (i + step) % N) for i in range(N)]
    return lax.ppermute(value, axis, pairs)


def far(value):
    return pltpu.with_memory_space_constraint(value, pltpu.HBM)


def swap(value):
    return lax.ppermute(value, "c", [(0, 1), (1, 0)])


def norm_kernel(pos, p0, p1, p2, p3, gain, h1, held, sems):
    y = pos[1]
    half = h1.shape[2]
    rows = p0.shape[0]
    copies = []
    for k, piece in enumerate((p0, p1, p2, p3)):
        copies.append(pltpu.make_async_copy(piece, held.at[k], sems.at[k]))
    for copy in copies:
        copy.start()
    for k in range(N):
        copies[k].wait()
        normed = norm_rows(held[k].astype(F32), gain[...]).astype(BF)
        at = pl.ds(pl.multiple_of(lax.rem(y - k + N, N) * rows, rows), rows)
        h1[0, at, :] = normed[:, :half]
        h1[1, at, :] = normed[:, half:]


def qkv_kernel(pos, h1, w_hbm, o0, o1, o2, o3, share, share_half, w, sems):
    x = pos[0]
    cols = w.shape[1]
    half = w.shape[2]
    copies = []
    for k in range(N):
        at = pl.ds(lax.rem(x - k + N, N) * 2, 2)
        copies.append(pltpu.make_async_copy(w_hbm.at[at, :cols, :], w.at[at], sems.at[k]))
    for j in range(2 * N):
        src = w_hbm.at[j, cols : cols + HEAD, :]
        dst = share.at[j // 2, :, j % 2 * half : (j % 2 + 1) * half]
        copies.append(pltpu.make_async_copy(src, dst, sems.at[N + j]))
    for j in range(N):
        src = w_hbm.at[2 * j + pos[3], cols : cols + HEAD, :]
        copies.append(pltpu.make_async_copy(src, share_half.at[j], sems.at[3 * N + j]))
    for copy in copies:
        copy.start()
    for k, out in enumerate((o0, o1, o2, o3)):
        at = lax.rem(x - k + N, N) * 2
        copies[k].wait()
        total = lax.dot_general(w[at], h1[0], NT, preferred_element_type=F32)
        total += lax.dot_general(w[at + 1], h1[1], NT, preferred_element_type=F32)
        out[:HEAD, :] = (total[:HEAD, :] * SCALE).astype(BF)
        out[HEAD:, :] = total[HEAD:, :].astype(BF)
    for copy in copies[N:]:
        copy.wait()


def attend_kernel(
    pos, work, r0, r1, r2, r3, id_row, id_col, o0, o1, o2, o3, qs, ks, vs, scores, outs
):
    x = pos[0]
    chunk = ks.shape[1]
    block = qs.shape[2]
    per = block // chunk
    for k, piece in enumerate((r0, r1, r2, r3)):
        at = lax.rem(x + k, N)
        qs[at] = piece[:HEAD, :]
        keys = jnp.transpose(piece[HEAD : 2 * HEAD, :])
        for j in range(per):
            ks[at * per + j] = keys[j * chunk : (j + 1) * chunk, :]
            vs[at * per + j] = piece[2 * HEAD :, j * chunk : (j + 1) * chunk]
    count = work[4, 0]

    def score(i):
        return jnp.dot(ks[work[1, i]], qs[work[0, i]], preferred_element_type=F32)

    scores[0] = score(0)

    def step(i, carry):
        top, total, acc = carry
        slot = lax.rem(i, 2)
        qb = work[0, i]
        kc = work[1, i]
        raw = scores[slot]
        scores[1 - slot] = score(jnp.minimum(i + 1, count - 1))
        key_ids = id_col[pl.ds(pl.multiple_of(kc * chunk, chunk), chunk), :]
        val = jnp.where(key_ids == id_row[qb], raw, -1e30)
        top = jnp.where(work[2, i] == 1, -1e30, top)
        new_top = jnp.maximum(top, jnp.max(val, axis=0, keepdims=True))
        alpha = jnp.exp2(top - new_top)
        alpha = jnp.where(work[2, i] == 1, 0.0, alpha)
        expo = jnp.exp2(val - new_top)
        total = total * alpha + jnp.sum(expo, axis=0, keepdims=True)
        acc = acc * alpha + jnp.dot(vs[kc], expo.astype(BF), preferred_element_type=F32)

        @pl.when(work[3, i] == 1)
        def _():
            outs[lax.rem(qb - x + N, N)] = (acc / total).astype(BF)

        return new_top, total, acc

    start = (
        jnp.full((1, block), -1e30, F32),
        jnp.zeros((1, block), F32),
        jnp.zeros((HEAD, block), F32),
    )
    lax.fori_loop(0, count, step, start)
    for k, out in enumerate((o0, o1, o2, o3)):
        out[...] = outs[k]


def pack_kernel(pos, g0, g1, g2, g3, out):
    x = pos[0]
    for k, piece in enumerate((g0, g1, g2, g3)):
        out[lax.rem(x - k + N, N)] = piece[...]


def copy_all(moves, sems):
    copies = [pltpu.make_async_copy(a, b, sems.at[i]) for i, (a, b) in enumerate(moves)]
    for copy in copies:
        copy.start()
    for copy in copies:
        copy.wait()


def fetch_kernel(pos, *refs):
    pieces = refs[0:4]
    near, w_hbm = refs[4:6]
    pass1, pass3, mine, other = refs[6:10]
    w_all, up, down, held, sems = refs[10:]
    y = pos[1]
    half = w_hbm.shape[3]
    skip = near.shape[1] - HEAD
    moves = []
    for j in range(N):
        for h in (0, 1):
            cols = slice(h * half, (h + 1) * half)
            moves.append((near.at[2 * j + h, skip : skip + HEAD, :], w_all.at[j, :, cols]))
    moves.append((pass1, w_all.at[N : 2 * N]))
    moves.append((pass3, w_all.at[3 * N :]))
    for k in range(N):
        moves.append((pieces[k], held.at[lax.rem(y - k + N, N)]))
    units = up.shape[1]
    for h in (0, 1):
        cols = slice(h * half, (h + 1) * half)
        moves.append((w_hbm.at[:, h, :units, :], up.at[:, :, cols]))
        moves.append((w_hbm.at[:, h, units:, :], down.at[:, :, cols]))
    for core in (0, 1):
        low = slice(core * half, (core + 1) * half)
        high = slice((1 - core) * half, (2 - core) * half)
        rows = slice(2 * N, 3 * N)

        @pl.when(pos[3] == core)
        def _(low=low, high=high, rows=rows):
            pair = [(mine, w_all.at[rows, :, low]), (other, w_all.at[rows, :, high])]
            copy_all(moves + pair, sems)


def fetch_merge_kernel(w_hbm, w, sems):
    parts = sems.shape[0]
    rows = w.shape[0] // parts
    cuts = [slice(i * rows, (i + 1) * rows) for i in range(parts)]
    copy_all([(w_hbm.at[cut], w.at[cut]) for cut in cuts], sems)


def mlp_kernel(offsets, pos, *refs):
    gathered = refs[0:4]
    w_all, up, down, held, gain = refs[4:9]
    outs = refs[9:]
    y = pos[1]
    rows = held.shape[1]
    width = held.shape[2]
    group = N * HEAD
    blocks = [lax.rem(y + k, N) for k in offsets]
    lhs = []
    start = []
    for block in blocks:
        cols = pl.ds(pl.multiple_of(block * rows, rows), rows)
        parts = [g[:, :, cols].reshape(group, rows) for g in gathered]
        lhs.append(jnp.transpose(jnp.concatenate(parts, axis=0)))
        start.append(held[block].astype(F32))
    lhs = jnp.concatenate(lhs, axis=0)
    start = jnp.concatenate(start, axis=0)
    attn = jnp.dot(lhs, w_all[...].reshape(N * group, width), preferred_element_type=F32)
    resid = (start + attn).astype(BF)
    normed = norm_rows(resid.astype(F32), gain[...]).astype(BF)
    count = up.shape[0] * up.shape[1]
    hidden = lax.dot_general(
        normed, up[...].reshape(count, width), NT, preferred_element_type=F32
    )
    hidden = (0.5 * hidden * (1.0 + lax.erf(hidden * math.sqrt(0.5)))).astype(BF)
    result = jnp.dot(hidden, down[...].reshape(count, width), preferred_element_type=F32)
    result = result.astype(BF)
    for i, k in enumerate(offsets):
        outs[i][...] = result[i * rows : (i + 1) * rows, :]
        if k == 0:
            outs[-1][...] = resid[i * rows : (i + 1) * rows, :]


def merge_kernel(early, late, w, select, tail, out, vision):
    sums = (early[...] + late[...].astype(F32)).astype(BF).astype(F32)
    full, width = early.shape
    count = full // 4
    tiles = width // 128
    for i in range(tiles):
        vision[i * full : (i + 1) * full, :] = sums[:, i * 128 : (i + 1) * 128]
    total = jnp.zeros((count, width), F32)
    for j in range(4):
        rows = [vision[pl.ds(i * full + j, count, stride=4), :] for i in range(tiles)]
        rows = jnp.concatenate(rows, axis=1).astype(BF)
        total += jnp.dot(rows, w[j * width : (j + 1) * width, :], preferred_element_type=F32)
    sent = jnp.dot(select[...], total.astype(BF), preferred_element_type=F32)
    out[:, :width] = sent.astype(BF)
    out[:, width:] = tail[...]


def local(
    patches,
    picture_ids,
    ln_attn,
    w_qkv,
    w_out,
    ln_mlp,
    w_up,
    w_down,
    w_merge,
    text_embed,
    slot_dest,
):
    rows = patches[0]
    count, width = rows.shape
    x = lax.axis_index("x")
    y = lax.axis_index("y")
    c = lax.axis_index("c")
    pos = jnp.stack([x, y, lax.axis_index("z"), c]).astype(jnp.int32)
    ids = picture_ids[0]

    half = width // 2
    w_heads = jnp.transpose(w_qkv, (0, 2, 1)).reshape(3 * HEAD, width)
    w_heads = jnp.concatenate([w_heads, w_out], axis=0)
    w_half = lax.dynamic_slice_in_dim(w_heads, c * half, half, 1)
    near = lax.all_gather(w_half, ("x", "c"), axis=0, tiled=False)
    z = lax.axis_index("z")
    units = w_down.shape[0] // N
    sizes = (units, half)
    packed = jnp.concatenate(
        [
            lax.dynamic_slice(w_up.T, (z * units, c * half), sizes),
            lax.dynamic_slice(w_down, (z * units, c * half), sizes),
        ],
        axis=0,
    )
    packed, _ = lax.optimization_barrier((packed, w_half))
    w_near = lax.all_gather(packed, ("x", "z", "c"), axis=0, tiled=False)
    w_near = w_near.reshape(N * N, 2, 2 * units, half)

    pieces = [rows] + [shift(rows, "y", k) for k in (1, 2, 3)]
    total_rows = count * N
    h1 = pl.pallas_call(
        norm_kernel,
        out_shape=jax.ShapeDtypeStruct((2, total_rows, half), BF),
        in_specs=[SMEM] + [HBM] * N + [VMEM],
        out_specs=VMEM,
        scratch_shapes=[
            pltpu.VMEM((N, count, width), BF),
            pltpu.SemaphoreType.DMA((N,)),
        ],
        compiler_params=params(16),
        name="norm",
    )(pos, *[far(piece) for piece in pieces], ln_attn[None, :])
    group_rows = ids.shape[0]
    chunk = 512
    chunks = group_rows // chunk
    held = (ids[:, None] == jnp.arange(16)[None, :]).reshape(chunks, chunk, 16)
    held = jnp.any(held, axis=1)
    per = chunks // N
    wanted = jnp.any(held.reshape(N, per, 16), axis=1)
    need = jnp.any(wanted[:, None, :] & held[None, :, :], axis=2)
    where = jnp.arange(chunks)[None, :]
    low = jnp.min(jnp.where(need, where, chunks - 1), axis=1)
    high = jnp.max(jnp.where(need, where + 1, 1), axis=1)
    low = jnp.minimum(low, high - 1)
    spans = high - low
    index = jnp.arange(N)
    ends = jnp.sum(jnp.where(index[None, :] <= index[:, None], spans[None, :], 0), axis=1)
    item = jnp.arange(N * chunks)
    block = jnp.sum((item[:, None] >= ends[None, :]).astype(jnp.int32), axis=1)
    block = jnp.minimum(block, N - 1)
    mark = block[:, None] == index[None, :]
    begin = jnp.sum(jnp.where(mark, (low + spans - ends)[None, :], 0), axis=1)
    key = jnp.clip(begin + item, 0, chunks - 1)
    is_first = jnp.any(mark & ((ends - spans)[None, :] == item[:, None]), axis=1)
    is_last = jnp.any(mark & ((ends - 1)[None, :] == item[:, None]), axis=1)
    total_items = jnp.full_like(item, 1) * ends[N - 1]
    work = jnp.stack([block, key, is_first, is_last, total_items]).astype(jnp.int32)

    merged_count = count // 4
    dest = slot_dest[0]
    prompt_rows = text_embed.shape[0]
    req_count = N * N
    row_count = lax.axis_size("z") * lax.axis_size("c")
    slot_cap = 2
    owner = jnp.where(dest >= 0, dest // prompt_rows // row_count, -1)
    order = jnp.arange(merged_count)
    same_owner = (owner[:, None] == owner[None, :]) & (order[None, :] < order[:, None])
    ranks = jnp.sum(same_owner.astype(jnp.int32), axis=1)
    target = jnp.where(owner >= 0, owner * slot_cap + ranks, -1)
    select = target[None, :] == jnp.arange(req_count * slot_cap)[:, None]
    places = jnp.sum(jnp.where(select, (dest % prompt_rows + 1)[None, :], 0), axis=1)
    lane = jnp.arange(128)[None, :] == 0
    tail = jnp.where(lane, places[:, None], 0).astype(BF)
    id_row = ids.reshape(N, 1, total_rows)
    id_col = ids[:, None]
    select = select.astype(BF)
    near, h1, work, id_col, select, tail = lax.optimization_barrier(
        (near, h1, work, id_col, select, tail)
    )
    *qkv, mine, mine_half = pl.pallas_call(
        qkv_kernel,
        out_shape=[jax.ShapeDtypeStruct((3 * HEAD, total_rows), BF)] * N
        + [
            jax.ShapeDtypeStruct((N, HEAD, width), BF),
            jax.ShapeDtypeStruct((N, HEAD, half), BF),
        ],
        in_specs=[SMEM, VMEM, HBM],
        out_specs=[VMEM] * (N + 2),
        scratch_shapes=[
            pltpu.VMEM((2 * N, 3 * HEAD, half), BF),
            pltpu.SemaphoreType.DMA((4 * N,)),
        ],
        compiler_params=params(16),
        name="qkv",
    )(pos, h1, far(near))
    blocks = [qkv[0]] + [shift(qkv[k], "x", -k) for k in (1, 2, 3)]
    pass1 = shift(mine, "y", 1)
    pass3 = shift(mine, "y", 3)
    blocks, mine_half = lax.optimization_barrier((blocks, mine_half))
    pass2 = shift(mine_half, "y", 2)

    attended = pl.pallas_call(
        attend_kernel,
        out_shape=[jax.ShapeDtypeStruct((HEAD, total_rows), BF)] * N,
        in_specs=[SMEM, SMEM] + [VMEM] * 6,
        out_specs=[VMEM] * N,
        scratch_shapes=[
            pltpu.VMEM((N, HEAD, total_rows), BF),
            pltpu.VMEM((chunks, chunk, HEAD), BF),
            pltpu.VMEM((chunks, HEAD, chunk), BF),
            pltpu.VMEM((2, chunk, total_rows), F32),
            pltpu.VMEM((N, HEAD, total_rows), BF),
        ],
        compiler_params=params(16),
        name="attend",
    )(pos, work, *blocks, id_row, id_col)
    attended, pass2 = lax.optimization_barrier((attended, pass2))
    swap2 = swap(pass2)
    heads = [attended[0]] + [shift(attended[k], "x", k) for k in (1, 2, 3)]
    heads, pass1, pass3 = lax.optimization_barrier((heads, pass1, pass3))
    heads = pl.pallas_call(
        pack_kernel,
        out_shape=jax.ShapeDtypeStruct((N, HEAD, total_rows), BF),
        in_specs=[SMEM] + [VMEM] * N,
        out_specs=VMEM,
        compiler_params=params(8),
        name="pack",
    )(pos, *heads)
    gathered = [heads] + [shift(heads, "y", k) for k in (1, 2, 3)]
    _, near, w_near, w_merge = lax.optimization_barrier((heads, near, w_near, w_merge))

    fetched = pl.pallas_call(
        fetch_kernel,
        out_shape=[
            jax.ShapeDtypeStruct((N * N, HEAD, width), BF),
            jax.ShapeDtypeStruct((N * N, units, width), BF),
            jax.ShapeDtypeStruct((N * N, units, width), BF),
            jax.ShapeDtypeStruct((N, count, width), BF),
        ],
        in_specs=[SMEM] + [HBM] * 10,
        out_specs=[VMEM] * 4,
        scratch_shapes=[pltpu.SemaphoreType.DMA((20,))],
        compiler_params=params(4),
        name="fetch",
    )(
        pos,
        *[far(v) for v in pieces],
        *[far(v) for v in (near, w_near, pass1, pass3, pass2, swap2)],
    )

    w_merge = pl.pallas_call(
        fetch_merge_kernel,
        out_shape=jax.ShapeDtypeStruct(w_merge.shape, BF),
        in_specs=[HBM],
        out_specs=VMEM,
        scratch_shapes=[pltpu.SemaphoreType.DMA((8,))],
        compiler_params=params(4),
        name="fetch_merge",
    )(far(w_merge))

    def mlp(offsets, name):
        outputs = len(offsets) + (0 in offsets)
        return pl.pallas_call(
            functools.partial(mlp_kernel, offsets),
            out_shape=[jax.ShapeDtypeStruct((count, width), BF)] * outputs,
            in_specs=[SMEM] + [VMEM] * 9,
            out_specs=[VMEM] * outputs,
            compiler_params=params(24),
            cost_estimate=pl.CostEstimate(
                flops=6 * len(offsets) * count * width * width,
                transcendentals=len(offsets) * count * width,
                bytes_accessed=6 * width * width,
            ),
            name=name,
        )(pos, *gathered, *fetched, ln_mlp[None, :])

    part2, part1 = mlp((2, 1), "mlp_first")
    gathered[0], w_merge, part2, part1 = lax.optimization_barrier(
        (gathered[0], w_merge, part2, part1)
    )
    part3, part0, resid = mlp((3, 0), "mlp_second")
    early = shift(part1, "y", 1).astype(F32) + shift(part2, "y", 2).astype(F32)
    sums = [resid.astype(F32) + part0.astype(F32) + early, shift(part3, "y", 3)]
    outgoing = pl.pallas_call(
        merge_kernel,
        out_shape=jax.ShapeDtypeStruct((req_count * slot_cap, width + 128), BF),
        in_specs=[VMEM] * 5,
        out_specs=VMEM,
        scratch_shapes=[pltpu.VMEM((count * width // 128, 128), F32)],
        compiler_params=params(8),
        name="merge",
    )(*sums, w_merge, select, tail)
    arrived = lax.all_to_all(
        outgoing.reshape(req_count, slot_cap, width + 128),
        ("x", "y"),
        split_axis=0,
        concat_axis=0,
        tiled=True,
    ).reshape(req_count * slot_cap, width + 128)
    landing = arrived[:, width].astype(jnp.int32) - 1
    placer = landing[None, :] == jnp.arange(prompt_rows)[:, None]
    placed = jnp.dot(
        placer.astype(BF), arrived[:, :width], preferred_element_type=F32
    ).astype(BF)
    filled = jnp.any(placer, axis=1)
    return jnp.where(filled[:, None], placed, text_embed)


def solution(mesh):
    grid = Mesh(mesh.devices.reshape(N, N, -1, 2), ("x", "y", "z", "c"))
    req = ("x", "y")
    row = ("z", "c")
    return jax.shard_map(
        local,
        mesh=grid,
        in_specs=(
            P(row, req, None),
            P(row, None),
            P(),
            P(None, None, req),
            P(req, None),
            P(),
            P(None, req),
            P(req, None),
            P(),
            P(("x", "y", "z", "c"), None),
            P(row, req),
        ),
        out_specs=P(("x", "y", "z", "c"), None),
        check_vma=False,
    )
```

```python
import functools
import math

import jax
import jax.numpy as jnp
from jax import lax
from jax.experimental import pallas as pl
from jax.experimental.pallas import tpu as pltpu
from jax.sharding import Mesh
from jax.sharding import PartitionSpec as P

HEAD = 80
SCALE = math.log2(math.e) / math.sqrt(HEAD)
N = 4
BF = jnp.bfloat16
F32 = jnp.float32
NT = (((1,), (1,)), ((), ()))
TN = (((0,), (0,)), ((), ()))
HBM = pl.BlockSpec(memory_space=pltpu.HBM)
VMEM = pl.BlockSpec(memory_space=pltpu.VMEM)
SMEM = pl.BlockSpec(memory_space=pltpu.SMEM)


def params(mib):
    return pltpu.CompilerParams(vmem_limit_bytes=mib << 20)


def norm_rows(rows32, gain):
    center = rows32 - jnp.mean(rows32, axis=-1, keepdims=True)
    spread = jnp.mean(center * center, axis=-1, keepdims=True)
    return center * lax.rsqrt(spread + 1e-06) * gain


def shift(value, axis, step):
    pairs = [(i, (i + step) % N) for i in range(N)]
    return lax.ppermute(value, axis, pairs)


def far(value):
    return pltpu.with_memory_space_constraint(value, pltpu.HBM)


def swap(value):
    return lax.ppermute(value, "c", [(0, 1), (1, 0)])


def norm_kernel(pos, p0, p1, p2, p3, gain, h1, held, sems):
    y = pos[1]
    half = h1.shape[2]
    rows = p0.shape[0]
    copies = []
    for k, piece in enumerate((p0, p1, p2, p3)):
        copies.append(pltpu.make_async_copy(piece, held.at[k], sems.at[k]))
    for copy in copies:
        copy.start()
    for k in range(N):
        copies[k].wait()
        normed = norm_rows(held[k].astype(F32), gain[...]).astype(BF)
        at = pl.ds(pl.multiple_of(lax.rem(y - k + N, N) * rows, rows), rows)
        h1[0, at, :] = normed[:, :half]
        h1[1, at, :] = normed[:, half:]


def qkv_kernel(pos, h1, w_hbm, o0, o1, o2, o3, share, share_half, w, sems):
    x = pos[0]
    cols = w.shape[1]
    half = w.shape[2]
    copies = []
    for k in range(N):
        at = pl.ds(lax.rem(x - k + N, N) * 2, 2)
        copies.append(pltpu.make_async_copy(w_hbm.at[at, :cols, :], w.at[at], sems.at[k]))
    for j in range(2 * N):
        src = w_hbm.at[j, cols : cols + HEAD, :]
        dst = share.at[j // 2, :, j % 2 * half : (j % 2 + 1) * half]
        copies.append(pltpu.make_async_copy(src, dst, sems.at[N + j]))
    for j in range(N):
        src = w_hbm.at[2 * j + pos[3], cols : cols + HEAD, :]
        copies.append(pltpu.make_async_copy(src, share_half.at[j], sems.at[3 * N + j]))
    for copy in copies:
        copy.start()
    for k, out in enumerate((o0, o1, o2, o3)):
        at = lax.rem(x - k + N, N) * 2
        copies[k].wait()
        total = lax.dot_general(w[at], h1[0], NT, preferred_element_type=F32)
        total += lax.dot_general(w[at + 1], h1[1], NT, preferred_element_type=F32)
        out[:HEAD, :] = (total[:HEAD, :] * SCALE).astype(BF)
        out[HEAD:, :] = total[HEAD:, :].astype(BF)
    for copy in copies[N:]:
        copy.wait()


def attend_kernel(
    pos, work, r0, r1, r2, r3, id_row, id_col, o0, o1, o2, o3, qs, ks, vs, scores, outs
):
    x = pos[0]
    chunk = ks.shape[1]
    block = qs.shape[2]
    per = block // chunk
    for k, piece in enumerate((r0, r1, r2, r3)):
        at = lax.rem(x + k, N)
        qs[at] = piece[:HEAD, :]
        keys = jnp.transpose(piece[HEAD : 2 * HEAD, :])
        for j in range(per):
            ks[at * per + j] = keys[j * chunk : (j + 1) * chunk, :]
            vs[at * per + j] = piece[2 * HEAD :, j * chunk : (j + 1) * chunk]
    count = work[4, 0]

    def score(i):
        return jnp.dot(ks[work[1, i]], qs[work[0, i]], preferred_element_type=F32)

    scores[0] = score(0)

    def step(i, carry):
        top, total, acc = carry
        slot = lax.rem(i, 2)
        qb = work[0, i]
        kc = work[1, i]
        raw = scores[slot]
        scores[1 - slot] = score(jnp.minimum(i + 1, count - 1))
        key_ids = id_col[pl.ds(pl.multiple_of(kc * chunk, chunk), chunk), :]
        val = jnp.where(key_ids == id_row[qb], raw, -1e30)
        top = jnp.where(work[2, i] == 1, -1e30, top)
        new_top = jnp.maximum(top, jnp.max(val, axis=0, keepdims=True))
        alpha = jnp.exp2(top - new_top)
        alpha = jnp.where(work[2, i] == 1, 0.0, alpha)
        expo = jnp.exp2(val - new_top)
        total = total * alpha + jnp.sum(expo, axis=0, keepdims=True)
        acc = acc * alpha + jnp.dot(vs[kc], expo.astype(BF), preferred_element_type=F32)

        @pl.when(work[3, i] == 1)
        def _():
            outs[lax.rem(qb - x + N, N)] = (acc / total).astype(BF)

        return new_top, total, acc

    start = (
        jnp.full((1, block), -1e30, F32),
        jnp.zeros((1, block), F32),
        jnp.zeros((HEAD, block), F32),
    )
    lax.fori_loop(0, count, step, start)
    for k, out in enumerate((o0, o1, o2, o3)):
        out[...] = outs[k]


def pack_kernel(pos, g0, g1, g2, g3, out):
    x = pos[0]
    for k, piece in enumerate((g0, g1, g2, g3)):
        out[lax.rem(x - k + N, N)] = piece[...]


def copy_all(moves, sems):
    copies = [pltpu.make_async_copy(a, b, sems.at[i]) for i, (a, b) in enumerate(moves)]
    for copy in copies:
        copy.start()
    for copy in copies:
        copy.wait()


def fetch_kernel(pos, *refs):
    pieces = refs[0:4]
    near, w_hbm = refs[4:6]
    pass1, pass3, mine, other = refs[6:10]
    w_all, up, down, held, sems = refs[10:]
    y = pos[1]
    half = w_hbm.shape[3]
    skip = near.shape[1] - HEAD
    moves = []
    for j in range(N):
        for h in (0, 1):
            cols = slice(h * half, (h + 1) * half)
            moves.append((near.at[2 * j + h, skip : skip + HEAD, :], w_all.at[j, :, cols]))
    moves.append((pass1, w_all.at[N : 2 * N]))
    moves.append((pass3, w_all.at[3 * N :]))
    for k in range(N):
        moves.append((pieces[k], held.at[lax.rem(y - k + N, N)]))
    units = up.shape[1]
    for h in (0, 1):
        cols = slice(h * half, (h + 1) * half)
        moves.append((w_hbm.at[:, h, :units, :], up.at[:, :, cols]))
        moves.append((w_hbm.at[:, h, units:, :], down.at[:, :, cols]))
    for core in (0, 1):
        low = slice(core * half, (core + 1) * half)
        high = slice((1 - core) * half, (2 - core) * half)
        rows = slice(2 * N, 3 * N)

        @pl.when(pos[3] == core)
        def _(low=low, high=high, rows=rows):
            pair = [(mine, w_all.at[rows, :, low]), (other, w_all.at[rows, :, high])]
            copy_all(moves + pair, sems)


def fetch_merge_kernel(w_hbm, w, sems):
    parts = sems.shape[0]
    rows = w.shape[0] // parts
    cuts = [slice(i * rows, (i + 1) * rows) for i in range(parts)]
    copy_all([(w_hbm.at[cut], w.at[cut]) for cut in cuts], sems)


def mlp_kernel(offsets, pos, *refs):
    gathered = refs[0:4]
    w_all, up, down, held, gain = refs[4:9]
    outs = refs[9:]
    y = pos[1]
    rows = held.shape[1]
    width = held.shape[2]
    group = N * HEAD
    blocks = [lax.rem(y + k, N) for k in offsets]
    lhs = []
    start = []
    for block in blocks:
        cols = pl.ds(pl.multiple_of(block * rows, rows), rows)
        parts = [g[:, :, cols].reshape(group, rows) for g in gathered]
        lhs.append(jnp.transpose(jnp.concatenate(parts, axis=0)))
        start.append(held[block].astype(F32))
    lhs = jnp.concatenate(lhs, axis=0)
    start = jnp.concatenate(start, axis=0)
    attn = jnp.dot(lhs, w_all[...].reshape(N * group, width), preferred_element_type=F32)
    resid = (start + attn).astype(BF)
    normed = norm_rows(resid.astype(F32), gain[...]).astype(BF)
    count = up.shape[0] * up.shape[1]
    hidden = lax.dot_general(
        normed, up[...].reshape(count, width), NT, preferred_element_type=F32
    )
    hidden = (0.5 * hidden * (1.0 + lax.erf(hidden * math.sqrt(0.5)))).astype(BF)
    result = jnp.dot(hidden, down[...].reshape(count, width), preferred_element_type=F32)
    result = result.astype(BF)
    for i, k in enumerate(offsets):
        outs[i][...] = result[i * rows : (i + 1) * rows, :]
        if k == 0:
            outs[-1][...] = resid[i * rows : (i + 1) * rows, :]


def merge_kernel(early, late, w, select, tail, out, vision):
    sums = (early[...] + late[...].astype(F32)).astype(BF).astype(F32)
    full, width = early.shape
    count = full // 4
    tiles = width // 128
    for i in range(tiles):
        vision[i * full : (i + 1) * full, :] = sums[:, i * 128 : (i + 1) * 128]
    total = jnp.zeros((count, width), F32)
    for j in range(4):
        rows = [vision[pl.ds(i * full + j, count, stride=4), :] for i in range(tiles)]
        rows = jnp.concatenate(rows, axis=1).astype(BF)
        total += jnp.dot(rows, w[j * width : (j + 1) * width, :], preferred_element_type=F32)
    sent = jnp.dot(select[...], total.astype(BF), preferred_element_type=F32)
    out[:, :width] = sent.astype(BF)
    out[:, width:] = tail[...]


def local(
    patches,
    picture_ids,
    ln_attn,
    w_qkv,
    w_out,
    ln_mlp,
    w_up,
    w_down,
    w_merge,
    text_embed,
    slot_dest,
):
    rows = patches[0]
    count, width = rows.shape
    x = lax.axis_index("x")
    y = lax.axis_index("y")
    c = lax.axis_index("c")
    pos = jnp.stack([x, y, lax.axis_index("z"), c]).astype(jnp.int32)
    ids = picture_ids[0]

    half = width // 2
    w_heads = jnp.transpose(w_qkv, (0, 2, 1)).reshape(3 * HEAD, width)
    w_heads = jnp.concatenate([w_heads, w_out], axis=0)
    w_half = lax.dynamic_slice_in_dim(w_heads, c * half, half, 1)
    near = lax.all_gather(w_half, ("x", "c"), axis=0, tiled=False)
    z = lax.axis_index("z")
    units = w_down.shape[0] // N
    sizes = (units, half)
    packed = jnp.concatenate(
        [
            lax.dynamic_slice(w_up.T, (z * units, c * half), sizes),
            lax.dynamic_slice(w_down, (z * units, c * half), sizes),
        ],
        axis=0,
    )
    packed, _ = lax.optimization_barrier((packed, w_half))
    w_near = lax.all_gather(packed, ("x", "z", "c"), axis=0, tiled=False)
    w_near = w_near.reshape(N * N, 2, 2 * units, half)

    pieces = [rows] + [shift(rows, "y", k) for k in (1, 2, 3)]
    total_rows = count * N
    h1 = pl.pallas_call(
        norm_kernel,
        out_shape=jax.ShapeDtypeStruct((2, total_rows, half), BF),
        in_specs=[SMEM] + [HBM] * N + [VMEM],
        out_specs=VMEM,
        scratch_shapes=[
            pltpu.VMEM((N, count, width), BF),
            pltpu.SemaphoreType.DMA((N,)),
        ],
        compiler_params=params(16),
        name="norm",
    )(pos, *[far(piece) for piece in pieces], ln_attn[None, :])
    group_rows = ids.shape[0]
    chunk = 512
    chunks = group_rows // chunk
    held = (ids[:, None] == jnp.arange(16)[None, :]).reshape(chunks, chunk, 16)
    held = jnp.any(held, axis=1)
    per = chunks // N
    wanted = jnp.any(held.reshape(N, per, 16), axis=1)
    need = jnp.any(wanted[:, None, :] & held[None, :, :], axis=2)
    where = jnp.arange(chunks)[None, :]
    low = jnp.min(jnp.where(need, where, chunks - 1), axis=1)
    high = jnp.max(jnp.where(need, where + 1, 1), axis=1)
    low = jnp.minimum(low, high - 1)
    spans = high - low
    index = jnp.arange(N)
    ends = jnp.sum(jnp.where(index[None, :] <= index[:, None], spans[None, :], 0), axis=1)
    item = jnp.arange(N * chunks)
    block = jnp.sum((item[:, None] >= ends[None, :]).astype(jnp.int32), axis=1)
    block = jnp.minimum(block, N - 1)
    mark = block[:, None] == index[None, :]
    begin = jnp.sum(jnp.where(mark, (low + spans - ends)[None, :], 0), axis=1)
    key = jnp.clip(begin + item, 0, chunks - 1)
    is_first = jnp.any(mark & ((ends - spans)[None, :] == item[:, None]), axis=1)
    is_last = jnp.any(mark & ((ends - 1)[None, :] == item[:, None]), axis=1)
    total_items = jnp.full_like(item, 1) * ends[N - 1]
    work = jnp.stack([block, key, is_first, is_last, total_items]).astype(jnp.int32)

    merged_count = count // 4
    dest = slot_dest[0]
    prompt_rows = text_embed.shape[0]
    req_count = N * N
    row_count = lax.axis_size("z") * lax.axis_size("c")
    slot_cap = 2
    owner = jnp.where(dest >= 0, dest // prompt_rows // row_count, -1)
    order = jnp.arange(merged_count)
    same_owner = (owner[:, None] == owner[None, :]) & (order[None, :] < order[:, None])
    ranks = jnp.sum(same_owner.astype(jnp.int32), axis=1)
    target = jnp.where(owner >= 0, owner * slot_cap + ranks, -1)
    select = target[None, :] == jnp.arange(req_count * slot_cap)[:, None]
    places = jnp.sum(jnp.where(select, (dest % prompt_rows + 1)[None, :], 0), axis=1)
    lane = jnp.arange(128)[None, :] == 0
    tail = jnp.where(lane, places[:, None], 0).astype(BF)
    id_row = ids.reshape(N, 1, total_rows)
    id_col = ids[:, None]
    select = select.astype(BF)
    near, h1, work, id_col, select, tail = lax.optimization_barrier(
        (near, h1, work, id_col, select, tail)
    )
    *qkv, mine, mine_half = pl.pallas_call(
        qkv_kernel,
        out_shape=[jax.ShapeDtypeStruct((3 * HEAD, total_rows), BF)] * N
        + [
            jax.ShapeDtypeStruct((N, HEAD, width), BF),
            jax.ShapeDtypeStruct((N, HEAD, half), BF),
        ],
        in_specs=[SMEM, VMEM, HBM],
        out_specs=[VMEM] * (N + 2),
        scratch_shapes=[
            pltpu.VMEM((2 * N, 3 * HEAD, half), BF),
            pltpu.SemaphoreType.DMA((4 * N,)),
        ],
        compiler_params=params(16),
        name="qkv",
    )(pos, h1, far(near))
    blocks = [qkv[0]] + [shift(qkv[k], "x", -k) for k in (1, 2, 3)]
    pass1 = shift(mine, "y", 1)
    pass3 = shift(mine, "y", 3)
    blocks, mine_half = lax.optimization_barrier((blocks, mine_half))
    pass2 = shift(mine_half, "y", 2)

    attended = pl.pallas_call(
        attend_kernel,
        out_shape=[jax.ShapeDtypeStruct((HEAD, total_rows), BF)] * N,
        in_specs=[SMEM, SMEM] + [VMEM] * 6,
        out_specs=[VMEM] * N,
        scratch_shapes=[
            pltpu.VMEM((N, HEAD, total_rows), BF),
            pltpu.VMEM((chunks, chunk, HEAD), BF),
            pltpu.VMEM((chunks, HEAD, chunk), BF),
            pltpu.VMEM((2, chunk, total_rows), F32),
            pltpu.VMEM((N, HEAD, total_rows), BF),
        ],
        compiler_params=params(16),
        name="attend",
    )(pos, work, *blocks, id_row, id_col)
    heads = [attended[0]] + [shift(attended[k], "x", k) for k in (1, 2, 3)]
    heads[1], pass2 = lax.optimization_barrier((heads[1], pass2))
    swap2 = swap(pass2)
    heads, pass1, pass3 = lax.optimization_barrier((heads, pass1, pass3))
    heads = pl.pallas_call(
        pack_kernel,
        out_shape=jax.ShapeDtypeStruct((N, HEAD, total_rows), BF),
        in_specs=[SMEM] + [VMEM] * N,
        out_specs=VMEM,
        compiler_params=params(8),
        name="pack",
    )(pos, *heads)
    gathered = [heads] + [shift(heads, "y", k) for k in (1, 2, 3)]
    _, near, w_near, w_merge = lax.optimization_barrier((heads, near, w_near, w_merge))

    fetched = pl.pallas_call(
        fetch_kernel,
        out_shape=[
            jax.ShapeDtypeStruct((N * N, HEAD, width), BF),
            jax.ShapeDtypeStruct((N * N, units, width), BF),
            jax.ShapeDtypeStruct((N * N, units, width), BF),
            jax.ShapeDtypeStruct((N, count, width), BF),
        ],
        in_specs=[SMEM] + [HBM] * 10,
        out_specs=[VMEM] * 4,
        scratch_shapes=[pltpu.SemaphoreType.DMA((20,))],
        compiler_params=params(4),
        name="fetch",
    )(
        pos,
        *[far(v) for v in pieces],
        *[far(v) for v in (near, w_near, pass1, pass3, pass2, swap2)],
    )

    w_merge = pl.pallas_call(
        fetch_merge_kernel,
        out_shape=jax.ShapeDtypeStruct(w_merge.shape, BF),
        in_specs=[HBM],
        out_specs=VMEM,
        scratch_shapes=[pltpu.SemaphoreType.DMA((8,))],
        compiler_params=params(4),
        name="fetch_merge",
    )(far(w_merge))

    def mlp(offsets, name):
        outputs = len(offsets) + (0 in offsets)
        return pl.pallas_call(
            functools.partial(mlp_kernel, offsets),
            out_shape=[jax.ShapeDtypeStruct((count, width), BF)] * outputs,
            in_specs=[SMEM] + [VMEM] * 9,
            out_specs=[VMEM] * outputs,
            compiler_params=params(24),
            cost_estimate=pl.CostEstimate(
                flops=6 * len(offsets) * count * width * width,
                transcendentals=len(offsets) * count * width,
                bytes_accessed=6 * width * width,
            ),
            name=name,
        )(pos, *gathered, *fetched, ln_mlp[None, :])

    part3, part1 = mlp((3, 1), "mlp_first")
    gathered[0], w_merge, part3, part1 = lax.optimization_barrier(
        (gathered[0], w_merge, part3, part1)
    )
    part2, part0, resid = mlp((2, 0), "mlp_second")
    early = shift(part1, "y", 1).astype(F32) + shift(part3, "y", 3).astype(F32)
    sums = [resid.astype(F32) + part0.astype(F32) + early, shift(part2, "y", 2)]
    outgoing = pl.pallas_call(
        merge_kernel,
        out_shape=jax.ShapeDtypeStruct((req_count * slot_cap, width + 128), BF),
        in_specs=[VMEM] * 5,
        out_specs=VMEM,
        scratch_shapes=[pltpu.VMEM((count * width // 128, 128), F32)],
        compiler_params=params(8),
        name="merge",
    )(*sums, w_merge, select, tail)
    arrived = lax.all_to_all(
        outgoing.reshape(req_count, slot_cap, width + 128),
        ("x", "y"),
        split_axis=0,
        concat_axis=0,
        tiled=True,
    ).reshape(req_count * slot_cap, width + 128)
    landing = arrived[:, width].astype(jnp.int32) - 1
    placer = landing[None, :] == jnp.arange(prompt_rows)[:, None]
    placed = jnp.dot(
        placer.astype(BF), arrived[:, :width], preferred_element_type=F32
    ).astype(BF)
    filled = jnp.any(placer, axis=1)
    return jnp.where(filled[:, None], placed, text_embed)


def solution(mesh):
    grid = Mesh(mesh.devices.reshape(N, N, -1, 2), ("x", "y", "z", "c"))
    req = ("x", "y")
    row = ("z", "c")
    return jax.shard_map(
        local,
        mesh=grid,
        in_specs=(
            P(row, req, None),
            P(row, None),
            P(),
            P(None, None, req),
            P(req, None),
            P(),
            P(None, req),
            P(req, None),
            P(),
            P(("x", "y", "z", "c"), None),
            P(row, req),
        ),
        out_specs=P(("x", "y", "z", "c"), None),
        check_vma=False,
    )
```

```python
import functools
import math

import jax
import jax.numpy as jnp
from jax import lax
from jax.experimental import pallas as pl
from jax.experimental.pallas import tpu as pltpu
from jax.sharding import Mesh
from jax.sharding import PartitionSpec as P

HEAD = 80
SCALE = math.log2(math.e) / math.sqrt(HEAD)
N = 4
BF = jnp.bfloat16
F32 = jnp.float32
NT = (((1,), (1,)), ((), ()))
TN = (((0,), (0,)), ((), ()))
HBM = pl.BlockSpec(memory_space=pltpu.HBM)
VMEM = pl.BlockSpec(memory_space=pltpu.VMEM)
SMEM = pl.BlockSpec(memory_space=pltpu.SMEM)


def params(mib):
    return pltpu.CompilerParams(vmem_limit_bytes=mib << 20)


def norm_rows(rows32, gain):
    center = rows32 - jnp.mean(rows32, axis=-1, keepdims=True)
    spread = jnp.mean(center * center, axis=-1, keepdims=True)
    return center * lax.rsqrt(spread + 1e-06) * gain


def shift(value, axis, step):
    pairs = [(i, (i + step) % N) for i in range(N)]
    return lax.ppermute(value, axis, pairs)


def far(value):
    return pltpu.with_memory_space_constraint(value, pltpu.HBM)


def swap(value):
    return lax.ppermute(value, "c", [(0, 1), (1, 0)])


def norm_kernel(pos, p0, p1, p2, p3, gain, h1, held, sems):
    y = pos[1]
    half = h1.shape[2]
    rows = p0.shape[0]
    copies = []
    for k, piece in enumerate((p0, p1, p2, p3)):
        copies.append(pltpu.make_async_copy(piece, held.at[k], sems.at[k]))
    for copy in copies:
        copy.start()
    for k in range(N):
        copies[k].wait()
        normed = norm_rows(held[k].astype(F32), gain[...]).astype(BF)
        at = pl.ds(pl.multiple_of(lax.rem(y - k + N, N) * rows, rows), rows)
        h1[0, at, :] = normed[:, :half]
        h1[1, at, :] = normed[:, half:]


def qkv_kernel(pos, h1, w_hbm, o0, o1, o2, o3, share, share_half, w, sems):
    x = pos[0]
    cols = w.shape[1]
    half = w.shape[2]
    copies = []
    for k in range(N):
        at = pl.ds(lax.rem(x - k + N, N) * 2, 2)
        copies.append(pltpu.make_async_copy(w_hbm.at[at, :cols, :], w.at[at], sems.at[k]))
    for j in range(2 * N):
        src = w_hbm.at[j, cols : cols + HEAD, :]
        dst = share.at[j // 2, :, j % 2 * half : (j % 2 + 1) * half]
        copies.append(pltpu.make_async_copy(src, dst, sems.at[N + j]))
    for j in range(N):
        src = w_hbm.at[2 * j + pos[3], cols : cols + HEAD, :]
        copies.append(pltpu.make_async_copy(src, share_half.at[j], sems.at[3 * N + j]))
    for copy in copies:
        copy.start()
    for k, out in enumerate((o0, o1, o2, o3)):
        at = lax.rem(x - k + N, N) * 2
        copies[k].wait()
        total = lax.dot_general(w[at], h1[0], NT, preferred_element_type=F32)
        total += lax.dot_general(w[at + 1], h1[1], NT, preferred_element_type=F32)
        out[:HEAD, :] = (total[:HEAD, :] * SCALE).astype(BF)
        out[HEAD:, :] = total[HEAD:, :].astype(BF)
    for copy in copies[N:]:
        copy.wait()


def attend_kernel(
    pos, work, r0, r1, r2, r3, id_row, id_col, o0, o1, o2, o3, qs, ks, vs, scores, outs
):
    x = pos[0]
    chunk = ks.shape[1]
    block = qs.shape[2]
    per = block // chunk
    for k, piece in enumerate((r0, r1, r2, r3)):
        at = lax.rem(x + k, N)
        qs[at] = piece[:HEAD, :]
        keys = jnp.transpose(piece[HEAD : 2 * HEAD, :])
        for j in range(per):
            ks[at * per + j] = keys[j * chunk : (j + 1) * chunk, :]
            vs[at * per + j] = piece[2 * HEAD :, j * chunk : (j + 1) * chunk]
    count = work[4, 0]

    def score(i):
        return jnp.dot(ks[work[1, i]], qs[work[0, i]], preferred_element_type=F32)

    scores[0] = score(0)

    def step(i, carry):
        top, total, acc = carry
        slot = lax.rem(i, 2)
        qb = work[0, i]
        kc = work[1, i]
        raw = scores[slot]
        scores[1 - slot] = score(jnp.minimum(i + 1, count - 1))
        key_ids = id_col[pl.ds(pl.multiple_of(kc * chunk, chunk), chunk), :]
        val = jnp.where(key_ids == id_row[qb], raw, -1e30)
        top = jnp.where(work[2, i] == 1, -1e30, top)
        new_top = jnp.maximum(top, jnp.max(val, axis=0, keepdims=True))
        alpha = jnp.exp2(top - new_top)
        alpha = jnp.where(work[2, i] == 1, 0.0, alpha)
        expo = jnp.exp2(val - new_top)
        total = total * alpha + jnp.sum(expo, axis=0, keepdims=True)
        acc = acc * alpha + jnp.dot(vs[kc], expo.astype(BF), preferred_element_type=F32)

        @pl.when(work[3, i] == 1)
        def _():
            outs[lax.rem(qb - x + N, N)] = (acc / total).astype(BF)

        return new_top, total, acc

    start = (
        jnp.full((1, block), -1e30, F32),
        jnp.zeros((1, block), F32),
        jnp.zeros((HEAD, block), F32),
    )
    lax.fori_loop(0, count, step, start)
    for k, out in enumerate((o0, o1, o2, o3)):
        out[...] = outs[k]


def pack_kernel(pos, g0, g1, g2, g3, out):
    x = pos[0]
    for k, piece in enumerate((g0, g1, g2, g3)):
        out[lax.rem(x - k + N, N)] = piece[...]


def copy_all(moves, sems):
    copies = [pltpu.make_async_copy(a, b, sems.at[i]) for i, (a, b) in enumerate(moves)]
    for copy in copies:
        copy.start()
    for copy in copies:
        copy.wait()


def fetch_kernel(pos, *refs):
    pieces = refs[0:4]
    near, w_hbm = refs[4:6]
    pass1, pass3, mine, other = refs[6:10]
    w_all, up, down, held, sems = refs[10:]
    y = pos[1]
    half = w_hbm.shape[3]
    skip = near.shape[1] - HEAD
    moves = []
    for j in range(N):
        for h in (0, 1):
            cols = slice(h * half, (h + 1) * half)
            moves.append((near.at[2 * j + h, skip : skip + HEAD, :], w_all.at[j, :, cols]))
    moves.append((pass1, w_all.at[N : 2 * N]))
    moves.append((pass3, w_all.at[3 * N :]))
    for k in range(N):
        moves.append((pieces[k], held.at[lax.rem(y - k + N, N)]))
    units = up.shape[1]
    for h in (0, 1):
        cols = slice(h * half, (h + 1) * half)
        moves.append((w_hbm.at[:, h, :units, :], up.at[:, :, cols]))
        moves.append((w_hbm.at[:, h, units:, :], down.at[:, :, cols]))
    for core in (0, 1):
        low = slice(core * half, (core + 1) * half)
        high = slice((1 - core) * half, (2 - core) * half)
        rows = slice(2 * N, 3 * N)

        @pl.when(pos[3] == core)
        def _(low=low, high=high, rows=rows):
            pair = [(mine, w_all.at[rows, :, low]), (other, w_all.at[rows, :, high])]
            copy_all(moves + pair, sems)


def fetch_merge_kernel(w_hbm, w, sems):
    parts = sems.shape[0]
    rows = w.shape[0] // parts
    cuts = [slice(i * rows, (i + 1) * rows) for i in range(parts)]
    copy_all([(w_hbm.at[cut], w.at[cut]) for cut in cuts], sems)


def mlp_kernel(offsets, pos, *refs):
    gathered = refs[0:4]
    w_all, up, down, held, gain = refs[4:9]
    outs = refs[9:]
    y = pos[1]
    rows = held.shape[1]
    width = held.shape[2]
    group = N * HEAD
    blocks = [lax.rem(y + k, N) for k in offsets]
    lhs = []
    start = []
    for block in blocks:
        cols = pl.ds(pl.multiple_of(block * rows, rows), rows)
        parts = [g[:, :, cols].reshape(group, rows) for g in gathered]
        lhs.append(jnp.transpose(jnp.concatenate(parts, axis=0)))
        start.append(held[block].astype(F32))
    lhs = jnp.concatenate(lhs, axis=0)
    start = jnp.concatenate(start, axis=0)
    attn = jnp.dot(lhs, w_all[...].reshape(N * group, width), preferred_element_type=F32)
    resid = (start + attn).astype(BF)
    normed = norm_rows(resid.astype(F32), gain[...]).astype(BF)
    count = up.shape[0] * up.shape[1]
    hidden = lax.dot_general(
        normed, up[...].reshape(count, width), NT, preferred_element_type=F32
    )
    hidden = (0.5 * hidden * (1.0 + lax.erf(hidden * math.sqrt(0.5)))).astype(BF)
    result = jnp.dot(hidden, down[...].reshape(count, width), preferred_element_type=F32)
    result = result.astype(BF)
    for i, k in enumerate(offsets):
        outs[i][...] = result[i * rows : (i + 1) * rows, :]
        if k == 0:
            outs[-1][...] = resid[i * rows : (i + 1) * rows, :]


def merge_kernel(early, late, w, select, tail, out, vision):
    sums = (early[...] + late[...].astype(F32)).astype(BF).astype(F32)
    full, width = early.shape
    count = full // 4
    tiles = width // 128
    for i in range(tiles):
        vision[i * full : (i + 1) * full, :] = sums[:, i * 128 : (i + 1) * 128]
    total = jnp.zeros((count, width), F32)
    for j in range(4):
        rows = [vision[pl.ds(i * full + j, count, stride=4), :] for i in range(tiles)]
        rows = jnp.concatenate(rows, axis=1).astype(BF)
        total += jnp.dot(rows, w[j * width : (j + 1) * width, :], preferred_element_type=F32)
    sent = jnp.dot(select[...], total.astype(BF), preferred_element_type=F32)
    out[:, :width] = sent.astype(BF)
    out[:, width:] = tail[...]


def local(
    patches,
    picture_ids,
    ln_attn,
    w_qkv,
    w_out,
    ln_mlp,
    w_up,
    w_down,
    w_merge,
    text_embed,
    slot_dest,
):
    rows = patches[0]
    count, width = rows.shape
    x = lax.axis_index("x")
    y = lax.axis_index("y")
    c = lax.axis_index("c")
    pos = jnp.stack([x, y, lax.axis_index("z"), c]).astype(jnp.int32)
    ids = picture_ids[0]

    half = width // 2
    w_heads = jnp.transpose(w_qkv, (0, 2, 1)).reshape(3 * HEAD, width)
    w_heads = jnp.concatenate([w_heads, w_out], axis=0)
    w_half = lax.dynamic_slice_in_dim(w_heads, c * half, half, 1)
    near = lax.all_gather(w_half, ("x", "c"), axis=0, tiled=False)
    z = lax.axis_index("z")
    units = w_down.shape[0] // N
    sizes = (units, half)
    packed = jnp.concatenate(
        [
            lax.dynamic_slice(w_up.T, (z * units, c * half), sizes),
            lax.dynamic_slice(w_down, (z * units, c * half), sizes),
        ],
        axis=0,
    )
    packed, _ = lax.optimization_barrier((packed, w_half))
    w_near = lax.all_gather(packed, ("x", "z", "c"), axis=0, tiled=False)
    w_near = w_near.reshape(N * N, 2, 2 * units, half)

    pieces = [rows] + [shift(rows, "y", k) for k in (1, 2, 3)]
    total_rows = count * N
    h1 = pl.pallas_call(
        norm_kernel,
        out_shape=jax.ShapeDtypeStruct((2, total_rows, half), BF),
        in_specs=[SMEM] + [HBM] * N + [VMEM],
        out_specs=VMEM,
        scratch_shapes=[
            pltpu.VMEM((N, count, width), BF),
            pltpu.SemaphoreType.DMA((N,)),
        ],
        compiler_params=params(16),
        name="norm",
    )(pos, *[far(piece) for piece in pieces], ln_attn[None, :])
    group_rows = ids.shape[0]
    chunk = 512
    chunks = group_rows // chunk
    held = (ids[:, None] == jnp.arange(16)[None, :]).reshape(chunks, chunk, 16)
    held = jnp.any(held, axis=1)
    per = chunks // N
    wanted = jnp.any(held.reshape(N, per, 16), axis=1)
    need = jnp.any(wanted[:, None, :] & held[None, :, :], axis=2)
    where = jnp.arange(chunks)[None, :]
    low = jnp.min(jnp.where(need, where, chunks - 1), axis=1)
    high = jnp.max(jnp.where(need, where + 1, 1), axis=1)
    low = jnp.minimum(low, high - 1)
    spans = high - low
    index = jnp.arange(N)
    ends = jnp.sum(jnp.where(index[None, :] <= index[:, None], spans[None, :], 0), axis=1)
    item = jnp.arange(N * chunks)
    block = jnp.sum((item[:, None] >= ends[None, :]).astype(jnp.int32), axis=1)
    block = jnp.minimum(block, N - 1)
    mark = block[:, None] == index[None, :]
    begin = jnp.sum(jnp.where(mark, (low + spans - ends)[None, :], 0), axis=1)
    key = jnp.clip(begin + item, 0, chunks - 1)
    is_first = jnp.any(mark & ((ends - spans)[None, :] == item[:, None]), axis=1)
    is_last = jnp.any(mark & ((ends - 1)[None, :] == item[:, None]), axis=1)
    total_items = jnp.full_like(item, 1) * ends[N - 1]
    work = jnp.stack([block, key, is_first, is_last, total_items]).astype(jnp.int32)

    merged_count = count // 4
    dest = slot_dest[0]
    prompt_rows = text_embed.shape[0]
    req_count = N * N
    row_count = lax.axis_size("z") * lax.axis_size("c")
    slot_cap = 2
    owner = jnp.where(dest >= 0, dest // prompt_rows // row_count, -1)
    order = jnp.arange(merged_count)
    same_owner = (owner[:, None] == owner[None, :]) & (order[None, :] < order[:, None])
    ranks = jnp.sum(same_owner.astype(jnp.int32), axis=1)
    target = jnp.where(owner >= 0, owner * slot_cap + ranks, -1)
    select = target[None, :] == jnp.arange(req_count * slot_cap)[:, None]
    places = jnp.sum(jnp.where(select, (dest % prompt_rows + 1)[None, :], 0), axis=1)
    lane = jnp.arange(128)[None, :] == 0
    tail = jnp.where(lane, places[:, None], 0).astype(BF)
    id_row = ids.reshape(N, 1, total_rows)
    id_col = ids[:, None]
    select = select.astype(BF)
    near, h1, work, id_col, select, tail = lax.optimization_barrier(
        (near, h1, work, id_col, select, tail)
    )
    *qkv, mine, mine_half = pl.pallas_call(
        qkv_kernel,
        out_shape=[jax.ShapeDtypeStruct((3 * HEAD, total_rows), BF)] * N
        + [
            jax.ShapeDtypeStruct((N, HEAD, width), BF),
            jax.ShapeDtypeStruct((N, HEAD, half), BF),
        ],
        in_specs=[SMEM, VMEM, HBM],
        out_specs=[VMEM] * (N + 2),
        scratch_shapes=[
            pltpu.VMEM((2 * N, 3 * HEAD, half), BF),
            pltpu.SemaphoreType.DMA((4 * N,)),
        ],
        compiler_params=params(16),
        name="qkv",
    )(pos, h1, far(near))
    blocks = [qkv[0]] + [shift(qkv[k], "x", -k) for k in (1, 2, 3)]
    pass1 = shift(mine, "y", 1)
    pass3 = shift(mine, "y", 3)
    blocks, mine_half = lax.optimization_barrier((blocks, mine_half))
    pass2 = shift(mine_half, "y", 2)

    attended = pl.pallas_call(
        attend_kernel,
        out_shape=[jax.ShapeDtypeStruct((HEAD, total_rows), BF)] * N,
        in_specs=[SMEM, SMEM] + [VMEM] * 6,
        out_specs=[VMEM] * N,
        scratch_shapes=[
            pltpu.VMEM((N, HEAD, total_rows), BF),
            pltpu.VMEM((chunks, chunk, HEAD), BF),
            pltpu.VMEM((chunks, HEAD, chunk), BF),
            pltpu.VMEM((2, chunk, total_rows), F32),
            pltpu.VMEM((N, HEAD, total_rows), BF),
        ],
        compiler_params=params(16),
        name="attend",
    )(pos, work, *blocks, id_row, id_col)
    attended = list(attended)
    attended[3], pass2 = lax.optimization_barrier((attended[3], pass2))
    swap2 = swap(pass2)
    heads = [attended[0]] + [shift(attended[k], "x", k) for k in (1, 2, 3)]
    heads, pass1, pass3 = lax.optimization_barrier((heads, pass1, pass3))
    heads = pl.pallas_call(
        pack_kernel,
        out_shape=jax.ShapeDtypeStruct((N, HEAD, total_rows), BF),
        in_specs=[SMEM] + [VMEM] * N,
        out_specs=VMEM,
        compiler_params=params(8),
        name="pack",
    )(pos, *heads)
    gathered = [heads] + [shift(heads, "y", k) for k in (1, 2, 3)]
    _, near, w_near, w_merge = lax.optimization_barrier((heads, near, w_near, w_merge))

    fetched = pl.pallas_call(
        fetch_kernel,
        out_shape=[
            jax.ShapeDtypeStruct((N * N, HEAD, width), BF),
            jax.ShapeDtypeStruct((N * N, units, width), BF),
            jax.ShapeDtypeStruct((N * N, units, width), BF),
            jax.ShapeDtypeStruct((N, count, width), BF),
        ],
        in_specs=[SMEM] + [HBM] * 10,
        out_specs=[VMEM] * 4,
        scratch_shapes=[pltpu.SemaphoreType.DMA((20,))],
        compiler_params=params(4),
        name="fetch",
    )(
        pos,
        *[far(v) for v in pieces],
        *[far(v) for v in (near, w_near, pass1, pass3, pass2, swap2)],
    )

    w_merge = pl.pallas_call(
        fetch_merge_kernel,
        out_shape=jax.ShapeDtypeStruct(w_merge.shape, BF),
        in_specs=[HBM],
        out_specs=VMEM,
        scratch_shapes=[pltpu.SemaphoreType.DMA((8,))],
        compiler_params=params(4),
        name="fetch_merge",
    )(far(w_merge))

    def mlp(offsets, name):
        outputs = len(offsets) + (0 in offsets)
        return pl.pallas_call(
            functools.partial(mlp_kernel, offsets),
            out_shape=[jax.ShapeDtypeStruct((count, width), BF)] * outputs,
            in_specs=[SMEM] + [VMEM] * 9,
            out_specs=[VMEM] * outputs,
            compiler_params=params(24),
            cost_estimate=pl.CostEstimate(
                flops=6 * len(offsets) * count * width * width,
                transcendentals=len(offsets) * count * width,
                bytes_accessed=6 * width * width,
            ),
            name=name,
        )(pos, *gathered, *fetched, ln_mlp[None, :])

    part2, part1 = mlp((2, 1), "mlp_first")
    gathered[0], w_merge, part2, part1 = lax.optimization_barrier(
        (gathered[0], w_merge, part2, part1)
    )
    part3, part0, resid = mlp((3, 0), "mlp_second")
    early = shift(part1, "y", 1).astype(F32) + shift(part2, "y", 2).astype(F32)
    sums = [resid.astype(F32) + part0.astype(F32) + early, shift(part3, "y", 3)]
    outgoing = pl.pallas_call(
        merge_kernel,
        out_shape=jax.ShapeDtypeStruct((req_count * slot_cap, width + 128), BF),
        in_specs=[VMEM] * 5,
        out_specs=VMEM,
        scratch_shapes=[pltpu.VMEM((count * width // 128, 128), F32)],
        compiler_params=params(8),
        name="merge",
    )(*sums, w_merge, select, tail)
    arrived = lax.all_to_all(
        outgoing.reshape(req_count, slot_cap, width + 128),
        ("x", "y"),
        split_axis=0,
        concat_axis=0,
        tiled=True,
    ).reshape(req_count * slot_cap, width + 128)
    landing = arrived[:, width].astype(jnp.int32) - 1
    placer = landing[None, :] == jnp.arange(prompt_rows)[:, None]
    placed = jnp.dot(
        placer.astype(BF), arrived[:, :width], preferred_element_type=F32
    ).astype(BF)
    filled = jnp.any(placer, axis=1)
    return jnp.where(filled[:, None], placed, text_embed)


def solution(mesh):
    grid = Mesh(mesh.devices.reshape(N, N, -1, 2), ("x", "y", "z", "c"))
    req = ("x", "y")
    row = ("z", "c")
    return jax.shard_map(
        local,
        mesh=grid,
        in_specs=(
            P(row, req, None),
            P(row, None),
            P(),
            P(None, None, req),
            P(req, None),
            P(),
            P(None, req),
            P(req, None),
            P(),
            P(("x", "y", "z", "c"), None),
            P(row, req),
        ),
        out_specs=P(("x", "y", "z", "c"), None),
        check_vma=False,
    )
```
